256 devices in a mesh: freq: 4 (over x_hi, core), order: 64 (over z, y, x_lo).
Axes of the slice: x: 4 (x_hi: 2, x_lo: 2; x = x_hi * 2 + x_lo), y: 4, z: 8, core: 2. Of those that a mesh axis runs over, the one named last changes fastest.
Arguments:
- harmonics: bfloat16 [32, 128, 2, 4096], P(None, 'order'), may hold values from -6 to 6
- legendre: bfloat16 [128, 4096, 512], P('order'), may hold values from -0.09375 to 0.09375
- beam_window: float32 [4, 4096], replicated, may hold values from 0.2 to 1
- order_ids: int32 [128], replicated, may hold values from 0 to 4095, as said below
- noise_weight: float32 [4, 512, 8192], P('freq', 'order'), may hold values from 0.3 to 3
Outputs:
- applied: float32 [32, 128, 2, 4096], P('freq', 'order')
The draws below stay inside these ranges and needn't reach their ends.
Inputs may be any that keep to these rules, and one draw needn't show every extreme that they name: `order_ids`: all distinct; slots 2k and 2k + 1 hold the orders m and 4095 - m for some m < 2048; one pair holds the orders 0 and 4095.
All inputs are finite; a program needn't handle non-finite values.
Results may differ from the reference program's by a relative error of at most 0.0027.
Values may be sent and summed in bfloat16 or wider, within the bound.
No kernel may reach another device: no remote copies, remote signals or barrier semaphores. Data moves between devices by JAX's collectives and lax.ppermute only.
A program may use at most 64 MiB of HBM per device.

```python
import math
import jax
import jax.numpy as jnp
from jax import lax

L = 4096
NLON = 8192
MAPS = 32
GROUPS = 4
ORDERS = 128
LATS = 512


def draw_order_ids(key, part):
    first_key, second_key = jax.random.split(jax.random.fold_in(key, 17))
    others = jax.random.permutation(first_key, L // 2 - 1)[:ORDERS // 2 - 1].astype(jnp.int32) + 1
    half = jnp.concatenate([jnp.zeros((1,), jnp.int32), others])
    half = jax.random.permutation(second_key, half)
    paired = jnp.stack([half, L - 1 - half], 1).reshape(-1)
    return paired.astype(jnp.int32)


def block_levels(own_key, shape, shards, smallest, top_value):
    level = 1.0
    for position, blocks in shards:
        draws = jax.random.uniform(jax.random.fold_in(jax.random.fold_in(own_key, 6), position), (blocks,), jnp.float32, smallest / len(shards), top_value / len(shards))
        level = level * jnp.repeat(jnp.exp(draws), shape[position] // blocks).reshape((-1,) + (1,) * (len(shape) - 1 - position))
    return level


def centred(own_key, dims, spread, bound, cuts=(), kind=jnp.bfloat16):
    drawn = jax.random.normal(own_key, dims, jnp.float32) * spread
    if len(cuts) > 0:
        drawn = block_levels(own_key, dims, cuts, -0.22, 0.18) * drawn
    return jnp.clip(drawn, min=-bound, max=bound).astype(kind)


def setup_inputs(seed: int = 0) -> dict:
    keys = jax.random.split(jax.random.key(seed), 6)
    return {
        "harmonics": centred(keys[0], (MAPS, ORDERS, 2, L), 1.0, 6.0, ((1, 64),)),
        "legendre": centred(keys[1], (ORDERS, L, LATS), L ** -0.5, 0.09375, ((0, 64),)),
        "beam_window": jnp.clip(jnp.exp(jax.random.uniform(keys[2], (GROUPS, L), jnp.float32, math.log(0.2), math.log(1.0))), 0.2, 1.0),
        "order_ids": draw_order_ids(jax.random.fold_in(keys[5], 71), 0),
        "noise_weight": jnp.clip(jnp.exp(math.log(3.0) - 2.3025851 * jax.random.uniform(keys[4], (GROUPS, LATS, NLON), jnp.float32) ** block_levels(keys[4], (GROUPS, LATS, NLON), ((0, 4), (1, 64)), -0.2, 0.2)), 0.3, 3.0),
    }


def make_table(order_ids, nlon):
    steps = jnp.arange(nlon, dtype=jnp.int32)
    turns = order_ids.astype(jnp.int32)[:, None] * steps[None, :] % nlon
    angle = turns.astype(jnp.float32) * (2.0 * math.pi / nlon)
    factor = jnp.where(order_ids == 0, 1.0, 2.0).astype(jnp.float32)[:, None]
    return jnp.stack([factor * jnp.cos(angle), -factor * jnp.sin(angle)], 1).astype(jnp.bfloat16)

def synthesize(smoothed, legendre):

    def one_order(pair):
        piece, values = pair
        out = jnp.dot(piece.reshape(-1, piece.shape[-1]), values, preferred_element_type=jnp.float32)
        return out.reshape(piece.shape[0], piece.shape[1], values.shape[1]).astype(jnp.bfloat16)
    stacked = lax.map(one_order, (jnp.moveaxis(smoothed, 1, 0), legendre))
    return jnp.moveaxis(stacked, 0, 1)

def analyze(band_terms, legendre):

    def one_order(pair):
        piece, values = pair
        out = jnp.dot(piece.reshape(-1, piece.shape[-1]), values.T, preferred_element_type=jnp.float32)
        return out.reshape(piece.shape[0], piece.shape[1], values.shape[0])
    stacked = lax.map(one_order, (jnp.moveaxis(band_terms, 1, 0), legendre))
    return jnp.moveaxis(stacked, 0, 1)

def reference(harmonics, legendre, beam_window, order_ids, noise_weight):
    live_mask = (jnp.arange(L, dtype=jnp.int32)[None, :] >= order_ids[:, None]).astype(jnp.float32)
    table_wide = make_table(order_ids, NLON).astype(jnp.float32)
    fwd_scale = 1.0 / math.sqrt(2.0 * ORDERS)
    back_scale = 1.0 / math.sqrt(1.0 * NLON)
    total = jnp.zeros((MAPS, ORDERS, 2, L), jnp.float32)
    for group in range(GROUPS):
        shaping = (beam_window[group][None, :] * live_mask)[None, :, None, :]
        smoothed = (harmonics.astype(jnp.float32) * shaping).astype(jnp.bfloat16)
        columns = synthesize(smoothed, legendre)
        field = jnp.einsum('bocr,ocj->brj', columns.astype(jnp.float32), table_wide, precision=lax.Precision.HIGHEST) * fwd_scale
        weighted = (field * noise_weight[group][None]).astype(jnp.bfloat16)
        band_terms = (jnp.einsum('brj,ocj->bocr', weighted.astype(jnp.float32), table_wide, precision=lax.Precision.HIGHEST) * back_scale).astype(jnp.bfloat16)
        total = total + analyze(band_terms, legendre) * shaping
    return total
```

```python
import math

import jax
import jax.numpy as jnp
from jax import lax
from jax.sharding import PartitionSpec as P

ORD_DEV = 2


def make_table(order_ids, nlon):
    fine = 128
    coarse = nlon // fine
    unit = 2.0 * math.pi / nlon
    a_turns = order_ids[:, None] * (fine * jnp.arange(coarse, dtype=jnp.int32))[None, :] % nlon
    b_turns = order_ids[:, None] * jnp.arange(fine, dtype=jnp.int32)[None, :] % nlon
    a = a_turns.astype(jnp.float32) * unit
    b = b_turns.astype(jnp.float32) * unit
    factor = jnp.where(order_ids == 0, 1.0, 2.0).astype(jnp.float32)[:, None]
    ca, sa = (factor * jnp.cos(a))[:, :, None], (factor * jnp.sin(a))[:, :, None]
    cb, sb = jnp.cos(b)[:, None, :], jnp.sin(b)[:, None, :]
    cos = (ca * cb - sa * sb).astype(jnp.bfloat16).reshape(-1, nlon)
    sin = (-(sa * cb + ca * sb)).astype(jnp.bfloat16).reshape(-1, nlon)
    return jnp.stack([cos, sin], 1)


def on_device(harmonics, legendre, beam_window, order_ids, noise_weight):
    maps = harmonics.shape[0]
    degrees = harmonics.shape[3]
    lats = legendre.shape[2]
    nlon = noise_weight.shape[2]
    orders_all = order_ids.shape[0]
    groups = beam_window.shape[0]
    first_slot = lax.axis_index("order") * ORD_DEV
    local_ids = lax.dynamic_slice_in_dim(order_ids, first_slot, ORD_DEV, 0)
    live_mask = (jnp.arange(degrees, dtype=jnp.int32)[None, :] >= local_ids[:, None]).astype(
        jnp.float32
    )
    own_beam = lax.dynamic_index_in_dim(beam_window, lax.axis_index("freq"), 0, keepdims=False)
    own_shaping = (own_beam[None, :] * live_mask)[None, :, None, :]
    smoothed = (harmonics.astype(jnp.float32) * own_shaping).astype(jnp.bfloat16)
    columns = jnp.einsum(
        "bocl,olr->bocr", smoothed, legendre, preferred_element_type=jnp.float32
    ).astype(jnp.bfloat16)
    dft_table = make_table(order_ids, nlon)
    fwd_scale = 1.0 / math.sqrt(2.0 * orders_all)
    back_scale = 1.0 / math.sqrt(1.0 * nlon)
    pixel_weights = noise_weight[0]
    field = (
        jnp.einsum(
            "bocr,ocj->brj",
            lax.all_to_all(columns, "order", split_axis=3, concat_axis=1, tiled=True),
            dft_table,
            preferred_element_type=jnp.float32,
        )
        * fwd_scale
    )
    weighted = (field * pixel_weights[None]).astype(jnp.bfloat16)
    summed = jnp.einsum("brj,ocj->bocr", weighted, dft_table, preferred_element_type=jnp.float32)
    band_terms = (summed * back_scale).astype(jnp.bfloat16)
    own_maps = maps // groups
    order_devs = orders_all // ORD_DEV
    rows = lats // order_devs
    send = band_terms.reshape(groups, own_maps, order_devs, ORD_DEV, 2, rows)
    send = send.transpose(0, 2, 3, 4, 1, 5).reshape(groups * order_devs, 2, -1)
    got = lax.all_to_all(send, ("freq", "order"), split_axis=0, concat_axis=0, tiled=True)
    got = got.reshape(groups, order_devs, ORD_DEV, 2, own_maps, rows)
    got = got.transpose(2, 0, 3, 4, 1, 5).reshape(ORD_DEV, groups, 2, own_maps, lats)
    projected = jnp.einsum("ofcbr,olr->ofcbl", got, legendre, preferred_element_type=jnp.float32)
    shaping = beam_window[None, :, :] * live_mask[:, None, :]
    total = jnp.sum(projected * shaping[:, :, None, None, :], axis=1)
    return total.transpose(2, 0, 1, 3)


def solution(mesh):
    return jax.shard_map(
        on_device,
        mesh=mesh,
        in_specs=(
            P(None, "order", None, None),
            P("order", None, None),
            P(),
            P(),
            P("freq", "order", None),
        ),
        out_specs=P("freq", "order", None, None),
        check_vma=False,
    )
```

```python
import math

import jax
import jax.numpy as jnp
from jax import lax
from jax.experimental import pallas as pl
from jax.experimental.pallas import tpu as pltpu
from jax.sharding import PartitionSpec as P

ORD_DEV = 2
LANES = 128
F32 = jnp.float32
BF16 = jnp.bfloat16


def lane_ids(shape):
    return lax.broadcasted_iota(jnp.int32, shape, len(shape) - 1)


def swap_halves(a, b):
    low = lane_ids(a.shape) < LANES // 2
    first = jnp.where(low, a, pltpu.roll(b, LANES // 2, a.ndim - 1))
    second = jnp.where(low, pltpu.roll(a, LANES // 2, a.ndim - 1), b)
    return first, second


def forward_kernel(parts, ids_ref, beam_ref, harm_ref, leg_ref, out_ref, leg_v, wide, lhs, sems):
    degrees, lats = leg_ref.shape[1], leg_ref.shape[2]
    maps = out_ref.shape[1] // (2 * ORD_DEV)
    tiles = degrees // LANES
    step = degrees // parts
    copies = []
    for o in range(ORD_DEV):
        for p in range(parts):
            copy = pltpu.make_async_copy(
                leg_ref.at[o, pl.ds(p * step, step), :],
                leg_v.at[o, pl.ds(p * step, step), :],
                sems.at[o * parts + p],
            )
            copy.start()
            copies.append(copy)
    slot = lax.axis_index("order") * ORD_DEV
    group = lax.axis_index("freq")
    wide[...] = harm_ref[...].astype(F32)
    beam = beam_ref[pl.ds(group, 1), :]
    degree = lane_ids((1, degrees))
    sums = []
    for o in range(ORD_DEV):
        shaping = jnp.where(degree >= ids_ref[slot + o], beam, 0.0)
        total = jnp.zeros((2 * maps, lats), F32)
        for p in range(parts):
            for t in range(p * tiles // parts, (p + 1) * tiles // parts):
                cols = pl.ds(t * LANES, LANES)
                for c in range(2):
                    rows = wide[pl.ds((o * tiles + t) * 2 + c, maps, stride=ORD_DEV * tiles * 2), :]
                    lhs[pl.ds(c * maps, maps), cols] = (
                        rows * shaping[:, t * LANES : (t + 1) * LANES]
                    ).astype(BF16)
            copies[o * parts + p].wait()
            total += jnp.dot(
                lhs[:, pl.ds(p * step, step)],
                leg_v[o, pl.ds(p * step, step), :],
                preferred_element_type=F32,
            )
        sums.append(total)
    both = jnp.concatenate(sums, 0)
    out_ref[...] = both.T.astype(BF16)


def forward(order_ids, beam, harm, legendre, maps, parts=4):
    degrees, lats = legendre.shape[1:]
    return pl.pallas_call(
        lambda *refs: forward_kernel(parts, *refs),
        name="forward",
        out_shape=jax.ShapeDtypeStruct((lats, ORD_DEV * 2 * maps), BF16),
        in_specs=[
            pl.BlockSpec(memory_space=pltpu.SMEM),
            pl.BlockSpec(memory_space=pltpu.VMEM),
            pl.BlockSpec(memory_space=pltpu.VMEM),
            pl.BlockSpec(memory_space=pl.ANY),
        ],
        out_specs=pl.BlockSpec(memory_space=pltpu.VMEM),
        scratch_shapes=[
            pltpu.VMEM(legendre.shape, BF16),
            pltpu.VMEM(harm.shape, F32),
            pltpu.VMEM((2 * maps, degrees), BF16),
            pltpu.SemaphoreType.DMA((ORD_DEV * parts,)),
        ],
    )(order_ids, beam, harm, legendre)


def table_kernel(coarse_ref, mid_ref, fine_ref, out_ref, base):
    rows = coarse_ref.shape[1]
    mids, coarses = mid_ref.shape[2], coarse_ref.shape[2]
    fc, fs = fine_ref[0], fine_ref[1]
    for q in range(mids):
        mc, ms = mid_ref[0, :, q : q + 1], mid_ref[1, :, q : q + 1]
        cols = slice(q * LANES, (q + 1) * LANES)
        base[0, :, cols] = mc * fc - ms * fs
        base[1, :, cols] = ms * fc + mc * fs
    half = rows // ORD_DEV
    span = mids * LANES
    for p in range(coarses):
        cc, cs = coarse_ref[0, :, p : p + 1], coarse_ref[1, :, p : p + 1]
        cos = (cc * base[0] - cs * base[1]).astype(BF16)
        sin = (-(cs * base[0] + cc * base[1])).astype(BF16)
        for o in range(ORD_DEV):
            part = slice(o * half, (o + 1) * half)
            out_ref[pl.ds(o * rows, half), pl.ds(p * span, span)] = cos[part]
            out_ref[pl.ds(o * rows + half, half), pl.ds(p * span, span)] = sin[part]


def make_table(order_ids, nlon):
    ids = order_ids.reshape(-1, ORD_DEV).T.reshape(-1, 1)
    mids = 8
    coarses = nlon // (mids * LANES)
    unit = 2.0 * math.pi / nlon

    def pair(step, count, factor):
        turns = ids * (step * jnp.arange(count, dtype=jnp.int32))[None, :] % nlon
        angle = turns.astype(F32) * unit
        return jnp.stack([factor * jnp.cos(angle), factor * jnp.sin(angle)])

    factor = jnp.where(ids == 0, 1.0, 2.0).astype(F32)
    coarse = pair(mids * LANES, coarses, factor)
    mid = pair(LANES, mids, 1.0)
    fine = pair(1, LANES, 1.0)
    rows = ids.shape[0]
    return pl.pallas_call(
        table_kernel,
        name="table",
        out_shape=jax.ShapeDtypeStruct((2 * rows, nlon), BF16),
        in_specs=[pl.BlockSpec(memory_space=pltpu.VMEM)] * 3,
        out_specs=pl.BlockSpec(memory_space=pltpu.VMEM),
        scratch_shapes=[pltpu.VMEM((2, rows, mids * LANES), F32)],
    )(coarse, mid, fine)


def pixel_kernel(groups, chunk, scales, got_ref, table_ref, weight_ref, out_ref, wide, lhs, mixed):
    fwd_scale, back_scale = scales
    rows = weight_ref.shape[0]
    pairs = got_ref.shape[0] // rows
    maps = got_ref.shape[1] // (2 * ORD_DEV)
    nlon = table_ref.shape[1]
    wide[...] = got_ref[...].astype(F32)
    for r in range(0, rows, 2):
        stacked = jnp.concatenate(
            [wide[pl.ds(r + i, pairs, stride=rows), :] for i in range(2)], 0
        )
        turned = stacked.T
        for o in range(ORD_DEV):
            cos = turned[(2 * o) * maps : (2 * o + 1) * maps]
            sin = turned[(2 * o + 1) * maps : (2 * o + 2) * maps]
            for i, half in enumerate(swap_halves(cos, sin)):
                lhs[pl.ds((r + i) * maps, maps), pl.ds(o * LANES, LANES)] = half.astype(BF16)
    total = jnp.zeros((rows * maps, 2 * LANES), F32)
    for j in range(nlon // chunk):
        cols = pl.ds(j * chunk, chunk)
        part = table_ref[:, cols]
        field = jnp.dot(lhs[...], part, preferred_element_type=F32)
        weight = weight_ref[:, cols] * fwd_scale
        weighted = jnp.concatenate(
            [
                (field[r * maps : (r + 1) * maps] * weight[r : r + 1]).astype(BF16)
                for r in range(rows)
            ],
            0,
        )
        total += lax.dot_general(
            weighted, part, (((1,), (1,)), ((), ())), preferred_element_type=F32
        )
    total = total * back_scale
    own = maps // groups
    low_rows = rows // 2
    for f in range(groups):
        pieces = []
        for low in range(low_rows):
            for o in range(ORD_DEV):
                at = [(high * low_rows + low) * maps + f * own for high in range(2)]
                pieces += list(
                    swap_halves(
                        *[total[a : a + own, o * LANES : (o + 1) * LANES] for a in at]
                    )
                )
        turned = jnp.concatenate(pieces, 0).T
        for high in range(2):
            mixed[pl.ds(f * 2 * pairs + high, pairs, stride=2), :] = turned[
                high * pairs : (high + 1) * pairs
            ]
    out_ref[...] = mixed[...].astype(BF16)


def pixels(got, table, weight, groups, scales, chunk=512):
    return pl.pallas_call(
        lambda *refs: pixel_kernel(groups, chunk, scales, *refs),
        name="pixels",
        out_shape=jax.ShapeDtypeStruct(got.shape, BF16),
        in_specs=[pl.BlockSpec(memory_space=pltpu.VMEM)] * 3,
        out_specs=pl.BlockSpec(memory_space=pltpu.VMEM),
        scratch_shapes=[
            pltpu.VMEM(got.shape, F32),
            pltpu.VMEM((got.shape[0] // 2, 2 * LANES), BF16),
            pltpu.VMEM(got.shape, F32),
        ],
    )(got, table, weight)


def backward_kernel(parts, ids_ref, beam_ref, got_ref, leg_ref, out_ref, leg_v, mixed, sems):
    degrees, lats = leg_ref.shape[1], leg_ref.shape[2]
    groups = beam_ref.shape[0]
    tiles = degrees // LANES
    step = degrees // parts
    copies = []
    for o in range(ORD_DEV):
        for p in range(parts):
            copy = pltpu.make_async_copy(
                leg_ref.at[o, pl.ds(p * step, step), :],
                leg_v.at[o, pl.ds(p * step, step), :],
                sems.at[o * parts + p],
            )
            copy.start()
            copies.append(copy)
    slot = lax.axis_index("order") * ORD_DEV
    span = got_ref.shape[0] // groups
    width = LANES // groups
    lows = lats // span
    own = width // (2 * ORD_DEV)
    blocks = [got_ref[pl.ds(f * span, span), :].astype(F32) for f in range(groups)]
    lane_group = lane_ids((span, LANES)) // width
    turned = [
        [v if k == 0 else pltpu.roll(v, k * width, 1) for k in range(groups)] for v in blocks
    ]
    for low in range(lows):
        merged = turned[0][(0 - low) % groups]
        for f in range(1, groups):
            merged = jnp.where(lane_group == f, turned[f][(f - low) % groups], merged)
        mixed[pl.ds(low, span, stride=lows), :] = merged
    rows = mixed[...].T.astype(BF16)
    degree = lane_ids((1, degrees))
    for o in range(ORD_DEV):
        lhs = jnp.concatenate(
            [
                rows[f * width + o * 2 * own : f * width + (o + 1) * 2 * own]
                for f in range(groups)
            ],
            0,
        )
        for p in range(parts):
            copies[o * parts + p].wait()
            cols = slice(p * step, (p + 1) * step)
            terms = lax.dot_general(
                lhs,
                leg_v[o, pl.ds(p * step, step), :],
                (((1,), (1,)), ((), ())),
                preferred_element_type=F32,
            )
            live = degree[:, cols] >= ids_ref[slot + o]
            total = jnp.zeros((2 * own, step), F32)
            for f in range(groups):
                shaping = jnp.where(live, beam_ref[f : f + 1, cols], 0.0)
                total += terms[f * 2 * own : (f + 1) * 2 * own] * shaping
            for t in range(tiles // parts):
                for c in range(2):
                    at = o * tiles * 2 + (p * tiles // parts + t) * 2 + c
                    out_ref[pl.ds(at, own, stride=ORD_DEV * tiles * 2), :] = total[
                        c * own : (c + 1) * own, t * LANES : (t + 1) * LANES
                    ]


def backward(order_ids, beam, got, legendre, own, parts=4):
    degrees = legendre.shape[1]
    return pl.pallas_call(
        lambda *refs: backward_kernel(parts, *refs),
        name="backward",
        out_shape=jax.ShapeDtypeStruct((own * ORD_DEV * 2 * degrees // LANES, LANES), F32),
        in_specs=[
            pl.BlockSpec(memory_space=pltpu.SMEM),
            pl.BlockSpec(memory_space=pltpu.VMEM),
            pl.BlockSpec(memory_space=pltpu.VMEM),
            pl.BlockSpec(memory_space=pl.ANY),
        ],
        out_specs=pl.BlockSpec(memory_space=pltpu.VMEM),
        scratch_shapes=[
            pltpu.VMEM(legendre.shape, BF16),
            pltpu.VMEM((legendre.shape[2], LANES), F32),
            pltpu.SemaphoreType.DMA((ORD_DEV * parts,)),
        ],
    )(order_ids, beam, got, legendre)


def on_device(harmonics, legendre, beam_window, order_ids, noise_weight):
    maps, _, _, degrees = harmonics.shape
    lats = legendre.shape[2]
    nlon = noise_weight.shape[2]
    orders_all = order_ids.shape[0]
    groups = beam_window.shape[0]
    tiles = degrees // LANES
    own = maps // groups
    pairs = orders_all // ORD_DEV
    scales = (1.0 / math.sqrt(2.0 * orders_all), 1.0 / math.sqrt(1.0 * nlon))
    harm = harmonics.reshape(maps, ORD_DEV, 2, tiles, LANES).transpose(0, 1, 3, 2, 4)
    harm = harm.reshape(-1, LANES)
    columns = forward(order_ids, beam_window, harm, legendre, maps)
    columns = columns.reshape(pairs, lats // pairs, -1)
    got = lax.all_to_all(columns, "order", split_axis=0, concat_axis=0, tiled=True)
    table = make_table(order_ids, nlon)
    terms = pixels(got.reshape(lats, -1), table, noise_weight[0], groups, scales)
    terms = terms.reshape(groups * pairs, -1, LANES)
    back = lax.all_to_all(terms, ("freq", "order"), split_axis=0, concat_axis=0, tiled=True)
    out = backward(order_ids, beam_window, back.reshape(-1, LANES), legendre, own)
    out = out.reshape(own, ORD_DEV, tiles, 2, LANES).transpose(0, 1, 3, 2, 4)
    return out.reshape(own, ORD_DEV, 2, degrees)


def solution(mesh):
    return jax.shard_map(
        on_device,
        mesh=mesh,
        in_specs=(
            P(None, "order", None, None),
            P("order", None, None),
            P(),
            P(),
            P("freq", "order", None),
        ),
        out_specs=P("freq", "order", None, None),
        check_vma=False,
    )
```

```python
import math

import jax
import jax.numpy as jnp
from jax import lax
from jax.experimental import pallas as pl
from jax.experimental.pallas import tpu as pltpu
from jax.sharding import PartitionSpec as P

ORD_DEV = 2
LANES = 128
F32 = jnp.float32
BF16 = jnp.bfloat16


def limits(mib):
    return pltpu.CompilerParams(vmem_limit_bytes=mib << 20)


def on_chip(value):
    return pltpu.with_memory_space_constraint(value, pltpu.VMEM)


def off_chip(value):
    return pltpu.with_memory_space_constraint(value, pltpu.HBM)


def lane_ids(shape):
    return lax.broadcasted_iota(jnp.int32, shape, len(shape) - 1)


def swap_halves(a, b):
    low = lane_ids(a.shape) < LANES // 2
    first = jnp.where(low, a, pltpu.roll(b, LANES // 2, a.ndim - 1))
    second = jnp.where(low, pltpu.roll(a, LANES // 2, a.ndim - 1), b)
    return first, second


def forward_kernel(
    parts, ids_hbm, beam_ref, harm_ref, leg_ref, out_ref, leg_v, beam_v, harm_v, wide, lhs, ids_ref, sems
):
    degrees, lats = leg_ref.shape[1], leg_ref.shape[2]
    maps = harm_ref.shape[0]
    tiles = degrees // LANES
    step = lats // parts
    slot = lax.axis_index("order") * ORD_DEV
    group = lax.axis_index("freq")
    beam_copy = pltpu.make_async_copy(beam_ref, beam_v, sems.at[ORD_DEV * (parts + 1)])
    beam_copy.start()
    ids_copy = pltpu.make_async_copy(ids_hbm, ids_ref, sems.at[ORD_DEV * (parts + 1) + 1])
    ids_copy.start()
    harm_copies, leg_copies = [], []
    for o in range(ORD_DEV):
        base = o * (parts + 1)
        copy = pltpu.make_async_copy(harm_ref.at[:, o], harm_v.at[:, o], sems.at[base])
        copy.start()
        harm_copies.append(copy)
        for p in range(parts):
            cols = pl.ds(p * step, step)
            copy = pltpu.make_async_copy(
                leg_ref.at[o, :, cols], leg_v.at[o, :, cols], sems.at[base + 1 + p]
            )
            copy.start()
            leg_copies.append(copy)
    ids_copy.wait()
    beam_copy.wait()
    beam = beam_v[pl.ds(group, 1), :]
    degree = lane_ids((1, degrees))

    def prepare(o):
        harm_copies[o].wait()
        rows = 2 * tiles
        for b in range(maps):
            wide[o, pl.ds(b * rows, rows), :] = harm_v[b, o].astype(F32)
        shaping = jnp.where(degree >= ids_ref[slot + o], beam, 0.0)
        for t in range(tiles):
            cols = pl.ds(t * LANES, LANES)
            for c in range(2):
                values = wide[o, pl.ds(t * 2 + c, maps, stride=rows), :]
                lhs[o, pl.ds(c * maps, maps), cols] = (
                    values * shaping[:, t * LANES : (t + 1) * LANES]
                ).astype(BF16)

    prepare(0)
    for o in range(ORD_DEV):
        for p in range(parts):
            cols = pl.ds(p * step, step)
            leg_copies[o * parts + p].wait()
            sums = jnp.dot(lhs[o], leg_v[o, :, cols], preferred_element_type=F32)
            out_ref[cols, pl.ds(o * 2 * maps, 2 * maps)] = sums.T.astype(BF16)
            if o == 0 and p == 0:
                prepare(1)


def forward(order_ids, beam, harm, legendre, parts=2):
    degrees, lats = legendre.shape[1:]
    maps = harm.shape[0]
    return pl.pallas_call(
        lambda *refs: forward_kernel(parts, *refs),
        name="forward",
        out_shape=jax.ShapeDtypeStruct((lats, ORD_DEV * 2 * maps), BF16),
        in_specs=[pl.BlockSpec(memory_space=pl.ANY)] * 4,
        out_specs=pl.BlockSpec(memory_space=pltpu.VMEM),
        scratch_shapes=[
            pltpu.VMEM(legendre.shape, BF16),
            pltpu.VMEM(beam.shape, F32),
            pltpu.VMEM(harm.shape, BF16),
            pltpu.VMEM((ORD_DEV, maps * harm.shape[2], LANES), F32),
            pltpu.VMEM((ORD_DEV, 2 * maps, degrees), BF16),
            pltpu.SMEM(order_ids.shape, jnp.int32),
            pltpu.SemaphoreType.DMA((ORD_DEV * (parts + 1) + 2,)),
        ],
        compiler_params=limits(24),
    )(off_chip(order_ids), off_chip(beam), off_chip(harm), off_chip(legendre))


def table_kernel(nlon, ids_ref, out_ref, sign_ref, slots, small, fine):
    rows = ids_ref.shape[1]
    half = rows // ORD_DEV
    mids = 8
    span = mids * LANES
    coarses = out_ref.shape[1] // span
    unit = 2.0 * math.pi / nlon
    slots[...] = jnp.broadcast_to(ids_ref[...].astype(F32), (rows, rows)).T
    lane = lane_ids((half, LANES))
    steps = jnp.where(lane < LANES // 2, lane * LANES, (lane - LANES // 2) * span)
    for o in range(ORD_DEV):
        wide_ids = slots[pl.ds(o, half, stride=ORD_DEV), :]
        ids = wide_ids.astype(jnp.int32)
        factor = jnp.where((ids == 0) | (lane < LANES // 2), 1.0, 2.0)
        angle = ((ids * steps) & (nlon - 1)).astype(F32) * unit
        part = pl.ds(o * half, half)
        small[0, part, :] = factor * jnp.cos(angle)
        small[1, part, :] = factor * jnp.sin(angle)
        angle = ((ids * lane) & (nlon - 1)).astype(F32) * unit
        fine[0, part, :] = jnp.cos(angle)
        fine[1, part, :] = jnp.sin(angle)
        across = jnp.concatenate([wide_ids, wide_ids], 0).T[0:8]
        odd = across.astype(jnp.int32) & 1
        sign_ref[pl.ds(o * 8, 8), :] = (1 - 2 * odd).astype(F32)
    block = 16
    for r in range(0, rows, block):
        part = pl.ds(r, block)
        sc, ss = small[0, part, :], small[1, part, :]
        fc, fs = fine[0, part, :], fine[1, part, :]
        cos, sin = [], []
        for q in range(mids):
            mc, ms = sc[:, q : q + 1], ss[:, q : q + 1]
            cos.append(mc * fc - ms * fs)
            sin.append(ms * fc + mc * fs)
        at = (r // half) * rows + r % half
        for p in range(coarses):
            lead = LANES // 2 + p
            cc, cs = sc[:, lead : lead + 1], ss[:, lead : lead + 1]
            for q in range(mids):
                cols = pl.ds(p * span + q * LANES, LANES)
                out_ref[pl.ds(at, block), cols] = (cc * cos[q] - cs * sin[q]).astype(BF16)
                out_ref[pl.ds(at + half, block), cols] = (-(cs * cos[q] + cc * sin[q])).astype(BF16)


def make_table(order_ids, nlon):
    rows = order_ids.shape[0]
    return pl.pallas_call(
        lambda *refs: table_kernel(nlon, *refs),
        name="table",
        out_shape=(pltpu.VMEM((2 * rows, nlon // 2), BF16), pltpu.VMEM((8 * ORD_DEV, LANES), F32)),
        in_specs=[pl.BlockSpec(memory_space=pltpu.VMEM)],
        out_specs=(pl.BlockSpec(memory_space=pltpu.VMEM),) * 2,
        scratch_shapes=[
            pltpu.VMEM((rows, rows), F32),
            pltpu.VMEM((2, rows, LANES), F32),
            pltpu.VMEM((2, rows, LANES), F32),
        ],
        compiler_params=limits(8),
    )(order_ids.reshape(1, -1))


def pixel_kernel(
    groups, chunk, scales, got_ref, table_ref, sign_ref, weight_ref, leg_ref, out_ref, leg_v, wide, lhs, mixed, sem
):
    leg_copy = pltpu.make_async_copy(leg_ref, leg_v, sem)
    leg_copy.start()
    fwd_scale, back_scale = scales
    rows = weight_ref.shape[0]
    pairs = got_ref.shape[0] // rows
    maps = got_ref.shape[1] // (2 * ORD_DEV)
    size = rows * maps
    half = table_ref.shape[1]
    wide[...] = got_ref[...].astype(F32)
    signs = [sign_ref[pl.ds(o * 8, 1), :] for o in range(ORD_DEV)]
    for r in range(0, rows, 2):
        stacked = jnp.concatenate(
            [wide[pl.ds(r + i, pairs, stride=rows), :] for i in range(2)], 0
        )
        turned = stacked.T
        for o in range(ORD_DEV):
            cos = turned[(2 * o) * maps : (2 * o + 1) * maps]
            sin = turned[(2 * o + 1) * maps : (2 * o + 2) * maps]
            for i, part in enumerate(swap_halves(cos, sin)):
                cols = pl.ds(o * LANES, LANES)
                lhs[pl.ds((r + i) * maps, maps), cols] = part.astype(BF16)
                lhs[pl.ds(size + (r + i) * maps, maps), cols] = (part * signs[o]).astype(BF16)
    total = jnp.zeros((2 * size, 2 * LANES), F32)
    for j in range(half // chunk):
        cols = pl.ds(j * chunk, chunk)
        part = table_ref[:, cols]
        field = jnp.dot(lhs[...], part, preferred_element_type=F32)
        pieces = []
        for h in range(2):
            weight = weight_ref[:, pl.ds(h * half + j * chunk, chunk)] * fwd_scale
            for r in range(rows):
                at = h * size + r * maps
                pieces.append((field[at : at + maps] * weight[r : r + 1]).astype(BF16))
        total += lax.dot_general(
            jnp.concatenate(pieces, 0), part, (((1,), (1,)), ((), ())), preferred_element_type=F32
        )
    sign = jnp.concatenate(signs, 1)
    total = (total[:size] + total[size:] * sign) * back_scale
    own = maps // groups
    low_rows = rows // 2
    for f in range(groups):
        pieces = []
        for low in range(low_rows):
            for o in range(ORD_DEV):
                at = [(high * low_rows + low) * maps + f * own for high in range(2)]
                pieces += list(
                    swap_halves(
                        *[total[a : a + own, o * LANES : (o + 1) * LANES] for a in at]
                    )
                )
        turned = jnp.concatenate(pieces, 0).T
        for high in range(2):
            mixed[pl.ds(f * 2 * pairs + high, pairs, stride=2), :] = turned[
                high * pairs : (high + 1) * pairs
            ]
    out_ref[...] = mixed[...].astype(BF16)
    leg_copy.wait()


def pixels(got, table, signs, weight, legendre, groups, scales, chunk=512):
    return pl.pallas_call(
        lambda *refs: pixel_kernel(groups, chunk, scales, *refs),
        name="pixels",
        out_shape=(pltpu.VMEM(got.shape, BF16), pltpu.VMEM(legendre.shape, BF16)),
        in_specs=[pl.BlockSpec(memory_space=pltpu.VMEM)] * 4 + [pl.BlockSpec(memory_space=pl.ANY)],
        out_specs=(pl.BlockSpec(memory_space=pltpu.VMEM),) * 2,
        scratch_shapes=[
            pltpu.VMEM(got.shape, F32),
            pltpu.VMEM((got.shape[0], 2 * LANES), BF16),
            pltpu.VMEM(got.shape, F32),
            pltpu.SemaphoreType.DMA,
        ],
        compiler_params=limits(8),
    )(on_chip(got), table, signs, on_chip(weight), off_chip(legendre))


def backward_kernel(parts, ids_ref, beam_ref, got_ref, leg_ref, out_ref, mixed):
    degrees, lats = leg_ref.shape[1], leg_ref.shape[2]
    groups = beam_ref.shape[0]
    tiles = degrees // LANES
    step = degrees // parts
    slot = lax.axis_index("order") * ORD_DEV
    span = got_ref.shape[0] // groups
    width = LANES // groups
    lows = lats // span
    own = width // (2 * ORD_DEV)
    blocks = [got_ref[pl.ds(f * span, span), :].astype(F32) for f in range(groups)]
    lane_group = lane_ids((span, LANES)) // width
    turned = [
        [v if k == 0 else pltpu.roll(v, k * width, 1) for k in range(groups)] for v in blocks
    ]
    for low in range(lows):
        merged = turned[0][(0 - low) % groups]
        for f in range(1, groups):
            merged = jnp.where(lane_group == f, turned[f][(f - low) % groups], merged)
        mixed[pl.ds(low, span, stride=lows), :] = merged
    rows = mixed[...].T.astype(BF16)
    degree = lane_ids((1, degrees))
    for o in range(ORD_DEV):
        lhs = jnp.concatenate(
            [
                rows[f * width + o * 2 * own : f * width + (o + 1) * 2 * own]
                for f in range(groups)
            ],
            0,
        )
        for p in range(parts):
            cols = slice(p * step, (p + 1) * step)
            terms = lax.dot_general(
                lhs,
                leg_ref[o, pl.ds(p * step, step), :],
                (((1,), (1,)), ((), ())),
                preferred_element_type=F32,
            )
            live = degree[:, cols] >= ids_ref[slot + o]
            total = jnp.zeros((2 * own, step), F32)
            for f in range(groups):
                shaping = jnp.where(live, beam_ref[f : f + 1, cols], 0.0)
                total += terms[f * 2 * own : (f + 1) * 2 * own] * shaping
            for t in range(tiles // parts):
                for c in range(2):
                    at = o * tiles * 2 + (p * tiles // parts + t) * 2 + c
                    out_ref[pl.ds(at, own, stride=ORD_DEV * tiles * 2), :] = total[
                        c * own : (c + 1) * own, t * LANES : (t + 1) * LANES
                    ]


def backward(order_ids, beam, got, legendre, own, parts=4):
    degrees = legendre.shape[1]
    return pl.pallas_call(
        lambda *refs: backward_kernel(parts, *refs),
        name="backward",
        out_shape=jax.ShapeDtypeStruct((own * ORD_DEV * 2 * degrees // LANES, LANES), F32),
        in_specs=[
            pl.BlockSpec(memory_space=pltpu.SMEM),
            pl.BlockSpec(memory_space=pltpu.VMEM),
            pl.BlockSpec(memory_space=pltpu.VMEM),
            pl.BlockSpec(memory_space=pltpu.VMEM),
        ],
        out_specs=pl.BlockSpec(memory_space=pltpu.VMEM),
        scratch_shapes=[
            pltpu.VMEM((legendre.shape[2], LANES), F32),
        ],
        compiler_params=limits(8),
    )(order_ids, on_chip(beam), on_chip(got), legendre)


def on_device(harmonics, legendre, beam_window, order_ids, noise_weight):
    maps, _, _, degrees = harmonics.shape
    lats = legendre.shape[2]
    nlon = noise_weight.shape[2]
    orders_all = order_ids.shape[0]
    groups = beam_window.shape[0]
    tiles = degrees // LANES
    own = maps // groups
    pairs = orders_all // ORD_DEV
    scales = (1.0 / math.sqrt(2.0 * orders_all), 1.0 / math.sqrt(1.0 * nlon))
    harm = harmonics.reshape(maps, ORD_DEV, 2, tiles, LANES).transpose(0, 1, 3, 2, 4)
    harm = harm.reshape(maps, ORD_DEV, -1, LANES)
    columns = forward(order_ids, beam_window, harm, legendre)
    columns = columns.reshape(pairs, lats // pairs, -1)
    got = lax.all_to_all(columns, "order", split_axis=0, concat_axis=0, tiled=True)
    table, signs = make_table(order_ids, nlon)
    terms, legendre = pixels(
        got.reshape(lats, -1), table, signs, noise_weight[0], legendre, groups, scales
    )
    terms = terms.reshape(groups * pairs, -1, LANES)
    back = lax.all_to_all(terms, ("freq", "order"), split_axis=0, concat_axis=0, tiled=True)
    out = backward(order_ids, beam_window, back.reshape(-1, LANES), legendre, own)
    out = out.reshape(own, ORD_DEV, tiles, 2, LANES).transpose(0, 1, 3, 2, 4)
    return out.reshape(own, ORD_DEV, 2, degrees)


def solution(mesh):
    return jax.shard_map(
        on_device,
        mesh=mesh,
        in_specs=(
            P(None, "order", None, None),
            P("order", None, None),
            P(),
            P(),
            P("freq", "order", None),
        ),
        out_specs=P("freq", "order", None, None),
        check_vma=False,
    )
```

```python
import math

import jax
import jax.numpy as jnp
from jax import lax
from jax.experimental import pallas as pl
from jax.experimental.pallas import tpu as pltpu
from jax.sharding import PartitionSpec as P

ORD_DEV = 2
LANES = 128
F32 = jnp.float32
BF16 = jnp.bfloat16


def limits(mib):
    return pltpu.CompilerParams(vmem_limit_bytes=mib << 20)


def on_chip(value):
    return pltpu.with_memory_space_constraint(value, pltpu.VMEM)


def off_chip(value):
    return pltpu.with_memory_space_constraint(value, pltpu.HBM)


def lane_ids(shape):
    return lax.broadcasted_iota(jnp.int32, shape, len(shape) - 1)


def swap_halves(a, b):
    low = lane_ids(a.shape) < LANES // 2
    first = jnp.where(low, a, pltpu.roll(b, LANES // 2, a.ndim - 1))
    second = jnp.where(low, pltpu.roll(a, LANES // 2, a.ndim - 1), b)
    return first, second


def table_angles(nlon, ids_row, sign_ref, slots, small, fine, mids):
    rows = ids_row.shape[1]
    half = rows // ORD_DEV
    unit = 2.0 * math.pi / nlon
    slots[...] = jnp.broadcast_to(ids_row.astype(F32), (rows, rows)).T
    lane = lane_ids((half, LANES))
    steps = jnp.where(lane < LANES // 2, lane * LANES, (lane - LANES // 2) * (mids * LANES))
    for o in range(ORD_DEV):
        wide_ids = slots[pl.ds(o, half, stride=ORD_DEV), :]
        ids = wide_ids.astype(jnp.int32)
        factor = jnp.where((ids == 0) | (lane < LANES // 2), 1.0, 2.0)
        angle = ((ids * steps) & (nlon - 1)).astype(F32) * unit
        part = pl.ds(o * half, half)
        small[0, part, :] = factor * jnp.cos(angle)
        small[1, part, :] = factor * jnp.sin(angle)
        angle = ((ids * lane) & (nlon - 1)).astype(F32) * unit
        fine[0, part, :] = jnp.cos(angle)
        fine[1, part, :] = jnp.sin(angle)
        across = jnp.concatenate([wide_ids, wide_ids], 0).T[0:8]
        odd = across.astype(jnp.int32) & 1
        sign_ref[pl.ds(o * 8, 8), :] = (1 - 2 * odd).astype(F32)


def table_rows(out_ref, small, fine, mids, blocks):
    rows = small.shape[1]
    half = rows // ORD_DEV
    span = mids * LANES
    coarses = out_ref.shape[1] // span
    block = 16
    shape = (block, LANES)
    for r in blocks:
        part = pl.ds(r, block)
        sc, ss = small[0, part, :], small[1, part, :]
        fc, fs = fine[0, part, :], fine[1, part, :]
        at = (r // half) * rows + r % half
        lead = []
        for p in range(coarses):
            k = LANES // 2 + p
            cs = jnp.broadcast_to(ss[:, k : k + 1], shape)
            lead.append((jnp.broadcast_to(sc[:, k : k + 1], shape), cs))
        for q in range(mids):
            mc = jnp.broadcast_to(sc[:, q : q + 1], shape)
            ms = jnp.broadcast_to(ss[:, q : q + 1], shape)
            cos = mc * fc - ms * fs
            sin = ms * fc + mc * fs
            for p in range(coarses):
                cc, cs = lead[p]
                cols = pl.ds(p * span + q * LANES, LANES)
                out_ref[pl.ds(at, block), cols] = (cc * cos - cs * sin).astype(BF16)
                out_ref[pl.ds(at + half, block), cols] = (-(cs * cos) - cc * sin).astype(BF16)


def live_steps(ids_ref, slot, tiles):
    first = [ids_ref[slot + o] // LANES for o in range(ORD_DEV)]
    count = tiles - first[0]
    steps = []
    for i in range(tiles + 1):
        later = i >= count
        order = jnp.where(later, 1, 0)
        steps.append((order, jnp.where(later, first[1] + i - count, first[0] + i)))
    return steps


def forward_kernel(
    nlon,
    cuts,
    ids_hbm,
    ids_row_hbm,
    beam_ref,
    harm_ref,
    leg_ref,
    out_ref,
    leg_v,
    table_ref,
    sign_ref,
    ids_row,
    beam_v,
    own_beam,
    harm_v,
    wide,
    lhs,
    slots,
    small,
    fine,
    ids_ref,
    sems,
    leg_sems,
):
    degrees = leg_ref.shape[1]
    maps = harm_ref.shape[0]
    tiles = degrees // LANES
    rows = 2 * tiles
    mids = 8
    slot = lax.axis_index("order") * ORD_DEV
    group = lax.axis_index("freq")
    copies = [
        pltpu.make_async_copy(ids_hbm, ids_ref, sems.at[0]),
        pltpu.make_async_copy(ids_row_hbm, ids_row, sems.at[1]),
        pltpu.make_async_copy(beam_ref, beam_v, sems.at[2]),
        pltpu.make_async_copy(harm_ref, harm_v, sems.at[3]),
    ]
    for copy in copies:
        copy.start()
    copies[0].wait()
    steps = live_steps(ids_ref, slot, tiles)
    leg_copies = []
    for i, (order, tile) in enumerate(steps):
        copy = pltpu.make_async_copy(
            leg_ref.at[order, pl.ds(pl.multiple_of(tile * LANES, LANES), LANES), :],
            leg_v.at[pl.ds(i * LANES, LANES), :],
            leg_sems.at[i],
        )
        copy.start()
        leg_copies.append(copy)
    copies[1].wait()
    table_angles(nlon, ids_row[...], sign_ref, slots, small, fine, mids)
    copies[2].wait()
    own_beam[...] = beam_v[pl.ds(group, 1), :]
    copies[3].wait()
    for b in range(maps):
        for o in range(ORD_DEV):
            wide[pl.ds((b * ORD_DEV + o) * rows, rows), :] = harm_v[b, o].astype(F32)
    lane = lane_ids((1, LANES))
    blank = jnp.zeros((2 * maps, LANES), BF16)
    for i, (order, tile) in enumerate(steps):
        start = pl.multiple_of(tile * LANES, LANES)
        live = lane + start >= ids_ref[slot + order]
        shaping = jnp.where(live, own_beam[:, pl.ds(start, LANES)], 0.0)
        at = pl.multiple_of(order * (2 * maps), 2 * maps)
        cols = pl.ds(i * LANES, LANES)
        lhs[pl.ds(2 * maps - at, 2 * maps), cols] = blank
        for c in range(2):
            values = wide[pl.ds(order * rows + tile * 2 + c, maps, stride=ORD_DEV * rows), :]
            lhs[pl.ds(at + c * maps, maps), cols] = (values * shaping).astype(BF16)
    table_rows(table_ref, small, fine, mids, range(0, small.shape[1], 16))
    total = None
    for lo, hi in zip(cuts[:-1], cuts[1:]):
        for copy in leg_copies[lo:hi]:
            copy.wait()
        span = pl.ds(lo * LANES, (hi - lo) * LANES)
        part = jnp.dot(lhs[:, span], leg_v[span, :], preferred_element_type=F32)
        total = part if total is None else total + part
    out_ref[...] = total.T.astype(BF16)


def forward(order_ids, beam, harm, legendre, nlon):
    degrees, lats = legendre.shape[1:]
    maps = harm.shape[0]
    orders = order_ids.shape[0]
    ids_row = order_ids.reshape(1, -1)
    steps = degrees // LANES + 1
    cuts = (0, steps)
    return pl.pallas_call(
        lambda *refs: forward_kernel(nlon, cuts, *refs),
        name="forward",
        out_shape=(
            pltpu.VMEM((lats, ORD_DEV * 2 * maps), BF16),
            pltpu.VMEM((steps * LANES, lats), BF16),
            pltpu.VMEM((2 * orders, nlon // 2), BF16),
            pltpu.VMEM((8 * ORD_DEV, LANES), F32),
        ),
        in_specs=[pl.BlockSpec(memory_space=pl.ANY)] * 5,
        out_specs=(pl.BlockSpec(memory_space=pltpu.VMEM),) * 4,
        scratch_shapes=[
            pltpu.VMEM(ids_row.shape, jnp.int32),
            pltpu.VMEM(beam.shape, F32),
            pltpu.VMEM((1, degrees), F32),
            pltpu.VMEM(harm.shape, BF16),
            pltpu.VMEM((maps * ORD_DEV * harm.shape[2], LANES), F32),
            pltpu.VMEM((ORD_DEV * 2 * maps, steps * LANES), BF16),
            pltpu.VMEM((orders, orders), F32),
            pltpu.VMEM((2, orders, LANES), F32),
            pltpu.VMEM((2, orders, LANES), F32),
            pltpu.SMEM(order_ids.shape, jnp.int32),
            pltpu.SemaphoreType.DMA((4,)),
            pltpu.SemaphoreType.DMA((steps,)),
        ],
        compiler_params=limits(16),
    )(*[off_chip(v) for v in (order_ids, ids_row, beam, harm, legendre)])


def pixel_kernel(
    groups, chunk, scales, got_ref, table_ref, sign_ref, weight_ref, out_ref, wide, lhs, mixed
):
    fwd_scale, back_scale = scales
    rows = weight_ref.shape[0]
    pairs = got_ref.shape[0] // rows
    maps = got_ref.shape[1] // (2 * ORD_DEV)
    size = rows * maps
    half = table_ref.shape[1]
    wide[...] = got_ref[...].astype(F32)
    signs = [sign_ref[pl.ds(o * 8, 1), :] for o in range(ORD_DEV)]
    for r in range(0, rows, 2):
        stacked = jnp.concatenate(
            [wide[pl.ds(r + i, pairs, stride=rows), :] for i in range(2)], 0
        )
        turned = stacked.T
        for o in range(ORD_DEV):
            cos = turned[(2 * o) * maps : (2 * o + 1) * maps]
            sin = turned[(2 * o + 1) * maps : (2 * o + 2) * maps]
            for i, part in enumerate(swap_halves(cos, sin)):
                cols = pl.ds(o * LANES, LANES)
                lhs[pl.ds((r + i) * maps, maps), cols] = part.astype(BF16)
                lhs[pl.ds(size + (r + i) * maps, maps), cols] = (part * signs[o]).astype(BF16)
    total = jnp.zeros((2 * size, 2 * LANES), F32)
    for j in range(half // chunk):
        cols = pl.ds(j * chunk, chunk)
        part = table_ref[:, cols]
        field = jnp.dot(lhs[...], part, preferred_element_type=F32)
        pieces = []
        for h in range(2):
            weight = weight_ref[:, pl.ds(h * half + j * chunk, chunk)] * fwd_scale
            for r in range(rows):
                at = h * size + r * maps
                pieces.append((field[at : at + maps] * weight[r : r + 1]).astype(BF16))
        total += lax.dot_general(
            jnp.concatenate(pieces, 0), part, (((1,), (1,)), ((), ())), preferred_element_type=F32
        )
    sign = jnp.concatenate(signs, 1)
    total = (total[:size] + total[size:] * sign) * back_scale
    own = maps // groups
    low_rows = rows // 2
    for f in range(groups):
        pieces = []
        for low in range(low_rows):
            for o in range(ORD_DEV):
                at = [(high * low_rows + low) * maps + f * own for high in range(2)]
                pieces += list(
                    swap_halves(
                        *[total[a : a + own, o * LANES : (o + 1) * LANES] for a in at]
                    )
                )
        turned = jnp.concatenate(pieces, 0).T
        for high in range(2):
            mixed[pl.ds(f * 2 * pairs + high, pairs, stride=2), :] = turned[
                high * pairs : (high + 1) * pairs
            ]
    out_ref[...] = mixed[...].astype(BF16)


def pixels(got, table, signs, weight, groups, scales, chunk=256):
    return pl.pallas_call(
        lambda *refs: pixel_kernel(groups, chunk, scales, *refs),
        name="pixels",
        out_shape=pltpu.VMEM(got.shape, BF16),
        in_specs=[pl.BlockSpec(memory_space=pltpu.VMEM)] * 4,
        out_specs=pl.BlockSpec(memory_space=pltpu.VMEM),
        scratch_shapes=[
            pltpu.VMEM(got.shape, F32),
            pltpu.VMEM((got.shape[0], 2 * LANES), BF16),
            pltpu.VMEM(got.shape, F32),
        ],
        compiler_params=limits(8),
    )(on_chip(got), table, signs, on_chip(weight))


def backward_kernel(cuts, ids_ref, beam_ref, got_ref, leg_ref, out_ref, mixed, terms):
    lats = leg_ref.shape[1]
    groups, degrees = beam_ref.shape
    tiles = degrees // LANES
    slot = lax.axis_index("order") * ORD_DEV
    span = got_ref.shape[0] // groups
    width = LANES // groups
    lows = lats // span
    own = width // (2 * ORD_DEV)
    blocks = [got_ref[pl.ds(f * span, span), :].astype(F32) for f in range(groups)]
    lane_group = lane_ids((span, LANES)) // width
    turned = [
        [v if k == 0 else pltpu.roll(v, k * width, 1) for k in range(groups)] for v in blocks
    ]
    for low in range(lows):
        merged = turned[0][(0 - low) % groups]
        for f in range(1, groups):
            merged = jnp.where(lane_group == f, turned[f][(f - low) % groups], merged)
        mixed[pl.ds(low, span, stride=lows), :] = merged
    rows = mixed[...].T.astype(BF16)
    lhs = jnp.concatenate(
        [
            rows[f * width + o * 2 * own : f * width + (o + 1) * 2 * own]
            for o in range(ORD_DEV)
            for f in range(groups)
        ],
        0,
    )
    out_ref[...] = jnp.zeros_like(out_ref)
    lane = lane_ids((1, LANES))
    steps = live_steps(ids_ref, slot, tiles)
    half = groups * 2 * own
    for lo, hi in zip(cuts[:-1], cuts[1:]):
        cols = pl.ds(lo * LANES, (hi - lo) * LANES)
        terms[:, cols] = lax.dot_general(
            lhs, leg_ref[cols, :], (((1,), (1,)), ((), ())), preferred_element_type=F32
        )
        for i in range(lo, hi):
            order, tile = steps[i]
            start = pl.multiple_of(tile * LANES, LANES)
            live = lane + start >= ids_ref[slot + order]
            part = terms[pl.ds(pl.multiple_of(order * half, half), half), pl.ds(i * LANES, LANES)]
            total = jnp.zeros((2 * own, LANES), F32)
            for f in range(groups):
                shaping = jnp.where(live, beam_ref[f : f + 1, pl.ds(start, LANES)], 0.0)
                total += part[f * 2 * own : (f + 1) * 2 * own] * shaping
            for c in range(2):
                out_ref[:, order * 2 * tiles + tile * 2 + c, :] = total[c * own : (c + 1) * own]


def backward(order_ids, beam, got, legendre, own):
    degrees = beam.shape[1]
    shape = (own, ORD_DEV * 2 * degrees // LANES, LANES)
    cuts = (0, 33)
    return pl.pallas_call(
        lambda *refs: backward_kernel(cuts, *refs),
        name="backward",
        out_shape=jax.ShapeDtypeStruct(shape, F32),
        in_specs=[pl.BlockSpec(memory_space=pltpu.SMEM)] + [pl.BlockSpec(memory_space=pltpu.VMEM)] * 3,
        out_specs=pl.BlockSpec(memory_space=pltpu.VMEM),
        scratch_shapes=[
            pltpu.VMEM((legendre.shape[1], LANES), F32),
            pltpu.VMEM((LANES, legendre.shape[0]), F32),
        ],
        compiler_params=limits(8),
    )(order_ids, on_chip(beam), on_chip(got), legendre)


def on_device(harmonics, legendre, beam_window, order_ids, noise_weight):
    maps, _, _, degrees = harmonics.shape
    lats = legendre.shape[2]
    nlon = noise_weight.shape[2]
    orders_all = order_ids.shape[0]
    groups = beam_window.shape[0]
    tiles = degrees // LANES
    own = maps // groups
    pairs = orders_all // ORD_DEV
    scales = (1.0 / math.sqrt(2.0 * orders_all), 1.0 / math.sqrt(1.0 * nlon))
    harm = harmonics.reshape(maps, ORD_DEV, 2, tiles, LANES).transpose(0, 1, 3, 2, 4)
    harm = harm.reshape(maps, ORD_DEV, -1, LANES)
    columns, legendre, table, signs = forward(order_ids, beam_window, harm, legendre, nlon)
    columns = columns.reshape(pairs, lats // pairs, -1)
    got = lax.all_to_all(columns, "order", split_axis=0, concat_axis=0, tiled=True)
    terms = pixels(got.reshape(lats, -1), table, signs, noise_weight[0], groups, scales)
    terms = terms.reshape(groups * pairs, -1, LANES)
    back = lax.all_to_all(terms, ("freq", "order"), split_axis=0, concat_axis=0, tiled=True)
    out = backward(order_ids, beam_window, back.reshape(-1, LANES), legendre, own)
    out = out.reshape(own, ORD_DEV, tiles, 2, LANES).transpose(0, 1, 3, 2, 4)
    return out.reshape(own, ORD_DEV, 2, degrees)


def solution(mesh):
    return jax.shard_map(
        on_device,
        mesh=mesh,
        in_specs=(
            P(None, "order", None, None),
            P("order", None, None),
            P(),
            P(),
            P("freq", "order", None),
        ),
        out_specs=P("freq", "order", None, None),
        check_vma=False,
    )
```

```python
import math

import jax
import jax.numpy as jnp
from jax import lax
from jax.experimental import pallas as pl
from jax.experimental.pallas import tpu as pltpu
from jax.sharding import PartitionSpec as P

ORD_DEV = 2
LANES = 128
F32 = jnp.float32
BF16 = jnp.bfloat16


def limits(mib):
    return pltpu.CompilerParams(vmem_limit_bytes=mib << 20)


def on_chip(value):
    return pltpu.with_memory_space_constraint(value, pltpu.VMEM)


def off_chip(value):
    return pltpu.with_memory_space_constraint(value, pltpu.HBM)


def lane_ids(shape):
    return lax.broadcasted_iota(jnp.int32, shape, len(shape) - 1)


def swap_halves(a, b):
    low = lane_ids(a.shape) < LANES // 2
    first = jnp.where(low, a, pltpu.roll(b, LANES // 2, a.ndim - 1))
    second = jnp.where(low, pltpu.roll(a, LANES // 2, a.ndim - 1), b)
    return first, second


def table_angles(nlon, ids_row, sign_ref, slots, small, fine, mids):
    rows = ids_row.shape[1]
    half = rows // ORD_DEV
    unit = 2.0 * math.pi / nlon
    slots[...] = jnp.broadcast_to(ids_row.astype(F32), (rows, rows)).T
    lane = lane_ids((half, LANES))
    steps = jnp.where(lane < LANES // 2, lane * LANES, (lane - LANES // 2) * (mids * LANES))
    for o in range(ORD_DEV):
        wide_ids = slots[pl.ds(o, half, stride=ORD_DEV), :]
        ids = wide_ids.astype(jnp.int32)
        factor = jnp.where((ids == 0) | (lane < LANES // 2), 1.0, 2.0)
        angle = ((ids * steps) & (nlon - 1)).astype(F32) * unit
        part = pl.ds(o * half, half)
        small[0, part, :] = factor * jnp.cos(angle)
        small[1, part, :] = factor * jnp.sin(angle)
        angle = ((ids * lane) & (nlon - 1)).astype(F32) * unit
        fine[0, part, :] = jnp.cos(angle)
        fine[1, part, :] = jnp.sin(angle)
        across = jnp.concatenate([wide_ids, wide_ids], 0).T[0:8]
        odd = across.astype(jnp.int32) & 1
        sign_ref[pl.ds(o * 8, 8), :] = (1 - 2 * odd).astype(F32)


def table_rows(out_ref, small, fine, mids, blocks):
    rows = small.shape[1]
    half = rows // ORD_DEV
    span = mids * LANES
    coarses = out_ref.shape[1] // span
    block = 16
    shape = (block, LANES)
    for r in blocks:
        part = pl.ds(r, block)
        sc, ss = small[0, part, :], small[1, part, :]
        fc, fs = fine[0, part, :], fine[1, part, :]
        at = (r // half) * rows + r % half
        lead = []
        for p in range(coarses):
            k = LANES // 2 + p
            cs = jnp.broadcast_to(ss[:, k : k + 1], shape)
            lead.append((jnp.broadcast_to(sc[:, k : k + 1], shape), cs))
        for q in range(mids):
            mc = jnp.broadcast_to(sc[:, q : q + 1], shape)
            ms = jnp.broadcast_to(ss[:, q : q + 1], shape)
            cos = mc * fc - ms * fs
            sin = ms * fc + mc * fs
            for p in range(coarses):
                cc, cs = lead[p]
                cols = pl.ds(p * span + q * LANES, LANES)
                out_ref[pl.ds(at, block), cols] = (cc * cos - cs * sin).astype(BF16)
                out_ref[pl.ds(at + half, block), cols] = (-(cs * cos) - cc * sin).astype(BF16)


TILE = 2 * LANES


def lower_slot(ids_ref, slot):
    return jnp.where(ids_ref[slot] < ids_ref[slot + 1], 0, 1)


def live_steps(ids_ref, slot, degrees):
    tiles = degrees // TILE
    low = lower_slot(ids_ref, slot)
    first_low = ids_ref[slot + low] // TILE
    first_high = ids_ref[slot + 1 - low] // TILE
    count = tiles // 2 - first_low
    steps = [(low, degrees // 2 + k * TILE) for k in range(tiles // 2)]
    for k in range(tiles // 2 + 1):
        later = k >= count
        tile = jnp.where(later, first_high + k - count, first_low + k)
        steps.append((jnp.where(later, 1 - low, low), pl.multiple_of(tile * TILE, TILE)))
    return steps


def dead_steps(ids_ref, slot, degrees):
    tiles = degrees // TILE
    low = lower_slot(ids_ref, slot)
    count = ids_ref[slot + low] // TILE
    steps = []
    for k in range(tiles - 1):
        later = k >= count
        tile = jnp.where(later, k - count, k)
        steps.append((jnp.where(later, 1 - low, low), pl.multiple_of(tile * TILE, TILE)))
    return steps


def forward_kernel(
    nlon,
    plan,
    ids_hbm,
    ids_row_hbm,
    beam_ref,
    harm_ref,
    leg_ref,
    out_ref,
    leg_v,
    table_ref,
    sign_ref,
    ids_row,
    beam_v,
    own_beam,
    harm_v,
    wide,
    lhs,
    slots,
    small,
    fine,
    ids_ref,
    sems,
    leg_sems,
):
    degrees = leg_ref.shape[1]
    upper = degrees // 2
    maps = harm_ref.shape[0]
    rows = harm_ref.shape[2]
    mids = 8
    slot = lax.axis_index("order") * ORD_DEV
    group = lax.axis_index("freq")
    copies = [
        pltpu.make_async_copy(ids_hbm, ids_ref, sems.at[0]),
        pltpu.make_async_copy(ids_row_hbm, ids_row, sems.at[1]),
        pltpu.make_async_copy(beam_ref, beam_v, sems.at[2]),
        pltpu.make_async_copy(harm_ref, harm_v, sems.at[3]),
    ]

    def upper_copy(order):
        return pltpu.make_async_copy(
            leg_ref.at[order, pl.ds(upper, upper), :], leg_v.at[pl.ds(0, upper), :], sems.at[4]
        )

    for copy in copies:
        copy.start()
    upper_copy(0).start()
    copies[0].wait()
    steps = live_steps(ids_ref, slot, degrees)
    fixed = upper // TILE
    leg_copies = []
    for k, (order, start) in enumerate(steps[fixed:]):
        copy = pltpu.make_async_copy(
            leg_ref.at[order, pl.ds(start, TILE), :],
            leg_v.at[pl.ds(upper + k * TILE, TILE), :],
            leg_sems.at[k],
        )
        copy.start()
        leg_copies.append(copy)
    copies[1].wait()
    table_angles(nlon, ids_row[...], sign_ref, slots, small, fine, mids)
    copies[2].wait()
    own_beam[...] = beam_v[pl.ds(group, 1), :]
    copies[3].wait()
    for b in range(maps):
        for o in range(ORD_DEV):
            wide[pl.ds((b * ORD_DEV + o) * rows, rows), :] = harm_v[b, o].astype(F32)
    lane = lane_ids((1, LANES))
    blank = jnp.zeros((2 * maps, TILE), BF16)

    def prepare(some):
        for i in some:
            order, first = steps[i]
            at = pl.multiple_of(order * (2 * maps), 2 * maps)
            lhs[pl.ds(2 * maps - at, 2 * maps), pl.ds(i * TILE, TILE)] = blank
            for t in range(TILE // LANES):
                start = first + t * LANES
                if not isinstance(start, int):
                    start = pl.multiple_of(start, LANES)
                live = lane + start >= ids_ref[slot + order]
                shaping = jnp.where(live, own_beam[:, pl.ds(start, LANES)], 0.0)
                for c in range(2):
                    row = order * rows + start // LANES * 2 + c
                    values = wide[pl.ds(row, maps, stride=ORD_DEV * rows), :]
                    lhs[pl.ds(at + c * maps, maps), pl.ds(i * TILE + t * LANES, LANES)] = (
                        values * shaping
                    ).astype(BF16)

    table_blocks = list(range(0, small.shape[1], 16))
    prepare(range(fixed))
    table_rows(table_ref, small, fine, mids, table_blocks[: plan[0]])
    upper_copy(0).wait()

    @pl.when(lower_slot(ids_ref, slot) == 1)
    def _():
        copy = upper_copy(1)
        copy.start()
        copy.wait()

    total = jnp.dot(lhs[:, pl.ds(0, upper)], leg_v[pl.ds(0, upper), :], preferred_element_type=F32)
    prepare(range(fixed, len(steps)))
    table_rows(table_ref, small, fine, mids, table_blocks[plan[0] : plan[1]])
    for copy in leg_copies:
        copy.wait()
    rest = pl.ds(upper, leg_v.shape[0] - upper)
    total += jnp.dot(lhs[:, rest], leg_v[rest, :], preferred_element_type=F32)
    table_rows(table_ref, small, fine, mids, table_blocks[plan[1] :])
    out_ref[...] = total.T.astype(BF16)


def forward(order_ids, beam, harm, legendre, nlon):
    degrees, lats = legendre.shape[1:]
    maps = harm.shape[0]
    orders = order_ids.shape[0]
    ids_row = order_ids.reshape(1, -1)
    live = degrees + TILE
    return pl.pallas_call(
        lambda *refs: forward_kernel(nlon, (2, 5), *refs),
        name="forward",
        out_shape=(
            pltpu.VMEM((lats, ORD_DEV * 2 * maps), BF16),
            pltpu.VMEM((live, lats), BF16),
            pltpu.VMEM((2 * orders, nlon // 2), BF16),
            pltpu.VMEM((8 * ORD_DEV, LANES), F32),
        ),
        in_specs=[pl.BlockSpec(memory_space=pl.ANY)] * 5,
        out_specs=(pl.BlockSpec(memory_space=pltpu.VMEM),) * 4,
        scratch_shapes=[
            pltpu.VMEM(ids_row.shape, jnp.int32),
            pltpu.VMEM(beam.shape, F32),
            pltpu.VMEM((1, degrees), F32),
            pltpu.VMEM(harm.shape, BF16),
            pltpu.VMEM((maps * ORD_DEV * harm.shape[2], LANES), F32),
            pltpu.VMEM((ORD_DEV * 2 * maps, live), BF16),
            pltpu.VMEM((orders, orders), F32),
            pltpu.VMEM((2, orders, LANES), F32),
            pltpu.VMEM((2, orders, LANES), F32),
            pltpu.SMEM(order_ids.shape, jnp.int32),
            pltpu.SemaphoreType.DMA((5,)),
            pltpu.SemaphoreType.DMA((degrees // TILE // 2 + 1,)),
        ],
        compiler_params=limits(16),
    )(*[off_chip(v) for v in (order_ids, ids_row, beam, harm, legendre)])


def pixel_kernel(
    groups, chunk, scales, got_ref, table_ref, sign_ref, weight_ref, out_ref, wide, lhs, mixed
):
    fwd_scale, back_scale = scales
    rows = weight_ref.shape[0]
    pairs = got_ref.shape[0] // rows
    maps = got_ref.shape[1] // (2 * ORD_DEV)
    size = rows * maps
    half = table_ref.shape[1]
    wide[...] = got_ref[...].astype(F32)
    signs = [sign_ref[pl.ds(o * 8, 1), :] for o in range(ORD_DEV)]
    for r in range(0, rows, 2):
        stacked = jnp.concatenate(
            [wide[pl.ds(r + i, pairs, stride=rows), :] for i in range(2)], 0
        )
        turned = stacked.T
        for o in range(ORD_DEV):
            cos = turned[(2 * o) * maps : (2 * o + 1) * maps]
            sin = turned[(2 * o + 1) * maps : (2 * o + 2) * maps]
            for i, part in enumerate(swap_halves(cos, sin)):
                cols = pl.ds(o * LANES, LANES)
                lhs[pl.ds((r + i) * maps, maps), cols] = part.astype(BF16)
                lhs[pl.ds(size + (r + i) * maps, maps), cols] = (part * signs[o]).astype(BF16)
    total = jnp.zeros((2 * size, 2 * LANES), F32)
    for j in range(half // chunk):
        cols = pl.ds(j * chunk, chunk)
        part = table_ref[:, cols]
        field = jnp.dot(lhs[...], part, preferred_element_type=F32)
        pieces = []
        for h in range(2):
            weight = weight_ref[:, pl.ds(h * half + j * chunk, chunk)] * fwd_scale
            for r in range(rows):
                at = h * size + r * maps
                pieces.append((field[at : at + maps] * weight[r : r + 1]).astype(BF16))
        total += lax.dot_general(
            jnp.concatenate(pieces, 0), part, (((1,), (1,)), ((), ())), preferred_element_type=F32
        )
    sign = jnp.concatenate(signs, 1)
    total = (total[:size] + total[size:] * sign) * back_scale
    own = maps // groups
    low_rows = rows // 2
    for f in range(groups):
        pieces = []
        for low in range(low_rows):
            for o in range(ORD_DEV):
                at = [(high * low_rows + low) * maps + f * own for high in range(2)]
                pieces += list(
                    swap_halves(
                        *[total[a : a + own, o * LANES : (o + 1) * LANES] for a in at]
                    )
                )
        turned = jnp.concatenate(pieces, 0).T
        for high in range(2):
            mixed[pl.ds(f * 2 * pairs + high, pairs, stride=2), :] = turned[
                high * pairs : (high + 1) * pairs
            ]
    out_ref[...] = mixed[...].astype(BF16)


def pixels(got, table, signs, weight, groups, scales, chunk=256):
    return pl.pallas_call(
        lambda *refs: pixel_kernel(groups, chunk, scales, *refs),
        name="pixels",
        out_shape=pltpu.VMEM(got.shape, BF16),
        in_specs=[pl.BlockSpec(memory_space=pltpu.VMEM)] * 4,
        out_specs=pl.BlockSpec(memory_space=pltpu.VMEM),
        scratch_shapes=[
            pltpu.VMEM(got.shape, F32),
            pltpu.VMEM((got.shape[0], 2 * LANES), BF16),
            pltpu.VMEM(got.shape, F32),
        ],
        compiler_params=limits(8),
    )(on_chip(got), table, signs, on_chip(weight))


def backward_kernel(
    cuts, ids_vmem, beam_ref, got_ref, leg_ref, out_ref, mixed, terms, result, blank, ids_ref, sems, zero_sems
):
    ids_copy = pltpu.make_async_copy(ids_vmem, ids_ref, sems.at[cuts[-1]])
    ids_copy.start()
    lats = leg_ref.shape[1]
    groups, degrees = beam_ref.shape
    slot = lax.axis_index("order") * ORD_DEV
    span = got_ref.shape[0] // groups
    width = LANES // groups
    lows = lats // span
    own = width // (2 * ORD_DEV)
    blank[...] = jnp.zeros_like(blank)
    blocks = [got_ref[pl.ds(f * span, span), :].astype(F32) for f in range(groups)]
    lane_group = lane_ids((span, LANES)) // width
    turned = [
        [v if k == 0 else pltpu.roll(v, k * width, 1) for k in range(groups)] for v in blocks
    ]
    for low in range(lows):
        merged = turned[0][(0 - low) % groups]
        for f in range(1, groups):
            merged = jnp.where(lane_group == f, turned[f][(f - low) % groups], merged)
        mixed[pl.ds(low, span, stride=lows), :] = merged
    rows = mixed[...].T.astype(BF16)
    rhs = jnp.concatenate(
        [
            rows[f * width + o * 2 * own : f * width + (o + 1) * 2 * own]
            for o in range(ORD_DEV)
            for f in range(groups)
        ],
        0,
    )
    lane = lane_ids((1, LANES))
    ids_copy.wait()
    steps = live_steps(ids_ref, slot, degrees)
    per_tile = 2 * TILE // LANES
    per_order = 2 * degrees // LANES
    half = groups * 2 * own

    def out_rows(order, start):
        return pl.ds(order * per_order + start // LANES * 2, per_tile)

    copies = []
    for k, (order, start) in enumerate(dead_steps(ids_ref, slot, degrees)):
        copy = pltpu.make_async_copy(
            blank, out_ref.at[:, out_rows(order, start), :], zero_sems.at[k]
        )
        copy.start()
        copies.append(copy)
    for lo, hi in zip(cuts[:-1], cuts[1:]):
        cols = pl.ds(lo * TILE, (hi - lo) * TILE)
        terms[:, cols] = lax.dot_general(
            leg_ref[cols, :], rhs, (((1,), (1,)), ((), ())), preferred_element_type=F32
        ).T
        for i in range(lo, hi):
            order, first = steps[i]
            for t in range(TILE // LANES):
                start = first + t * LANES
                if not isinstance(start, int):
                    start = pl.multiple_of(start, LANES)
                live = lane + start >= ids_ref[slot + order]
                part = terms[
                    pl.ds(pl.multiple_of(order * half, half), half), pl.ds(i * TILE + t * LANES, LANES)
                ]
                total = jnp.zeros((2 * own, LANES), F32)
                for f in range(groups):
                    shaping = jnp.where(live, beam_ref[f : f + 1, pl.ds(start, LANES)], 0.0)
                    total += part[f * 2 * own : (f + 1) * 2 * own] * shaping
                for c in range(2):
                    result[i, :, t * 2 + c, :] = total[c * own : (c + 1) * own]
            copy = pltpu.make_async_copy(
                result.at[i], out_ref.at[:, out_rows(order, first), :], sems.at[i]
            )
            copy.start()
            copies.append(copy)
    for copy in copies:
        copy.wait()


def backward(order_ids, beam, got, legendre, own):
    degrees = beam.shape[1]
    tiles = legendre.shape[0] // TILE
    cuts = (0, 17)
    per_tile = 2 * TILE // LANES
    return pl.pallas_call(
        lambda *refs: backward_kernel(cuts, *refs),
        name="backward",
        out_shape=jax.ShapeDtypeStruct((own, ORD_DEV * 2 * degrees // LANES, LANES), F32),
        in_specs=[pl.BlockSpec(memory_space=pltpu.VMEM)] * 4,
        out_specs=pl.BlockSpec(memory_space=pl.ANY),
        scratch_shapes=[
            pltpu.VMEM((legendre.shape[1], LANES), F32),
            pltpu.VMEM((LANES, legendre.shape[0]), F32),
            pltpu.VMEM((tiles, own, per_tile, LANES), F32),
            pltpu.VMEM((own, per_tile, LANES), F32),
            pltpu.SMEM(order_ids.shape, jnp.int32),
            pltpu.SemaphoreType.DMA((tiles + 1,)),
            pltpu.SemaphoreType.DMA((degrees // TILE - 1,)),
        ],
        compiler_params=limits(8),
    )(on_chip(order_ids), on_chip(beam), on_chip(got), legendre)


def on_device(harmonics, legendre, beam_window, order_ids, noise_weight):
    maps, _, _, degrees = harmonics.shape
    lats = legendre.shape[2]
    nlon = noise_weight.shape[2]
    orders_all = order_ids.shape[0]
    groups = beam_window.shape[0]
    tiles = degrees // LANES
    own = maps // groups
    pairs = orders_all // ORD_DEV
    scales = (1.0 / math.sqrt(2.0 * orders_all), 1.0 / math.sqrt(1.0 * nlon))
    harm = harmonics.reshape(maps, ORD_DEV, 2, tiles, LANES).transpose(0, 1, 3, 2, 4)
    harm = harm.reshape(maps, ORD_DEV, -1, LANES)
    columns, legendre, table, signs = forward(order_ids, beam_window, harm, legendre, nlon)
    columns = columns.reshape(pairs, lats // pairs, -1)
    got = lax.all_to_all(columns, "order", split_axis=0, concat_axis=0, tiled=True)
    terms = pixels(got.reshape(lats, -1), table, signs, noise_weight[0], groups, scales)
    terms = terms.reshape(groups * pairs, -1, LANES)
    back = lax.all_to_all(terms, ("freq", "order"), split_axis=0, concat_axis=0, tiled=True)
    out = backward(order_ids, beam_window, back.reshape(-1, LANES), legendre, own)
    out = out.reshape(own, ORD_DEV, tiles, 2, LANES).transpose(0, 1, 3, 2, 4)
    return out.reshape(own, ORD_DEV, 2, degrees)


def solution(mesh):
    return jax.shard_map(
        on_device,
        mesh=mesh,
        in_specs=(
            P(None, "order", None, None),
            P("order", None, None),
            P(),
            P(),
            P("freq", "order", None),
        ),
        out_specs=P("freq", "order", None, None),
        check_vma=False,
    )
```

```python
import math

import jax
import jax.numpy as jnp
from jax import lax
from jax.experimental import pallas as pl
from jax.experimental.pallas import tpu as pltpu
from jax.sharding import PartitionSpec as P

ORD_DEV = 2
LANES = 128
F32 = jnp.float32
BF16 = jnp.bfloat16


def limits(mib):
    return pltpu.CompilerParams(vmem_limit_bytes=mib << 20)


def on_chip(value):
    return pltpu.with_memory_space_constraint(value, pltpu.VMEM)


def off_chip(value):
    return pltpu.with_memory_space_constraint(value, pltpu.HBM)


def lane_ids(shape):
    return lax.broadcasted_iota(jnp.int32, shape, len(shape) - 1)


def swap_halves(a, b):
    low = lane_ids(a.shape) < LANES // 2
    first = jnp.where(low, a, pltpu.roll(b, LANES // 2, a.ndim - 1))
    second = jnp.where(low, pltpu.roll(a, LANES // 2, a.ndim - 1), b)
    return first, second


def cos_sin(turns, nlon):
    quarter = nlon // 4
    quadrant = (turns + quarter // 2) // quarter
    x = (turns - quadrant * quarter).astype(F32) * (2.0 * math.pi / nlon)
    y = x * x
    cos = 1.0 + y * (-0.5 + y * (1.0 / 24 + y * (-1.0 / 720 + y * (1.0 / 40320))))
    sin = x + x * y * (-1.0 / 6 + y * (1.0 / 120 + y * (-1.0 / 5040 + y * (1.0 / 362880))))
    swap = (quadrant & 1) == 1
    first = jnp.where(swap, sin, cos)
    second = jnp.where(swap, cos, sin)
    first = jnp.where(((quadrant + 1) & 2) == 2, -first, first)
    second = jnp.where((quadrant & 2) == 2, -second, second)
    return first, second


def table_angles(nlon, ids_row, sign_ref, slots, small, fine, mids):
    rows = ids_row.shape[1]
    half = rows // ORD_DEV
    slots[...] = jnp.broadcast_to(ids_row.astype(F32), (rows, rows)).T
    lane = lane_ids((half, LANES))
    steps = jnp.where(lane < LANES // 2, lane * LANES, (lane - LANES // 2) * (mids * LANES))
    for o in range(ORD_DEV):
        wide_ids = slots[pl.ds(o, half, stride=ORD_DEV), :]
        ids = wide_ids.astype(jnp.int32)
        factor = jnp.where((ids == 0) | (lane < LANES // 2), 1.0, 2.0)
        part = pl.ds(o * half, half)
        cos, sin = cos_sin((ids * steps) & (nlon - 1), nlon)
        small[0, part, :] = factor * cos
        small[1, part, :] = factor * sin
        cos, sin = cos_sin((ids * lane) & (nlon - 1), nlon)
        fine[0, part, :] = cos
        fine[1, part, :] = sin
        across = jnp.concatenate([wide_ids, wide_ids], 0).T[0:8]
        odd = across.astype(jnp.int32) & 1
        sign_ref[pl.ds(o * 8, 8), :] = (1 - 2 * odd).astype(F32)


def table_rows(out_ref, small, fine, mids, blocks):
    rows = small.shape[1]
    half = rows // ORD_DEV
    span = mids * LANES
    coarses = out_ref.shape[1] // span
    block = 16
    shape = (block, LANES)
    for r in blocks:
        part = pl.ds(r, block)
        sc, ss = small[0, part, :], small[1, part, :]
        fc, fs = fine[0, part, :], fine[1, part, :]
        at = (r // half) * rows + r % half
        lead = []
        for p in range(coarses):
            k = LANES // 2 + p
            cs = jnp.broadcast_to(ss[:, k : k + 1], shape)
            lead.append((jnp.broadcast_to(sc[:, k : k + 1], shape), cs))
        for q in range(mids):
            mc = jnp.broadcast_to(sc[:, q : q + 1], shape)
            ms = jnp.broadcast_to(ss[:, q : q + 1], shape)
            cos = mc * fc - ms * fs
            sin = ms * fc + mc * fs
            for p in range(coarses):
                cc, cs = lead[p]
                cols = pl.ds(p * span + q * LANES, LANES)
                out_ref[pl.ds(at, block), cols] = (cc * cos - cs * sin).astype(BF16)
                out_ref[pl.ds(at + half, block), cols] = (-(cs * cos) - cc * sin).astype(BF16)


TILE = 2 * LANES
PAD = 9


def lower_slot(ids_ref, slot):
    return jnp.where(ids_ref[slot] < ids_ref[slot + 1], 0, 1)


def live_steps(ids_ref, slot, degrees):
    tiles = degrees // TILE
    low = lower_slot(ids_ref, slot)
    first_low = ids_ref[slot + low] // TILE
    first_high = ids_ref[slot + 1 - low] // TILE
    count = tiles // 2 - first_low
    steps = [(low, degrees // 2 + k * TILE) for k in range(tiles // 2)]
    for k in range(tiles // 2 + 1):
        later = k >= count
        tile = jnp.where(later, first_high + k - count, first_low + k)
        steps.append((jnp.where(later, 1 - low, low), pl.multiple_of(tile * TILE, TILE)))
    return steps


def dead_steps(ids_ref, slot, degrees):
    tiles = degrees // TILE
    low = lower_slot(ids_ref, slot)
    count = ids_ref[slot + low] // TILE
    steps = []
    for k in range(tiles - 1):
        later = k >= count
        tile = jnp.where(later, k - count, k)
        steps.append((jnp.where(later, 1 - low, low), pl.multiple_of(tile * TILE, TILE)))
    return steps


def forward_kernel(
    nlon,
    plan,
    ids_hbm,
    ids_row_hbm,
    beam_ref,
    harm_ref,
    leg_ref,
    out_ref,
    leg_v,
    table_ref,
    sign_ref,
    ids_row,
    beam_v,
    own_beam,
    harm_v,
    wide,
    lhs,
    slots,
    small,
    fine,
    partial,
    ids_ref,
    sems,
    leg_sems,
):
    degrees = leg_ref.shape[1]
    upper = degrees // 2
    maps = harm_ref.shape[0]
    rows = harm_ref.shape[2]
    mids = 8
    slot = lax.axis_index("order") * ORD_DEV
    group = lax.axis_index("freq")
    copies = [
        pltpu.make_async_copy(ids_hbm, ids_ref, sems.at[0]),
        pltpu.make_async_copy(ids_row_hbm, ids_row, sems.at[1]),
        pltpu.make_async_copy(beam_ref, beam_v, sems.at[2]),
        pltpu.make_async_copy(harm_ref, harm_v, sems.at[3]),
    ]

    def upper_copy(order):
        return pltpu.make_async_copy(
            leg_ref.at[order, pl.ds(upper, upper), :], leg_v.at[pl.ds(0, upper), :], sems.at[4]
        )

    for copy in copies:
        copy.start()
    upper_copy(0).start()
    copies[0].wait()
    steps = live_steps(ids_ref, slot, degrees)
    fixed = upper // TILE
    leg_copies = []
    for k, (order, start) in enumerate(steps[fixed:]):
        copy = pltpu.make_async_copy(
            leg_ref.at[order, pl.ds(start, TILE), :],
            leg_v.at[pl.ds(upper + k * TILE, TILE), :],
            leg_sems.at[k],
        )
        copy.start()
        leg_copies.append(copy)
    copies[1].wait()
    table_angles(nlon, ids_row[...], sign_ref, slots, small, fine, mids)
    copies[2].wait()
    own_beam[...] = beam_v[pl.ds(group, 1), :]
    copies[3].wait()
    for b in range(maps):
        for o in range(ORD_DEV):
            wide[pl.ds(b * (ORD_DEV * rows + PAD) + o * rows, rows), :] = harm_v[b, o].astype(F32)
    lane = lane_ids((1, LANES))
    blank = jnp.zeros((2 * maps, TILE), BF16)

    def prepare(some):
        for i in some:
            order, first = steps[i]
            at = pl.multiple_of(order * (2 * maps), 2 * maps)
            lhs[pl.ds(2 * maps - at, 2 * maps), pl.ds(i * TILE, TILE)] = blank
            for t in range(TILE // LANES):
                start = first + t * LANES
                if not isinstance(start, int):
                    start = pl.multiple_of(start, LANES)
                live = lane + start >= ids_ref[slot + order]
                shaping = jnp.where(live, own_beam[:, pl.ds(start, LANES)], 0.0)
                for c in range(2):
                    row = order * rows + start // LANES * 2 + c
                    values = wide[pl.ds(row, maps, stride=ORD_DEV * rows + PAD), :]
                    lhs[pl.ds(at + c * maps, maps), pl.ds(i * TILE + t * LANES, LANES)] = (
                        values * shaping
                    ).astype(BF16)

    table_blocks = list(range(0, small.shape[1], 16))
    prepare(range(fixed))
    table_rows(table_ref, small, fine, mids, table_blocks[: plan[0]])
    upper_copy(0).wait()

    @pl.when(lower_slot(ids_ref, slot) == 1)
    def _():
        copy = upper_copy(1)
        copy.start()
        copy.wait()

    partial[...] = jnp.dot(
        lhs[:, pl.ds(0, upper)], leg_v[pl.ds(0, upper), :], preferred_element_type=F32
    )
    prepare(range(fixed, len(steps)))
    table_rows(table_ref, small, fine, mids, table_blocks[plan[0] : plan[1]])

    def arrived(k, carry):
        pltpu.make_async_copy(
            leg_ref.at[0, pl.ds(0, TILE), :],
            leg_v.at[pl.ds(pl.multiple_of(upper + k * TILE, TILE), TILE), :],
            leg_sems.at[k],
        ).wait()
        return carry

    lax.fori_loop(0, len(leg_copies), arrived, 0)
    rest = pl.ds(upper, leg_v.shape[0] - upper)
    total = partial[...] + jnp.dot(lhs[:, rest], leg_v[rest, :], preferred_element_type=F32)
    table_rows(table_ref, small, fine, mids, table_blocks[plan[1] :])
    out_ref[...] = total.T.astype(BF16)


def forward(order_ids, beam, harm, legendre, nlon):
    degrees, lats = legendre.shape[1:]
    maps = harm.shape[0]
    orders = order_ids.shape[0]
    ids_row = order_ids.reshape(1, -1)
    live = degrees + TILE
    return pl.pallas_call(
        lambda *refs: forward_kernel(nlon, (8, 8), *refs),
        name="forward",
        out_shape=(
            pltpu.VMEM((lats, ORD_DEV * 2 * maps), BF16),
            pltpu.VMEM((live, lats), BF16),
            pltpu.VMEM((2 * orders, nlon // 2), BF16),
            pltpu.VMEM((8 * ORD_DEV, LANES), F32),
        ),
        in_specs=[pl.BlockSpec(memory_space=pl.ANY)] * 5,
        out_specs=(pl.BlockSpec(memory_space=pltpu.VMEM),) * 4,
        scratch_shapes=[
            pltpu.VMEM(ids_row.shape, jnp.int32),
            pltpu.VMEM(beam.shape, F32),
            pltpu.VMEM((1, degrees), F32),
            pltpu.VMEM(harm.shape, BF16),
            pltpu.VMEM((maps * (ORD_DEV * harm.shape[2] + PAD), LANES), F32),
            pltpu.VMEM((ORD_DEV * 2 * maps, live), BF16),
            pltpu.VMEM((orders, orders), F32),
            pltpu.VMEM((2, orders, LANES), F32),
            pltpu.VMEM((2, orders, LANES), F32),
            pltpu.VMEM((ORD_DEV * 2 * maps, lats), F32),
            pltpu.SMEM(order_ids.shape, jnp.int32),
            pltpu.SemaphoreType.DMA((5,)),
            pltpu.SemaphoreType.DMA((degrees // TILE // 2 + 1,)),
        ],
        compiler_params=limits(16),
    )(*[off_chip(v) for v in (order_ids, ids_row, beam, harm, legendre)])


def pixel_kernel(
    groups, chunk, scales, got_ref, table_ref, sign_ref, weight_ref, out_ref, wide, lhs, mixed
):
    fwd_scale, back_scale = scales
    rows = weight_ref.shape[0]
    pairs = got_ref.shape[0] // rows
    maps = got_ref.shape[1] // (2 * ORD_DEV)
    size = rows * maps
    half = table_ref.shape[1]
    wide[...] = got_ref[...].astype(F32)
    signs = [sign_ref[pl.ds(o * 8, 1), :] for o in range(ORD_DEV)]
    for r in range(0, rows, 2):
        stacked = jnp.concatenate(
            [wide[pl.ds(r + i, pairs, stride=rows), :] for i in range(2)], 0
        )
        turned = stacked.T
        for o in range(ORD_DEV):
            cos = turned[(2 * o) * maps : (2 * o + 1) * maps]
            sin = turned[(2 * o + 1) * maps : (2 * o + 2) * maps]
            for i, part in enumerate(swap_halves(cos, sin)):
                cols = pl.ds(o * LANES, LANES)
                lhs[pl.ds((r + i) * maps, maps), cols] = part.astype(BF16)
                lhs[pl.ds(size + (r + i) * maps, maps), cols] = (part * signs[o]).astype(BF16)
    total = jnp.zeros((2 * size, 2 * LANES), F32)
    for j in range(half // chunk):
        cols = pl.ds(j * chunk, chunk)
        part = table_ref[:, cols]
        field = jnp.dot(lhs[...], part, preferred_element_type=F32)
        pieces = []
        for h in range(2):
            weight = weight_ref[:, pl.ds(h * half + j * chunk, chunk)] * fwd_scale
            for r in range(rows):
                at = h * size + r * maps
                pieces.append((field[at : at + maps] * weight[r : r + 1]).astype(BF16))
        total += lax.dot_general(
            jnp.concatenate(pieces, 0), part, (((1,), (1,)), ((), ())), preferred_element_type=F32
        )
    sign = jnp.concatenate(signs, 1)
    total = (total[:size] + total[size:] * sign) * back_scale
    own = maps // groups
    low_rows = rows // 2
    for f in range(groups):
        pieces = []
        for low in range(low_rows):
            for o in range(ORD_DEV):
                at = [(high * low_rows + low) * maps + f * own for high in range(2)]
                pieces += list(
                    swap_halves(
                        *[total[a : a + own, o * LANES : (o + 1) * LANES] for a in at]
                    )
                )
        turned = jnp.concatenate(pieces, 0).T
        for high in range(2):
            mixed[pl.ds(f * 2 * pairs + high, pairs, stride=2), :] = turned[
                high * pairs : (high + 1) * pairs
            ]
    out_ref[...] = mixed[...].astype(BF16)


def pixels(got, table, signs, weight, groups, scales, chunk=256):
    return pl.pallas_call(
        lambda *refs: pixel_kernel(groups, chunk, scales, *refs),
        name="pixels",
        out_shape=pltpu.VMEM(got.shape, BF16),
        in_specs=[pl.BlockSpec(memory_space=pltpu.VMEM)] * 4,
        out_specs=pl.BlockSpec(memory_space=pltpu.VMEM),
        scratch_shapes=[
            pltpu.VMEM(got.shape, F32),
            pltpu.VMEM((got.shape[0], 2 * LANES), BF16),
            pltpu.VMEM(got.shape, F32),
        ],
        compiler_params=limits(8),
    )(on_chip(got), table, signs, on_chip(weight))


def backward_kernel(
    cuts, ids_vmem, beam_ref, got_ref, leg_ref, out_ref, mixed, terms, result, blank, ids_ref, sems, zero_sems
):
    ids_copy = pltpu.make_async_copy(ids_vmem, ids_ref, sems.at[cuts[-1]])
    ids_copy.start()
    lats = leg_ref.shape[1]
    groups, degrees = beam_ref.shape
    slot = lax.axis_index("order") * ORD_DEV
    span = got_ref.shape[0] // groups
    width = LANES // groups
    lows = lats // span
    own = width // (2 * ORD_DEV)
    blank[...] = jnp.zeros_like(blank)
    blocks = [got_ref[pl.ds(f * span, span), :].astype(F32) for f in range(groups)]
    lane_group = lane_ids((span, LANES)) // width
    turned = [
        [v if k == 0 else pltpu.roll(v, k * width, 1) for k in range(groups)] for v in blocks
    ]
    for low in range(lows):
        merged = turned[0][(0 - low) % groups]
        for f in range(1, groups):
            merged = jnp.where(lane_group == f, turned[f][(f - low) % groups], merged)
        mixed[pl.ds(low, span, stride=lows), :] = merged
    rhs = mixed[...].astype(BF16)
    lane = lane_ids((1, LANES))
    ids_copy.wait()
    steps = live_steps(ids_ref, slot, degrees)
    per_tile = 2 * TILE // LANES
    per_order = 2 * degrees // LANES

    def out_rows(order, start):
        return pl.ds(order * per_order + start // LANES * 2, per_tile)

    copies = []
    for k, (order, start) in enumerate(dead_steps(ids_ref, slot, degrees)):
        copy = pltpu.make_async_copy(
            blank, out_ref.at[:, out_rows(order, start), :], zero_sems.at[k]
        )
        copy.start()
        copies.append(copy)
    for lo, hi in zip(cuts[:-1], cuts[1:]):
        cols = pl.ds(lo * TILE, (hi - lo) * TILE)
        terms[:, cols] = jnp.dot(leg_ref[cols, :], rhs, preferred_element_type=F32).T
        for i in range(lo, hi):
            order, first = steps[i]
            for t in range(TILE // LANES):
                start = first + t * LANES
                if not isinstance(start, int):
                    start = pl.multiple_of(start, LANES)
                live = lane + start >= ids_ref[slot + order]
                total = jnp.zeros((2 * own, LANES), F32)
                for f in range(groups):
                    at = pl.multiple_of(f * width + order * (2 * own), 2 * own)
                    part = terms[pl.ds(at, 2 * own), pl.ds(i * TILE + t * LANES, LANES)]
                    shaping = jnp.where(live, beam_ref[f : f + 1, pl.ds(start, LANES)], 0.0)
                    total += part * shaping
                for c in range(2):
                    result[i, :, t * 2 + c, :] = total[c * own : (c + 1) * own]
            copy = pltpu.make_async_copy(
                result.at[i], out_ref.at[:, out_rows(order, first), :], sems.at[i]
            )
            copy.start()
            copies.append(copy)
    for copy in copies:
        copy.wait()


def backward(order_ids, beam, got, legendre, own):
    degrees = beam.shape[1]
    tiles = legendre.shape[0] // TILE
    cuts = (0, 17)
    per_tile = 2 * TILE // LANES
    return pl.pallas_call(
        lambda *refs: backward_kernel(cuts, *refs),
        name="backward",
        out_shape=jax.ShapeDtypeStruct((own, ORD_DEV * 2 * degrees // LANES, LANES), F32),
        in_specs=[pl.BlockSpec(memory_space=pltpu.VMEM)] * 4,
        out_specs=pl.BlockSpec(memory_space=pl.ANY),
        scratch_shapes=[
            pltpu.VMEM((legendre.shape[1], LANES), F32),
            pltpu.VMEM((LANES, legendre.shape[0]), F32),
            pltpu.VMEM((tiles, own, per_tile, LANES), F32),
            pltpu.VMEM((own, per_tile, LANES), F32),
            pltpu.SMEM(order_ids.shape, jnp.int32),
            pltpu.SemaphoreType.DMA((tiles + 1,)),
            pltpu.SemaphoreType.DMA((degrees // TILE - 1,)),
        ],
        compiler_params=limits(8),
    )(on_chip(order_ids), on_chip(beam), on_chip(got), legendre)


def on_device(harmonics, legendre, beam_window, order_ids, noise_weight):
    maps, _, _, degrees = harmonics.shape
    lats = legendre.shape[2]
    nlon = noise_weight.shape[2]
    orders_all = order_ids.shape[0]
    groups = beam_window.shape[0]
    tiles = degrees // LANES
    own = maps // groups
    pairs = orders_all // ORD_DEV
    scales = (1.0 / math.sqrt(2.0 * orders_all), 1.0 / math.sqrt(1.0 * nlon))
    harm = harmonics.reshape(maps, ORD_DEV, 2, tiles, LANES).transpose(0, 1, 3, 2, 4)
    harm = harm.reshape(maps, ORD_DEV, -1, LANES)
    columns, legendre, table, signs = forward(order_ids, beam_window, harm, legendre, nlon)
    columns = columns.reshape(pairs, lats // pairs, -1)
    got = lax.all_to_all(columns, "order", split_axis=0, concat_axis=0, tiled=True)
    terms = pixels(got.reshape(lats, -1), table, signs, noise_weight[0], groups, scales)
    terms = terms.reshape(groups * pairs, -1, LANES)
    back = lax.all_to_all(terms, ("freq", "order"), split_axis=0, concat_axis=0, tiled=True)
    out = backward(order_ids, beam_window, back.reshape(-1, LANES), legendre, own)
    out = out.reshape(own, ORD_DEV, tiles, 2, LANES).transpose(0, 1, 3, 2, 4)
    return out.reshape(own, ORD_DEV, 2, degrees)


def solution(mesh):
    return jax.shard_map(
        on_device,
        mesh=mesh,
        in_specs=(
            P(None, "order", None, None),
            P("order", None, None),
            P(),
            P(),
            P("freq", "order", None),
        ),
        out_specs=P("freq", "order", None, None),
        check_vma=False,
    )
```

```python
import math

import jax
import jax.numpy as jnp
from jax import lax
from jax.experimental import pallas as pl
from jax.experimental.pallas import tpu as pltpu
from jax.sharding import PartitionSpec as P

ORD_DEV = 2
LANES = 128
F32 = jnp.float32
BF16 = jnp.bfloat16


def limits(mib):
    return pltpu.CompilerParams(vmem_limit_bytes=mib << 20)


def on_chip(value):
    return pltpu.with_memory_space_constraint(value, pltpu.VMEM)


def off_chip(value):
    return pltpu.with_memory_space_constraint(value, pltpu.HBM)


def lane_ids(shape):
    return lax.broadcasted_iota(jnp.int32, shape, len(shape) - 1)


def swap_halves(a, b):
    low = lane_ids(a.shape) < LANES // 2
    first = jnp.where(low, a, pltpu.roll(b, LANES // 2, a.ndim - 1))
    second = jnp.where(low, pltpu.roll(a, LANES // 2, a.ndim - 1), b)
    return first, second


def cos_sin(turns, nlon):
    quarter = nlon // 4
    quadrant = (turns + quarter // 2) // quarter
    x = (turns - quadrant * quarter).astype(F32) * (2.0 * math.pi / nlon)
    y = x * x
    cos = 1.0 + y * (-0.5 + y * (1.0 / 24 + y * (-1.0 / 720 + y * (1.0 / 40320))))
    sin = x + x * y * (-1.0 / 6 + y * (1.0 / 120 + y * (-1.0 / 5040 + y * (1.0 / 362880))))
    swap = (quadrant & 1) == 1
    first = jnp.where(swap, sin, cos)
    second = jnp.where(swap, cos, sin)
    first = jnp.where(((quadrant + 1) & 2) == 2, -first, first)
    second = jnp.where((quadrant & 2) == 2, -second, second)
    return first, second


def table_angles(nlon, ids_row, sign_ref, slots, small, fine, mids):
    rows = ids_row.shape[1]
    half = rows // ORD_DEV
    slots[...] = jnp.broadcast_to(ids_row.astype(F32), (rows, rows)).T
    lane = lane_ids((half, LANES))
    steps = jnp.where(lane < LANES // 2, lane * LANES, (lane - LANES // 2) * (mids * LANES))
    for o in range(ORD_DEV):
        wide_ids = slots[pl.ds(o, half, stride=ORD_DEV), :]
        ids = wide_ids.astype(jnp.int32)
        factor = jnp.where((ids == 0) | (lane < LANES // 2), 1.0, 2.0)
        part = pl.ds(o * half, half)
        cos, sin = cos_sin((ids * steps) & (nlon - 1), nlon)
        small[0, part, :] = factor * cos
        small[1, part, :] = factor * sin
        cos, sin = cos_sin((ids * lane) & (nlon - 1), nlon)
        fine[0, part, :] = cos
        fine[1, part, :] = sin
        across = jnp.concatenate([wide_ids, wide_ids], 0).T[0:8]
        odd = across.astype(jnp.int32) & 1
        sign_ref[pl.ds(o * 8, 8), :] = (1 - 2 * odd).astype(F32)


def table_rows(out_ref, small, fine, mids, blocks):
    rows = small.shape[1]
    half = rows // ORD_DEV
    span = mids * LANES
    coarses = out_ref.shape[1] // span
    block = 16
    shape = (block, LANES)
    for r in blocks:
        part = pl.ds(r, block)
        sc, ss = small[0, part, :], small[1, part, :]
        fc, fs = fine[0, part, :], fine[1, part, :]
        at = (r // half) * rows + r % half
        lead = []
        for p in range(coarses):
            k = LANES // 2 + p
            cs = jnp.broadcast_to(ss[:, k : k + 1], shape)
            lead.append((jnp.broadcast_to(sc[:, k : k + 1], shape), cs))
        for q in range(mids):
            mc = jnp.broadcast_to(sc[:, q : q + 1], shape)
            ms = jnp.broadcast_to(ss[:, q : q + 1], shape)
            cos = mc * fc - ms * fs
            sin = ms * fc + mc * fs
            for p in range(coarses):
                cc, cs = lead[p]
                cols = pl.ds(p * span + q * LANES, LANES)
                out_ref[pl.ds(at, block), cols] = (cc * cos - cs * sin).astype(BF16)
                out_ref[pl.ds(at + half, block), cols] = (-(cs * cos) - cc * sin).astype(BF16)


TILE = 2 * LANES
PAD = 9


def lower_slot(ids_ref, slot):
    return jnp.where(ids_ref[slot] < ids_ref[slot + 1], 0, 1)


def live_steps(ids_ref, slot, degrees):
    tiles = degrees // TILE
    low = lower_slot(ids_ref, slot)
    first_low = ids_ref[slot + low] // TILE
    first_high = ids_ref[slot + 1 - low] // TILE
    count = tiles // 2 - first_low
    steps = [(low, degrees // 2 + k * TILE) for k in range(tiles // 2)]
    for k in range(tiles // 2 + 1):
        later = k >= count
        tile = jnp.where(later, first_high + k - count, first_low + k)
        steps.append((jnp.where(later, 1 - low, low), pl.multiple_of(tile * TILE, TILE)))
    return steps


def dead_steps(ids_ref, slot, degrees):
    tiles = degrees // TILE
    low = lower_slot(ids_ref, slot)
    count = ids_ref[slot + low] // TILE
    steps = []
    for k in range(tiles - 1):
        later = k >= count
        tile = jnp.where(later, k - count, k)
        steps.append((jnp.where(later, 1 - low, low), pl.multiple_of(tile * TILE, TILE)))
    return steps


def forward_kernel(
    nlon,
    plan,
    ids_hbm,
    ids_row_hbm,
    beam_ref,
    harm_ref,
    leg_ref,
    out_ref,
    leg_v,
    table_ref,
    sign_ref,
    ids_row,
    beam_v,
    own_beam,
    harm_v,
    wide,
    lhs,
    slots,
    small,
    fine,
    partial,
    ids_ref,
    sems,
    leg_sems,
):
    degrees = leg_ref.shape[1]
    upper = degrees // 2
    groups = beam_ref.shape[0]
    maps, _, rows, _ = harm_ref.shape
    own = maps // groups
    mids = 8
    slot = lax.axis_index("order") * ORD_DEV
    group = lax.axis_index("freq")
    copies = [
        pltpu.make_async_copy(ids_hbm, ids_ref, sems.at[0]),
        pltpu.make_async_copy(ids_row_hbm, ids_row, sems.at[1]),
        pltpu.make_async_copy(beam_ref, beam_v, sems.at[2]),
        pltpu.make_async_copy(harm_ref.at[pl.ds(group * own, own)], harm_v, sems.at[3]),
    ]

    def upper_copy(order):
        return pltpu.make_async_copy(
            leg_ref.at[order, pl.ds(upper, upper), :], leg_v.at[pl.ds(0, upper), :], sems.at[4]
        )

    for copy in copies:
        copy.start()
    upper_copy(0).start()
    copies[0].wait()
    steps = live_steps(ids_ref, slot, degrees)
    fixed = upper // TILE
    leg_copies = []
    for k, (order, start) in enumerate(steps[fixed:]):
        copy = pltpu.make_async_copy(
            leg_ref.at[order, pl.ds(start, TILE), :],
            leg_v.at[pl.ds(upper + k * TILE, TILE), :],
            leg_sems.at[k],
        )
        copy.start()
        leg_copies.append(copy)
    copies[1].wait()
    table_angles(nlon, ids_row[...], sign_ref, slots, small, fine, mids)
    copies[2].wait()
    for k in range(groups):
        own_beam[k : k + 1, :] = beam_v[pl.ds(group ^ k, 1), :]
    copies[3].wait()
    for b in range(own):
        for o in range(ORD_DEV):
            wide[pl.ds(b * (ORD_DEV * rows + PAD) + o * rows, rows), :] = harm_v[b, o].astype(F32)
    lane = lane_ids((1, LANES))
    blank = jnp.zeros((2 * maps, TILE), BF16)

    def prepare(some):
        for i in some:
            order, first = steps[i]
            at = pl.multiple_of(order * (2 * maps), 2 * maps)
            lhs[pl.ds(2 * maps - at, 2 * maps), pl.ds(i * TILE, TILE)] = blank
            for t in range(TILE // LANES):
                start = first + t * LANES
                if not isinstance(start, int):
                    start = pl.multiple_of(start, LANES)
                live = lane + start >= ids_ref[slot + order]
                shaping = jnp.where(live, own_beam[:, pl.ds(start, LANES)], 0.0)
                for c in range(2):
                    row = order * rows + start // LANES * 2 + c
                    values = wide[pl.ds(row, own, stride=ORD_DEV * rows + PAD), :]
                    shaped = jnp.concatenate(
                        [values * shaping[k : k + 1] for k in range(groups)], 0
                    )
                    lhs[pl.ds(at + c * maps, maps), pl.ds(i * TILE + t * LANES, LANES)] = (
                        shaped.astype(BF16)
                    )

    table_blocks = list(range(0, small.shape[1], 16))
    prepare(range(fixed))
    table_rows(table_ref, small, fine, mids, table_blocks[: plan[0]])
    upper_copy(0).wait()

    @pl.when(lower_slot(ids_ref, slot) == 1)
    def _():
        copy = upper_copy(1)
        copy.start()
        copy.wait()

    partial[...] = jnp.dot(
        lhs[:, pl.ds(0, upper)], leg_v[pl.ds(0, upper), :], preferred_element_type=F32
    )
    prepare(range(fixed, len(steps)))
    table_rows(table_ref, small, fine, mids, table_blocks[plan[0] : plan[1]])

    def arrived(k, carry):
        pltpu.make_async_copy(
            leg_ref.at[0, pl.ds(0, TILE), :],
            leg_v.at[pl.ds(pl.multiple_of(upper + k * TILE, TILE), TILE), :],
            leg_sems.at[k],
        ).wait()
        return carry

    lax.fori_loop(0, len(leg_copies), arrived, 0)
    rest = pl.ds(upper, leg_v.shape[0] - upper)
    total = partial[...] + jnp.dot(lhs[:, rest], leg_v[rest, :], preferred_element_type=F32)
    table_rows(table_ref, small, fine, mids, table_blocks[plan[1] :])
    out_ref[...] = total.T.astype(BF16)


def forward(order_ids, beam, harm, legendre, nlon):
    degrees, lats = legendre.shape[1:]
    maps = harm.shape[0]
    own = maps // beam.shape[0]
    orders = order_ids.shape[0]
    ids_row = order_ids.reshape(1, -1)
    live = degrees + TILE
    return pl.pallas_call(
        lambda *refs: forward_kernel(nlon, (8, 8), *refs),
        name="forward",
        out_shape=(
            pltpu.VMEM((lats, ORD_DEV * 2 * maps), BF16),
            pltpu.VMEM((live, lats), BF16),
            pltpu.VMEM((2 * orders, nlon // 2), BF16),
            pltpu.VMEM((8 * ORD_DEV, LANES), F32),
        ),
        in_specs=[pl.BlockSpec(memory_space=pl.ANY)] * 5,
        out_specs=(pl.BlockSpec(memory_space=pltpu.VMEM),) * 4,
        scratch_shapes=[
            pltpu.VMEM(ids_row.shape, jnp.int32),
            pltpu.VMEM(beam.shape, F32),
            pltpu.VMEM(beam.shape, F32),
            pltpu.VMEM((own,) + harm.shape[1:], BF16),
            pltpu.VMEM((own * (ORD_DEV * harm.shape[2] + PAD), LANES), F32),
            pltpu.VMEM((ORD_DEV * 2 * maps, live), BF16),
            pltpu.VMEM((orders, orders), F32),
            pltpu.VMEM((2, orders, LANES), F32),
            pltpu.VMEM((2, orders, LANES), F32),
            pltpu.VMEM((ORD_DEV * 2 * maps, lats), F32),
            pltpu.SMEM(order_ids.shape, jnp.int32),
            pltpu.SemaphoreType.DMA((5,)),
            pltpu.SemaphoreType.DMA((degrees // TILE // 2 + 1,)),
        ],
        compiler_params=limits(16),
    )(*[off_chip(v) for v in (order_ids, ids_row, beam, harm, legendre)])


def pixel_kernel(
    groups, chunk, scales, got_ref, table_ref, sign_ref, *refs
):
    weight_refs, (out_ref, wide, lhs, mixed) = refs[:groups], refs[groups:]
    fwd_scale, back_scale = scales
    rows = weight_refs[0].shape[0]
    pairs = got_ref.shape[0] // rows
    maps = got_ref.shape[1] // (2 * ORD_DEV)
    own = maps // groups
    size = rows * maps
    half = table_ref.shape[1]
    wide[...] = got_ref[...].astype(F32)
    signs = [sign_ref[pl.ds(o * 8, 1), :] for o in range(ORD_DEV)]
    for r in range(0, rows, 2):
        stacked = jnp.concatenate(
            [wide[pl.ds(r + i, pairs, stride=rows), :] for i in range(2)], 0
        )
        turned = stacked.T
        for o in range(ORD_DEV):
            cos = turned[(2 * o) * maps : (2 * o + 1) * maps]
            sin = turned[(2 * o + 1) * maps : (2 * o + 2) * maps]
            for i, part in enumerate(swap_halves(cos, sin)):
                cols = pl.ds(o * LANES, LANES)
                lhs[pl.ds((r + i) * maps, maps), cols] = part.astype(BF16)
                lhs[pl.ds(size + (r + i) * maps, maps), cols] = (part * signs[o]).astype(BF16)
    total = jnp.zeros((2 * size, 2 * LANES), F32)
    for j in range(half // chunk):
        cols = pl.ds(j * chunk, chunk)
        part = table_ref[:, cols]
        field = jnp.dot(lhs[...], part, preferred_element_type=F32)
        pieces = []
        for h in range(2):
            span = pl.ds(h * half + j * chunk, chunk)
            weights = [ref[:, span] * fwd_scale for ref in weight_refs]
            for r in range(rows):
                at = h * size + r * maps
                part_rows = [
                    field[at + k * own : at + (k + 1) * own] * weights[k][r : r + 1]
                    for k in range(groups)
                ]
                pieces.append(jnp.concatenate(part_rows, 0).astype(BF16))
        total += lax.dot_general(
            jnp.concatenate(pieces, 0), part, (((1,), (1,)), ((), ())), preferred_element_type=F32
        )
    sign = jnp.concatenate(signs, 1)
    total = (total[:size] + total[size:] * sign) * back_scale
    low_rows = rows // 2
    for f in range(groups):
        pieces = []
        for low in range(low_rows):
            for o in range(ORD_DEV):
                at = [(high * low_rows + low) * maps + f * own for high in range(2)]
                pieces += list(
                    swap_halves(
                        *[total[a : a + own, o * LANES : (o + 1) * LANES] for a in at]
                    )
                )
        turned = jnp.concatenate(pieces, 0).T
        for high in range(2):
            mixed[pl.ds(f * 2 + high, pairs, stride=2 * groups), :] = turned[
                high * pairs : (high + 1) * pairs
            ]
    out_ref[...] = mixed[...].astype(BF16)


def pixels(got, table, signs, weights, scales, chunk=256):
    groups = len(weights)
    return pl.pallas_call(
        lambda *refs: pixel_kernel(groups, chunk, scales, *refs),
        name="pixels",
        out_shape=pltpu.VMEM(got.shape, BF16),
        in_specs=[pl.BlockSpec(memory_space=pltpu.VMEM)] * (3 + groups),
        out_specs=pl.BlockSpec(memory_space=pltpu.VMEM),
        scratch_shapes=[
            pltpu.VMEM(got.shape, F32),
            pltpu.VMEM((got.shape[0], 2 * LANES), BF16),
            pltpu.VMEM(got.shape, F32),
        ],
        compiler_params=limits(8),
    )(on_chip(got), table, signs, *[on_chip(w) for w in weights])


def backward_kernel(
    cuts, ids_vmem, beam_ref, got_ref, leg_ref, out_ref, beam_v, wide, mixed, terms, result, blank, ids_ref, sems, zero_sems
):
    ids_copy = pltpu.make_async_copy(ids_vmem, ids_ref, sems.at[cuts[-1]])
    ids_copy.start()
    lats = leg_ref.shape[1]
    groups, degrees = beam_ref.shape
    slot = lax.axis_index("order") * ORD_DEV
    span = got_ref.shape[0] // groups
    width = LANES // groups
    lows = lats // span
    own = width // (2 * ORD_DEV)
    blank[...] = jnp.zeros_like(blank)
    group = lax.axis_index("freq")
    for k in range(groups):
        beam_v[k : k + 1, :] = beam_ref[pl.ds(group ^ k, 1), :]
    wide[...] = got_ref[...].astype(F32)
    pitch = 2 * groups
    devices = got_ref.shape[0] // pitch
    lane_group = lane_ids((devices, LANES)) // width
    for high in range(2):
        turned = []
        for k in range(groups):
            v = wide[pl.ds(k * 2 + high, devices, stride=pitch), :]
            turned.append([v if n == 0 else pltpu.roll(v, n * width, 1) for n in range(groups)])
        for low in range(lows):
            merged = turned[0][(0 - low) % groups]
            for k in range(1, groups):
                merged = jnp.where(lane_group == k, turned[k][(k - low) % groups], merged)
            mixed[pl.ds(high * lows + low, devices, stride=2 * lows), :] = merged
    rhs = mixed[...].astype(BF16)
    lane = lane_ids((1, LANES))
    ids_copy.wait()
    steps = live_steps(ids_ref, slot, degrees)
    per_tile = 2 * TILE // LANES
    per_order = 2 * degrees // LANES

    def out_rows(order, start):
        return pl.ds(order * per_order + start // LANES * 2, per_tile)

    copies = []
    for k, (order, start) in enumerate(dead_steps(ids_ref, slot, degrees)):
        copy = pltpu.make_async_copy(
            blank, out_ref.at[:, out_rows(order, start), :], zero_sems.at[k]
        )
        copy.start()
        copies.append(copy)
    for lo, hi in zip(cuts[:-1], cuts[1:]):
        cols = pl.ds(lo * TILE, (hi - lo) * TILE)
        terms[:, cols] = jnp.dot(leg_ref[cols, :], rhs, preferred_element_type=F32).T
        for i in range(lo, hi):
            order, first = steps[i]
            for t in range(TILE // LANES):
                start = first + t * LANES
                if not isinstance(start, int):
                    start = pl.multiple_of(start, LANES)
                live = lane + start >= ids_ref[slot + order]
                total = jnp.zeros((2 * own, LANES), F32)
                for f in range(groups):
                    at = pl.multiple_of(f * width + order * (2 * own), 2 * own)
                    part = terms[pl.ds(at, 2 * own), pl.ds(i * TILE + t * LANES, LANES)]
                    shaping = jnp.where(live, beam_v[f : f + 1, pl.ds(start, LANES)], 0.0)
                    total += part * shaping
                for c in range(2):
                    result[i, :, t * 2 + c, :] = total[c * own : (c + 1) * own]
            copy = pltpu.make_async_copy(
                result.at[i], out_ref.at[:, out_rows(order, first), :], sems.at[i]
            )
            copy.start()
            copies.append(copy)
    for copy in copies:
        copy.wait()


def backward(order_ids, beam, got, legendre, own):
    degrees = beam.shape[1]
    tiles = legendre.shape[0] // TILE
    cuts = (0, 17)
    per_tile = 2 * TILE // LANES
    return pl.pallas_call(
        lambda *refs: backward_kernel(cuts, *refs),
        name="backward",
        out_shape=jax.ShapeDtypeStruct((own, ORD_DEV * 2 * degrees // LANES, LANES), F32),
        in_specs=[pl.BlockSpec(memory_space=pltpu.VMEM)] * 4,
        out_specs=pl.BlockSpec(memory_space=pl.ANY),
        scratch_shapes=[
            pltpu.VMEM(beam.shape, F32),
            pltpu.VMEM(got.shape, F32),
            pltpu.VMEM((legendre.shape[1], LANES), F32),
            pltpu.VMEM((LANES, legendre.shape[0]), F32),
            pltpu.VMEM((tiles, own, per_tile, LANES), F32),
            pltpu.VMEM((own, per_tile, LANES), F32),
            pltpu.SMEM(order_ids.shape, jnp.int32),
            pltpu.SemaphoreType.DMA((tiles + 1,)),
            pltpu.SemaphoreType.DMA((degrees // TILE - 1,)),
        ],
        compiler_params=limits(8),
    )(on_chip(order_ids), on_chip(beam), on_chip(got), legendre)


def on_device(harmonics, legendre, beam_window, order_ids, noise_weight):
    maps, _, _, degrees = harmonics.shape
    lats = legendre.shape[2]
    nlon = noise_weight.shape[2]
    orders_all = order_ids.shape[0]
    groups = beam_window.shape[0]
    tiles = degrees // LANES
    own = maps // groups
    pairs = orders_all // ORD_DEV
    scales = (1.0 / math.sqrt(2.0 * orders_all), 1.0 / math.sqrt(1.0 * nlon))
    harm = harmonics.reshape(maps, ORD_DEV, 2, tiles, LANES).transpose(0, 1, 3, 2, 4)
    harm = harm.reshape(maps, ORD_DEV, -1, LANES)
    weights = [noise_weight[0]]
    for k in range(1, groups):
        pairing = [(i, i ^ k) for i in range(groups)]
        weights.append(lax.ppermute(noise_weight[0], "freq", pairing))
    columns, legendre, table, signs = forward(order_ids, beam_window, harm, legendre, nlon)
    columns = columns.reshape(pairs, lats // pairs, -1)
    got = lax.all_to_all(columns, "order", split_axis=0, concat_axis=0, tiled=True)
    terms = pixels(got.reshape(lats, -1), table, signs, weights, scales)
    terms = terms.reshape(pairs, -1, LANES)
    back = lax.all_to_all(terms, "order", split_axis=0, concat_axis=0, tiled=True)
    out = backward(order_ids, beam_window, back.reshape(-1, LANES), legendre, own)
    out = out.reshape(own, ORD_DEV, tiles, 2, LANES).transpose(0, 1, 3, 2, 4)
    return out.reshape(own, ORD_DEV, 2, degrees)


def solution(mesh):
    return jax.shard_map(
        on_device,
        mesh=mesh,
        in_specs=(
            P(None, "order", None, None),
            P("order", None, None),
            P(),
            P(),
            P("freq", "order", None),
        ),
        out_specs=P("freq", "order", None, None),
        check_vma=False,
    )
```

```python
import math

import jax
import jax.numpy as jnp
from jax import lax
from jax.experimental import pallas as pl
from jax.experimental.pallas import tpu as pltpu
from jax.sharding import PartitionSpec as P

ORD_DEV = 2
LANES = 128
F32 = jnp.float32
BF16 = jnp.bfloat16


def limits(mib):
    return pltpu.CompilerParams(vmem_limit_bytes=mib << 20)


def on_chip(value):
    return pltpu.with_memory_space_constraint(value, pltpu.VMEM)


def off_chip(value):
    return pltpu.with_memory_space_constraint(value, pltpu.HBM)


def lane_ids(shape):
    return lax.broadcasted_iota(jnp.int32, shape, len(shape) - 1)


def swap_halves(a, b):
    low = lane_ids(a.shape) < LANES // 2
    first = jnp.where(low, a, pltpu.roll(b, LANES // 2, a.ndim - 1))
    second = jnp.where(low, pltpu.roll(a, LANES // 2, a.ndim - 1), b)
    return first, second


def cos_sin(turns, nlon):
    quarter = nlon // 4
    quadrant = (turns + quarter // 2) // quarter
    x = (turns - quadrant * quarter).astype(F32) * (2.0 * math.pi / nlon)
    y = x * x
    cos = 1.0 + y * (-0.5 + y * (1.0 / 24 + y * (-1.0 / 720 + y * (1.0 / 40320))))
    sin = x + x * y * (-1.0 / 6 + y * (1.0 / 120 + y * (-1.0 / 5040 + y * (1.0 / 362880))))
    swap = (quadrant & 1) == 1
    first = jnp.where(swap, sin, cos)
    second = jnp.where(swap, cos, sin)
    first = jnp.where(((quadrant + 1) & 2) == 2, -first, first)
    second = jnp.where((quadrant & 2) == 2, -second, second)
    return first, second


def table_angles(nlon, ids_row, sign_ref, slots, small, fine, mids):
    rows = ids_row.shape[1]
    half = rows // ORD_DEV
    slots[...] = jnp.broadcast_to(ids_row.astype(F32), (rows, rows)).T
    lane = lane_ids((half, LANES))
    steps = jnp.where(lane < LANES // 2, lane * LANES, (lane - LANES // 2) * (mids * LANES))
    for o in range(ORD_DEV):
        wide_ids = slots[pl.ds(o, half, stride=ORD_DEV), :]
        ids = wide_ids.astype(jnp.int32)
        factor = jnp.where((ids == 0) | (lane < LANES // 2), 1.0, 2.0)
        part = pl.ds(o * half, half)
        cos, sin = cos_sin((ids * steps) & (nlon - 1), nlon)
        small[0, part, :] = factor * cos
        small[1, part, :] = factor * sin
        cos, sin = cos_sin((ids * lane) & (nlon - 1), nlon)
        fine[0, part, :] = cos
        fine[1, part, :] = sin
        across = jnp.concatenate([wide_ids, wide_ids], 0).T[0:8]
        odd = across.astype(jnp.int32) & 1
        sign_ref[pl.ds(o * 8, 8), :] = (1 - 2 * odd).astype(F32)


def table_rows(out_ref, small, fine, mids, blocks):
    rows = small.shape[1]
    half = rows // ORD_DEV
    span = mids * LANES
    coarses = out_ref.shape[1] // span
    block = 16
    shape = (block, LANES)
    for r in blocks:
        part = pl.ds(r, block)
        sc, ss = small[0, part, :], small[1, part, :]
        fc, fs = fine[0, part, :], fine[1, part, :]
        at = (r // half) * rows + r % half
        lead = []
        for p in range(coarses):
            k = LANES // 2 + p
            cs = jnp.broadcast_to(ss[:, k : k + 1], shape)
            lead.append((jnp.broadcast_to(sc[:, k : k + 1], shape), cs))
        for q in range(mids):
            mc = jnp.broadcast_to(sc[:, q : q + 1], shape)
            ms = jnp.broadcast_to(ss[:, q : q + 1], shape)
            cos = mc * fc - ms * fs
            sin = ms * fc + mc * fs
            for p in range(coarses):
                cc, cs = lead[p]
                cols = pl.ds(p * span + q * LANES, LANES)
                out_ref[pl.ds(at, block), cols] = (cc * cos - cs * sin).astype(BF16)
                out_ref[pl.ds(at + half, block), cols] = (-(cs * cos) - cc * sin).astype(BF16)


TILE = 2 * LANES
PAD = 9


def lower_slot(ids_ref, slot):
    return jnp.where(ids_ref[slot] < ids_ref[slot + 1], 0, 1)


def live_steps(ids_ref, slot, degrees):
    tiles = degrees // TILE
    low = lower_slot(ids_ref, slot)
    first_low = ids_ref[slot + low] // TILE
    first_high = ids_ref[slot + 1 - low] // TILE
    count = tiles // 2 - first_low
    steps = [(low, degrees // 2 + k * TILE) for k in range(tiles // 2)]
    for k in range(tiles // 2 + 1):
        later = k >= count
        tile = jnp.where(later, first_high + k - count, first_low + k)
        steps.append((jnp.where(later, 1 - low, low), pl.multiple_of(tile * TILE, TILE)))
    return steps


def dead_steps(ids_ref, slot, degrees):
    tiles = degrees // TILE
    low = lower_slot(ids_ref, slot)
    count = ids_ref[slot + low] // TILE
    steps = []
    for k in range(tiles - 1):
        later = k >= count
        tile = jnp.where(later, k - count, k)
        steps.append((jnp.where(later, 1 - low, low), pl.multiple_of(tile * TILE, TILE)))
    return steps


def forward_kernel(
    nlon,
    plan,
    ids_hbm,
    ids_row_hbm,
    beam_ref,
    harm_ref,
    leg_ref,
    out_ref,
    leg_v,
    table_ref,
    sign_ref,
    ids_row,
    beam_v,
    own_beam,
    harm_v,
    wide,
    lhs,
    slots,
    small,
    fine,
    partial,
    ids_ref,
    sems,
    leg_sems,
):
    degrees = leg_ref.shape[1]
    upper = degrees // 2
    groups = beam_ref.shape[0]
    maps, _, rows, _ = harm_ref.shape
    own = maps // groups
    mids = 8
    slot = lax.axis_index("order") * ORD_DEV
    group = lax.axis_index("freq")
    copies = [
        pltpu.make_async_copy(ids_hbm, ids_ref, sems.at[0]),
        pltpu.make_async_copy(ids_row_hbm, ids_row, sems.at[1]),
        pltpu.make_async_copy(beam_ref, beam_v, sems.at[2]),
        pltpu.make_async_copy(harm_ref.at[pl.ds(group * own, own)], harm_v, sems.at[3]),
    ]

    def upper_copy(order):
        return pltpu.make_async_copy(
            leg_ref.at[order, pl.ds(upper, upper), :], leg_v.at[pl.ds(0, upper), :], sems.at[4]
        )

    for copy in copies:
        copy.start()
    upper_copy(0).start()
    copies[0].wait()
    steps = live_steps(ids_ref, slot, degrees)
    fixed = upper // TILE
    leg_copies = []
    for k, (order, start) in enumerate(steps[fixed:]):
        copy = pltpu.make_async_copy(
            leg_ref.at[order, pl.ds(start, TILE), :],
            leg_v.at[pl.ds(upper + k * TILE, TILE), :],
            leg_sems.at[k],
        )
        copy.start()
        leg_copies.append(copy)
    copies[1].wait()
    table_angles(nlon, ids_row[...], sign_ref, slots, small, fine, mids)
    copies[2].wait()
    for k in range(groups):
        own_beam[k : k + 1, :] = beam_v[pl.ds(group ^ k, 1), :]
    copies[3].wait()
    for b in range(own):
        for o in range(ORD_DEV):
            wide[pl.ds(b * (ORD_DEV * rows + PAD) + o * rows, rows), :] = harm_v[b, o].astype(F32)
    lane = lane_ids((1, LANES))
    blank = jnp.zeros((2 * maps, TILE), BF16)

    def prepare(some):
        for i in some:
            order, first = steps[i]
            at = pl.multiple_of(order * (2 * maps), 2 * maps)
            lhs[pl.ds(2 * maps - at, 2 * maps), pl.ds(i * TILE, TILE)] = blank
            for t in range(TILE // LANES):
                start = first + t * LANES
                if not isinstance(start, int):
                    start = pl.multiple_of(start, LANES)
                live = lane + start >= ids_ref[slot + order]
                shaping = jnp.where(live, own_beam[:, pl.ds(start, LANES)], 0.0)
                for c in range(2):
                    row = order * rows + start // LANES * 2 + c
                    values = wide[pl.ds(row, own, stride=ORD_DEV * rows + PAD), :]
                    shaped = jnp.concatenate(
                        [values * shaping[k : k + 1] for k in range(groups)], 0
                    )
                    lhs[pl.ds(at + c * maps, maps), pl.ds(i * TILE + t * LANES, LANES)] = (
                        shaped.astype(BF16)
                    )

    table_blocks = list(range(0, small.shape[1], 16))
    prepare(range(fixed))
    table_rows(table_ref, small, fine, mids, table_blocks[: plan[0]])
    upper_copy(0).wait()

    @pl.when(lower_slot(ids_ref, slot) == 1)
    def _():
        copy = upper_copy(1)
        copy.start()
        copy.wait()

    partial[...] = jnp.dot(
        lhs[:, pl.ds(0, upper)], leg_v[pl.ds(0, upper), :], preferred_element_type=F32
    )
    prepare(range(fixed, len(steps)))
    table_rows(table_ref, small, fine, mids, table_blocks[plan[0] : plan[1]])

    def arrived(k, carry):
        pltpu.make_async_copy(
            leg_ref.at[0, pl.ds(0, TILE), :],
            leg_v.at[pl.ds(pl.multiple_of(upper + k * TILE, TILE), TILE), :],
            leg_sems.at[k],
        ).wait()
        return carry

    lax.fori_loop(0, len(leg_copies), arrived, 0)
    rest = pl.ds(upper, leg_v.shape[0] - upper)
    total = partial[...] + jnp.dot(lhs[:, rest], leg_v[rest, :], preferred_element_type=F32)
    table_rows(table_ref, small, fine, mids, table_blocks[plan[1] :])
    out_ref[...] = total.T.astype(BF16)


def forward(order_ids, beam, harm, legendre, nlon):
    degrees, lats = legendre.shape[1:]
    maps = harm.shape[0]
    own = maps // beam.shape[0]
    orders = order_ids.shape[0]
    ids_row = order_ids.reshape(1, -1)
    live = degrees + TILE
    return pl.pallas_call(
        lambda *refs: forward_kernel(nlon, (8, 8), *refs),
        name="forward",
        out_shape=(
            pltpu.VMEM((lats, ORD_DEV * 2 * maps), BF16),
            pltpu.VMEM((live, lats), BF16),
            pltpu.VMEM((2 * orders, nlon // 2), BF16),
            pltpu.VMEM((8 * ORD_DEV, LANES), F32),
        ),
        in_specs=[pl.BlockSpec(memory_space=pl.ANY)] * 5,
        out_specs=(pl.BlockSpec(memory_space=pltpu.VMEM),) * 4,
        scratch_shapes=[
            pltpu.VMEM(ids_row.shape, jnp.int32),
            pltpu.VMEM(beam.shape, F32),
            pltpu.VMEM(beam.shape, F32),
            pltpu.VMEM((own,) + harm.shape[1:], BF16),
            pltpu.VMEM((own * (ORD_DEV * harm.shape[2] + PAD), LANES), F32),
            pltpu.VMEM((ORD_DEV * 2 * maps, live), BF16),
            pltpu.VMEM((orders, orders), F32),
            pltpu.VMEM((2, orders, LANES), F32),
            pltpu.VMEM((2, orders, LANES), F32),
            pltpu.VMEM((ORD_DEV * 2 * maps, lats), F32),
            pltpu.SMEM(order_ids.shape, jnp.int32),
            pltpu.SemaphoreType.DMA((5,)),
            pltpu.SemaphoreType.DMA((degrees // TILE // 2 + 1,)),
        ],
        compiler_params=limits(16),
    )(*[off_chip(v) for v in (order_ids, ids_row, beam, harm, legendre)])


def pixel_kernel(
    groups, chunk, scales, got_ref, table_ref, sign_ref, *refs
):
    weight_refs, (out_ref, wide, lhs, mixed) = refs[: groups // 2], refs[groups // 2 :]
    fwd_scale, back_scale = scales
    rows = weight_refs[0].shape[0] // 2
    pairs = got_ref.shape[0] // rows
    maps = got_ref.shape[1] // (2 * ORD_DEV)
    own = maps // groups
    size = rows * maps
    half = table_ref.shape[1]
    wide[...] = got_ref[...].astype(F32)
    signs = [sign_ref[pl.ds(o * 8, 1), :] for o in range(ORD_DEV)]
    for r in range(0, rows, 2):
        stacked = jnp.concatenate(
            [wide[pl.ds(r + i, pairs, stride=rows), :] for i in range(2)], 0
        )
        turned = stacked.T
        for o in range(ORD_DEV):
            cos = turned[(2 * o) * maps : (2 * o + 1) * maps]
            sin = turned[(2 * o + 1) * maps : (2 * o + 2) * maps]
            for i, part in enumerate(swap_halves(cos, sin)):
                cols = pl.ds(o * LANES, LANES)
                lhs[pl.ds((r + i) * maps, maps), cols] = part.astype(BF16)
                lhs[pl.ds(size + (r + i) * maps, maps), cols] = (part * signs[o]).astype(BF16)
    total = jnp.zeros((2 * size, 2 * LANES), F32)
    for j in range(half // chunk):
        cols = pl.ds(j * chunk, chunk)
        part = table_ref[:, cols]
        field = jnp.dot(lhs[...], part, preferred_element_type=F32)
        pieces = []
        for h in range(2):
            span = pl.ds(h * half + j * chunk, chunk)
            weights = [
                weight_refs[k // 2][pl.ds(k % 2 * rows, rows), span] * fwd_scale for k in range(groups)
            ]
            for r in range(rows):
                at = h * size + r * maps
                part_rows = [
                    field[at + k * own : at + (k + 1) * own] * weights[k][r : r + 1]
                    for k in range(groups)
                ]
                pieces.append(jnp.concatenate(part_rows, 0).astype(BF16))
        total += lax.dot_general(
            jnp.concatenate(pieces, 0), part, (((1,), (1,)), ((), ())), preferred_element_type=F32
        )
    sign = jnp.concatenate(signs, 1)
    total = (total[:size] + total[size:] * sign) * back_scale
    low_rows = rows // 2
    for f in range(groups):
        pieces = []
        for low in range(low_rows):
            for o in range(ORD_DEV):
                at = [(high * low_rows + low) * maps + f * own for high in range(2)]
                pieces += list(
                    swap_halves(
                        *[total[a : a + own, o * LANES : (o + 1) * LANES] for a in at]
                    )
                )
        turned = jnp.concatenate(pieces, 0).T
        for high in range(2):
            mixed[pl.ds(f * 2 + high, pairs, stride=2 * groups), :] = turned[
                high * pairs : (high + 1) * pairs
            ]
    out_ref[...] = mixed[...].astype(BF16)


def pixels(got, table, signs, weights, scales, chunk=256):
    groups = 2 * len(weights)
    return pl.pallas_call(
        lambda *refs: pixel_kernel(groups, chunk, scales, *refs),
        name="pixels",
        out_shape=pltpu.VMEM(got.shape, BF16),
        in_specs=[pl.BlockSpec(memory_space=pltpu.VMEM)] * (3 + len(weights)),
        out_specs=pl.BlockSpec(memory_space=pltpu.VMEM),
        scratch_shapes=[
            pltpu.VMEM(got.shape, F32),
            pltpu.VMEM((got.shape[0], 2 * LANES), BF16),
            pltpu.VMEM(got.shape, F32),
        ],
        compiler_params=limits(8),
    )(on_chip(got), table, signs, *[on_chip(w) for w in weights])


def backward_kernel(
    cuts, ids_vmem, beam_ref, got_ref, leg_ref, out_ref, beam_v, wide, mixed, terms, result, blank, ids_ref, sems, zero_sems
):
    ids_copy = pltpu.make_async_copy(ids_vmem, ids_ref, sems.at[cuts[-1]])
    ids_copy.start()
    lats = leg_ref.shape[1]
    groups, degrees = beam_ref.shape
    slot = lax.axis_index("order") * ORD_DEV
    span = got_ref.shape[0] // groups
    width = LANES // groups
    lows = lats // span
    own = width // (2 * ORD_DEV)
    blank[...] = jnp.zeros_like(blank)
    group = lax.axis_index("freq")
    for k in range(groups):
        beam_v[k : k + 1, :] = beam_ref[pl.ds(group ^ k, 1), :]
    wide[...] = got_ref[...].astype(F32)
    pitch = 2 * groups
    devices = got_ref.shape[0] // pitch
    lane_group = lane_ids((devices, LANES)) // width
    for high in range(2):
        turned = []
        for k in range(groups):
            v = wide[pl.ds(k * 2 + high, devices, stride=pitch), :]
            turned.append([v if n == 0 else pltpu.roll(v, n * width, 1) for n in range(groups)])
        for low in range(lows):
            merged = turned[0][(0 - low) % groups]
            for k in range(1, groups):
                merged = jnp.where(lane_group == k, turned[k][(k - low) % groups], merged)
            mixed[pl.ds(high * lows + low, devices, stride=2 * lows), :] = merged
    rhs = mixed[...].astype(BF16)
    lane = lane_ids((1, LANES))
    ids_copy.wait()
    steps = live_steps(ids_ref, slot, degrees)
    per_tile = 2 * TILE // LANES
    per_order = 2 * degrees // LANES

    def out_rows(order, start):
        return pl.ds(order * per_order + start // LANES * 2, per_tile)

    copies = []
    for k, (order, start) in enumerate(dead_steps(ids_ref, slot, degrees)):
        copy = pltpu.make_async_copy(
            blank, out_ref.at[:, out_rows(order, start), :], zero_sems.at[k]
        )
        copy.start()
        copies.append(copy)
    for lo, hi in zip(cuts[:-1], cuts[1:]):
        cols = pl.ds(lo * TILE, (hi - lo) * TILE)
        terms[:, cols] = jnp.dot(leg_ref[cols, :], rhs, preferred_element_type=F32).T
        for i in range(lo, hi):
            order, first = steps[i]
            for t in range(TILE // LANES):
                start = first + t * LANES
                if not isinstance(start, int):
                    start = pl.multiple_of(start, LANES)
                live = lane + start >= ids_ref[slot + order]
                total = jnp.zeros((2 * own, LANES), F32)
                for f in range(groups):
                    at = pl.multiple_of(f * width + order * (2 * own), 2 * own)
                    part = terms[pl.ds(at, 2 * own), pl.ds(i * TILE + t * LANES, LANES)]
                    shaping = jnp.where(live, beam_v[f : f + 1, pl.ds(start, LANES)], 0.0)
                    total += part * shaping
                for c in range(2):
                    result[i, :, t * 2 + c, :] = total[c * own : (c + 1) * own]
            copy = pltpu.make_async_copy(
                result.at[i], out_ref.at[:, out_rows(order, first), :], sems.at[i]
            )
            copy.start()
            copies.append(copy)
    for copy in copies:
        copy.wait()


def backward(order_ids, beam, got, legendre, own):
    degrees = beam.shape[1]
    tiles = legendre.shape[0] // TILE
    cuts = (0, 17)
    per_tile = 2 * TILE // LANES
    return pl.pallas_call(
        lambda *refs: backward_kernel(cuts, *refs),
        name="backward",
        out_shape=jax.ShapeDtypeStruct((own, ORD_DEV * 2 * degrees // LANES, LANES), F32),
        in_specs=[pl.BlockSpec(memory_space=pltpu.VMEM)] * 4,
        out_specs=pl.BlockSpec(memory_space=pl.ANY),
        scratch_shapes=[
            pltpu.VMEM(beam.shape, F32),
            pltpu.VMEM(got.shape, F32),
            pltpu.VMEM((legendre.shape[1], LANES), F32),
            pltpu.VMEM((LANES, legendre.shape[0]), F32),
            pltpu.VMEM((tiles, own, per_tile, LANES), F32),
            pltpu.VMEM((own, per_tile, LANES), F32),
            pltpu.SMEM(order_ids.shape, jnp.int32),
            pltpu.SemaphoreType.DMA((tiles + 1,)),
            pltpu.SemaphoreType.DMA((degrees // TILE - 1,)),
        ],
        compiler_params=limits(8),
    )(on_chip(order_ids), on_chip(beam), on_chip(got), legendre)


def on_device(harmonics, legendre, beam_window, order_ids, noise_weight):
    maps, _, _, degrees = harmonics.shape
    lats = legendre.shape[2]
    nlon = noise_weight.shape[2]
    orders_all = order_ids.shape[0]
    groups = beam_window.shape[0]
    tiles = degrees // LANES
    own = maps // groups
    pairs = orders_all // ORD_DEV
    scales = (1.0 / math.sqrt(2.0 * orders_all), 1.0 / math.sqrt(1.0 * nlon))
    harm = harmonics.reshape(maps, ORD_DEV, 2, tiles, LANES).transpose(0, 1, 3, 2, 4)
    harm = harm.reshape(maps, ORD_DEV, -1, LANES)
    own_weight = noise_weight[0]
    near = lax.ppermute(own_weight, "freq", [(i, i ^ 1) for i in range(groups)])
    columns, legendre, table, signs = forward(order_ids, beam_window, harm, legendre, nlon)
    signs, near = lax.optimization_barrier((signs, near))
    pair = jnp.concatenate([own_weight, near], 0)
    weights = [pair, lax.ppermute(pair, "freq", [(i, i ^ 2) for i in range(groups)])]
    columns = columns.reshape(pairs, lats // pairs, -1)
    got = lax.all_to_all(columns, "order", split_axis=0, concat_axis=0, tiled=True)
    terms = pixels(got.reshape(lats, -1), table, signs, weights, scales)
    terms = terms.reshape(pairs, -1, LANES)
    back = lax.all_to_all(terms, "order", split_axis=0, concat_axis=0, tiled=True)
    out = backward(order_ids, beam_window, back.reshape(-1, LANES), legendre, own)
    out = out.reshape(own, ORD_DEV, tiles, 2, LANES).transpose(0, 1, 3, 2, 4)
    return out.reshape(own, ORD_DEV, 2, degrees)


def solution(mesh):
    return jax.shard_map(
        on_device,
        mesh=mesh,
        in_specs=(
            P(None, "order", None, None),
            P("order", None, None),
            P(),
            P(),
            P("freq", "order", None),
        ),
        out_specs=P("freq", "order", None, None),
        check_vma=False,
    )
```

```python
import math

import jax
import jax.numpy as jnp
from jax import lax
from jax.experimental import pallas as pl
from jax.experimental.pallas import tpu as pltpu
from jax.sharding import PartitionSpec as P

ORD_DEV = 2
LANES = 128
F32 = jnp.float32
BF16 = jnp.bfloat16


def limits(mib):
    return pltpu.CompilerParams(vmem_limit_bytes=mib << 20)


def on_chip(value):
    return pltpu.with_memory_space_constraint(value, pltpu.VMEM)


def off_chip(value):
    return pltpu.with_memory_space_constraint(value, pltpu.HBM)


def lane_ids(shape):
    return lax.broadcasted_iota(jnp.int32, shape, len(shape) - 1)


def swap_halves(a, b):
    low = lane_ids(a.shape) < LANES // 2
    first = jnp.where(low, a, pltpu.roll(b, LANES // 2, a.ndim - 1))
    second = jnp.where(low, pltpu.roll(a, LANES // 2, a.ndim - 1), b)
    return first, second


def cos_sin(turns, nlon):
    quarter = nlon // 4
    quadrant = (turns + quarter // 2) // quarter
    x = (turns - quadrant * quarter).astype(F32) * (2.0 * math.pi / nlon)
    y = x * x
    cos = 1.0 + y * (-0.5 + y * (1.0 / 24 + y * (-1.0 / 720 + y * (1.0 / 40320))))
    sin = x + x * y * (-1.0 / 6 + y * (1.0 / 120 + y * (-1.0 / 5040 + y * (1.0 / 362880))))
    swap = (quadrant & 1) == 1
    first = jnp.where(swap, sin, cos)
    second = jnp.where(swap, cos, sin)
    first = jnp.where(((quadrant + 1) & 2) == 2, -first, first)
    second = jnp.where((quadrant & 2) == 2, -second, second)
    return first, second


def table_angles(nlon, ids_row, sign_ref, slots, small, fine, mids):
    rows = ids_row.shape[1]
    half = rows // ORD_DEV
    slots[...] = jnp.broadcast_to(ids_row.astype(F32), (rows, rows)).T
    lane = lane_ids((half, LANES))
    steps = jnp.where(lane < LANES // 2, lane * LANES, (lane - LANES // 2) * (mids * LANES))
    for o in range(ORD_DEV):
        wide_ids = slots[pl.ds(o, half, stride=ORD_DEV), :]
        ids = wide_ids.astype(jnp.int32)
        factor = jnp.where((ids == 0) | (lane < LANES // 2), 1.0, 2.0)
        part = pl.ds(o * half, half)
        cos, sin = cos_sin((ids * steps) & (nlon - 1), nlon)
        small[0, part, :] = factor * cos
        small[1, part, :] = factor * sin
        cos, sin = cos_sin((ids * lane) & (nlon - 1), nlon)
        fine[0, part, :] = cos
        fine[1, part, :] = sin
        across = jnp.concatenate([wide_ids, wide_ids], 0).T[0:8]
        odd = across.astype(jnp.int32) & 1
        sign_ref[pl.ds(o * 8, 8), :] = (1 - 2 * odd).astype(F32)


def table_rows(out_ref, small, fine, mids, blocks):
    rows = small.shape[1]
    half = rows // ORD_DEV
    span = mids * LANES
    coarses = out_ref.shape[1] // span
    block = 16
    shape = (block, LANES)
    for r in blocks:
        part = pl.ds(r, block)
        sc, ss = small[0, part, :], small[1, part, :]
        fc, fs = fine[0, part, :], fine[1, part, :]
        at = (r // half) * rows + r % half
        lead = []
        for p in range(coarses):
            k = LANES // 2 + p
            cs = jnp.broadcast_to(ss[:, k : k + 1], shape)
            lead.append((jnp.broadcast_to(sc[:, k : k + 1], shape), cs))
        for q in range(mids):
            mc = jnp.broadcast_to(sc[:, q : q + 1], shape)
            ms = jnp.broadcast_to(ss[:, q : q + 1], shape)
            cos = mc * fc - ms * fs
            sin = ms * fc + mc * fs
            for p in range(coarses):
                cc, cs = lead[p]
                cols = pl.ds(p * span + q * LANES, LANES)
                out_ref[pl.ds(at, block), cols] = (cc * cos - cs * sin).astype(BF16)
                out_ref[pl.ds(at + half, block), cols] = (-(cs * cos) - cc * sin).astype(BF16)


TILE = 2 * LANES
PAD = 9


def lower_slot(ids_ref, slot):
    return jnp.where(ids_ref[slot] < ids_ref[slot + 1], 0, 1)


def live_steps(ids_ref, slot, degrees):
    tiles = degrees // TILE
    low = lower_slot(ids_ref, slot)
    first_low = ids_ref[slot + low] // TILE
    first_high = ids_ref[slot + 1 - low] // TILE
    count = tiles // 2 - first_low
    steps = [(low, degrees // 2 + k * TILE) for k in range(tiles // 2)]
    for k in range(tiles // 2 + 1):
        later = k >= count
        tile = jnp.where(later, first_high + k - count, first_low + k)
        steps.append((jnp.where(later, 1 - low, low), pl.multiple_of(tile * TILE, TILE)))
    return steps


def dead_steps(ids_ref, slot, degrees):
    tiles = degrees // TILE
    low = lower_slot(ids_ref, slot)
    count = ids_ref[slot + low] // TILE
    steps = []
    for k in range(tiles - 1):
        later = k >= count
        tile = jnp.where(later, k - count, k)
        steps.append((jnp.where(later, 1 - low, low), pl.multiple_of(tile * TILE, TILE)))
    return steps


def forward_kernel(
    nlon,
    plan,
    ids_hbm,
    ids_row_hbm,
    beam_ref,
    harm_ref,
    leg_ref,
    out_ref,
    leg_v,
    table_ref,
    sign_ref,
    own_beam,
    ids_row,
    beam_v,
    harm_v,
    wide,
    lhs,
    slots,
    small,
    fine,
    partial,
    ids_ref,
    sems,
    leg_sems,
):
    degrees = leg_ref.shape[1]
    upper = degrees // 2
    groups = beam_ref.shape[0]
    maps, _, rows, _ = harm_ref.shape
    own = maps // groups
    mids = 8
    slot = lax.axis_index("order") * ORD_DEV
    group = lax.axis_index("freq")
    copies = [
        pltpu.make_async_copy(ids_hbm, ids_ref, sems.at[0]),
        pltpu.make_async_copy(ids_row_hbm, ids_row, sems.at[1]),
        pltpu.make_async_copy(beam_ref, beam_v, sems.at[2]),
        pltpu.make_async_copy(harm_ref.at[pl.ds(group * own, own)], harm_v, sems.at[3]),
    ]

    def upper_copy(order):
        return pltpu.make_async_copy(
            leg_ref.at[order, pl.ds(upper, upper), :], leg_v.at[pl.ds(0, upper), :], sems.at[4]
        )

    for copy in copies:
        copy.start()
    upper_copy(0).start()
    copies[0].wait()
    steps = live_steps(ids_ref, slot, degrees)
    fixed = upper // TILE
    leg_copies = []
    for k, (order, start) in enumerate(steps[fixed:]):
        copy = pltpu.make_async_copy(
            leg_ref.at[order, pl.ds(start, TILE), :],
            leg_v.at[pl.ds(upper + k * TILE, TILE), :],
            leg_sems.at[k],
        )
        copy.start()
        leg_copies.append(copy)
    copies[1].wait()
    table_angles(nlon, ids_row[...], sign_ref, slots, small, fine, mids)
    copies[2].wait()
    for k in range(groups):
        own_beam[k : k + 1, :] = beam_v[pl.ds(group ^ k, 1), :]
    copies[3].wait()
    for b in range(own):
        for o in range(ORD_DEV):
            wide[pl.ds(b * (ORD_DEV * rows + PAD) + o * rows, rows), :] = harm_v[b, o].astype(F32)
    lane = lane_ids((1, LANES))
    blank = jnp.zeros((2 * maps, TILE), BF16)

    def prepare(some):
        for i in some:
            order, first = steps[i]
            at = pl.multiple_of(order * (2 * maps), 2 * maps)
            lhs[pl.ds(2 * maps - at, 2 * maps), pl.ds(i * TILE, TILE)] = blank
            for t in range(TILE // LANES):
                start = first + t * LANES
                if not isinstance(start, int):
                    start = pl.multiple_of(start, LANES)
                live = lane + start >= ids_ref[slot + order]
                shaping = jnp.where(live, own_beam[:, pl.ds(start, LANES)], 0.0)
                for c in range(2):
                    row = order * rows + start // LANES * 2 + c
                    values = wide[pl.ds(row, own, stride=ORD_DEV * rows + PAD), :]
                    shaped = jnp.concatenate(
                        [values * shaping[k : k + 1] for k in range(groups)], 0
                    )
                    lhs[pl.ds(at + c * maps, maps), pl.ds(i * TILE + t * LANES, LANES)] = (
                        shaped.astype(BF16)
                    )

    table_blocks = list(range(0, small.shape[1], 16))
    prepare(range(fixed))
    table_rows(table_ref, small, fine, mids, table_blocks[: plan[0]])
    upper_copy(0).wait()

    @pl.when(lower_slot(ids_ref, slot) == 1)
    def _():
        copy = upper_copy(1)
        copy.start()
        copy.wait()

    partial[...] = jnp.dot(
        lhs[:, pl.ds(0, upper)], leg_v[pl.ds(0, upper), :], preferred_element_type=F32
    )
    prepare(range(fixed, len(steps)))
    table_rows(table_ref, small, fine, mids, table_blocks[plan[0] : plan[1]])

    def arrived(k, carry):
        pltpu.make_async_copy(
            leg_ref.at[0, pl.ds(0, TILE), :],
            leg_v.at[pl.ds(pl.multiple_of(upper + k * TILE, TILE), TILE), :],
            leg_sems.at[k],
        ).wait()
        return carry

    lax.fori_loop(0, len(leg_copies), arrived, 0)
    rest = pl.ds(upper, leg_v.shape[0] - upper)
    total = partial[...] + jnp.dot(lhs[:, rest], leg_v[rest, :], preferred_element_type=F32)
    table_rows(table_ref, small, fine, mids, table_blocks[plan[1] :])
    out_ref[...] = total.T.astype(BF16)


def forward(order_ids, beam, harm, legendre, nlon):
    degrees, lats = legendre.shape[1:]
    maps = harm.shape[0]
    own = maps // beam.shape[0]
    orders = order_ids.shape[0]
    ids_row = order_ids.reshape(1, -1)
    live = degrees + TILE
    return pl.pallas_call(
        lambda *refs: forward_kernel(nlon, (8, 8), *refs),
        name="forward",
        out_shape=(
            pltpu.VMEM((lats, ORD_DEV * 2 * maps), BF16),
            pltpu.VMEM((live, lats), BF16),
            pltpu.VMEM((2 * orders, nlon // 2), BF16),
            pltpu.VMEM((8 * ORD_DEV, LANES), F32),
            pltpu.VMEM(beam.shape, F32),
        ),
        in_specs=[pl.BlockSpec(memory_space=pl.ANY)] * 5,
        out_specs=(pl.BlockSpec(memory_space=pltpu.VMEM),) * 5,
        scratch_shapes=[
            pltpu.VMEM(ids_row.shape, jnp.int32),
            pltpu.VMEM(beam.shape, F32),
            pltpu.VMEM((own,) + harm.shape[1:], BF16),
            pltpu.VMEM((own * (ORD_DEV * harm.shape[2] + PAD), LANES), F32),
            pltpu.VMEM((ORD_DEV * 2 * maps, live), BF16),
            pltpu.VMEM((orders, orders), F32),
            pltpu.VMEM((2, orders, LANES), F32),
            pltpu.VMEM((2, orders, LANES), F32),
            pltpu.VMEM((ORD_DEV * 2 * maps, lats), F32),
            pltpu.SMEM(order_ids.shape, jnp.int32),
            pltpu.SemaphoreType.DMA((5,)),
            pltpu.SemaphoreType.DMA((degrees // TILE // 2 + 1,)),
        ],
        compiler_params=limits(16),
    )(*[off_chip(v) for v in (order_ids, ids_row, beam, harm, legendre)])


def pixel_kernel(
    groups, chunk, scales, got_ref, table_ref, sign_ref, *refs
):
    weight_refs, (out_ref, wide, lhs, mixed) = refs[: groups // 2], refs[groups // 2 :]
    fwd_scale, back_scale = scales
    rows = weight_refs[0].shape[0] // 2
    pairs = got_ref.shape[0] // rows
    maps = got_ref.shape[1] // (2 * ORD_DEV)
    own = maps // groups
    size = rows * maps
    half = table_ref.shape[1]
    wide[...] = got_ref[...].astype(F32)
    signs = [sign_ref[pl.ds(o * 8, 1), :] for o in range(ORD_DEV)]
    for r in range(0, rows, 2):
        stacked = jnp.concatenate(
            [wide[pl.ds(r + i, pairs, stride=rows), :] for i in range(2)], 0
        )
        turned = stacked.T
        for o in range(ORD_DEV):
            cos = turned[(2 * o) * maps : (2 * o + 1) * maps]
            sin = turned[(2 * o + 1) * maps : (2 * o + 2) * maps]
            for i, part in enumerate(swap_halves(cos, sin)):
                cols = pl.ds(o * LANES, LANES)
                lhs[pl.ds((r + i) * maps, maps), cols] = part.astype(BF16)
                lhs[pl.ds(size + (r + i) * maps, maps), cols] = (part * signs[o]).astype(BF16)
    total = jnp.zeros((2 * size, 2 * LANES), F32)
    for j in range(half // chunk):
        cols = pl.ds(j * chunk, chunk)
        part = table_ref[:, cols]
        field = jnp.dot(lhs[...], part, preferred_element_type=F32)
        pieces = []
        for h in range(2):
            span = pl.ds(h * half + j * chunk, chunk)
            weights = [
                weight_refs[k // 2][pl.ds(k % 2 * rows, rows), span] * fwd_scale for k in range(groups)
            ]
            for r in range(rows):
                at = h * size + r * maps
                part_rows = [
                    field[at + k * own : at + (k + 1) * own] * weights[k][r : r + 1]
                    for k in range(groups)
                ]
                pieces.append(jnp.concatenate(part_rows, 0).astype(BF16))
        total += lax.dot_general(
            jnp.concatenate(pieces, 0), part, (((1,), (1,)), ((), ())), preferred_element_type=F32
        )
    sign = jnp.concatenate(signs, 1)
    total = (total[:size] + total[size:] * sign) * back_scale
    low_rows = rows // 2
    for f in range(groups):
        pieces = []
        for low in range(low_rows):
            for o in range(ORD_DEV):
                at = [(high * low_rows + low) * maps + f * own for high in range(2)]
                pieces += list(
                    swap_halves(
                        *[total[a : a + own, o * LANES : (o + 1) * LANES] for a in at]
                    )
                )
        turned = jnp.concatenate(pieces, 0).T
        for high in range(2):
            mixed[pl.ds(f * 2 + high, pairs, stride=2 * groups), :] = turned[
                high * pairs : (high + 1) * pairs
            ]
    out_ref[...] = mixed[...].astype(BF16)


def pixels(got, table, signs, weights, scales, chunk=256):
    groups = 2 * len(weights)
    return pl.pallas_call(
        lambda *refs: pixel_kernel(groups, chunk, scales, *refs),
        name="pixels",
        out_shape=pltpu.VMEM(got.shape, BF16),
        in_specs=[pl.BlockSpec(memory_space=pltpu.VMEM)] * (3 + len(weights)),
        out_specs=pl.BlockSpec(memory_space=pltpu.VMEM),
        scratch_shapes=[
            pltpu.VMEM(got.shape, F32),
            pltpu.VMEM((got.shape[0], 2 * LANES), BF16),
            pltpu.VMEM(got.shape, F32),
        ],
        compiler_params=limits(8),
    )(on_chip(got), table, signs, *[on_chip(w) for w in weights])


def backward_kernel(
    cuts, ids_vmem, beam_ref, got_ref, leg_ref, out_ref, wide, mixed, terms, result, blank, ids_ref, sems, zero_sems
):
    ids_copy = pltpu.make_async_copy(ids_vmem, ids_ref, sems.at[cuts[-1]])
    ids_copy.start()
    lats = leg_ref.shape[1]
    groups, degrees = beam_ref.shape
    slot = lax.axis_index("order") * ORD_DEV
    span = got_ref.shape[0] // groups
    width = LANES // groups
    lows = lats // span
    own = width // (2 * ORD_DEV)
    blank[...] = jnp.zeros_like(blank)
    wide[...] = got_ref[...].astype(F32)
    pitch = 2 * groups
    devices = got_ref.shape[0] // pitch
    lane_group = lane_ids((devices, LANES)) // width
    for high in range(2):
        turned = []
        for k in range(groups):
            v = wide[pl.ds(k * 2 + high, devices, stride=pitch), :]
            turned.append([v if n == 0 else pltpu.roll(v, n * width, 1) for n in range(groups)])
        for low in range(lows):
            merged = turned[0][(0 - low) % groups]
            for k in range(1, groups):
                merged = jnp.where(lane_group == k, turned[k][(k - low) % groups], merged)
            mixed[pl.ds(high * lows + low, devices, stride=2 * lows), :] = merged
    rhs = mixed[...].astype(BF16)
    lane = lane_ids((1, LANES))
    ids_copy.wait()
    steps = live_steps(ids_ref, slot, degrees)
    per_tile = 2 * TILE // LANES
    per_order = 2 * degrees // LANES

    def out_rows(order, start):
        return pl.ds(order * per_order + start // LANES * 2, per_tile)

    copies = []
    for k, (order, start) in enumerate(dead_steps(ids_ref, slot, degrees)):
        copy = pltpu.make_async_copy(
            blank, out_ref.at[:, out_rows(order, start), :], zero_sems.at[k]
        )
        copy.start()
        copies.append(copy)
    for lo, hi in zip(cuts[:-1], cuts[1:]):
        cols = pl.ds(lo * TILE, (hi - lo) * TILE)
        terms[:, cols] = jnp.dot(leg_ref[cols, :], rhs, preferred_element_type=F32).T
        for i in range(lo, hi):
            order, first = steps[i]
            for t in range(TILE // LANES):
                start = first + t * LANES
                if not isinstance(start, int):
                    start = pl.multiple_of(start, LANES)
                live = lane + start >= ids_ref[slot + order]
                total = jnp.zeros((2 * own, LANES), F32)
                for f in range(groups):
                    at = pl.multiple_of(f * width + order * (2 * own), 2 * own)
                    part = terms[pl.ds(at, 2 * own), pl.ds(i * TILE + t * LANES, LANES)]
                    shaping = jnp.where(live, beam_ref[f : f + 1, pl.ds(start, LANES)], 0.0)
                    total += part * shaping
                for c in range(2):
                    result[i, :, t * 2 + c, :] = total[c * own : (c + 1) * own]
            copy = pltpu.make_async_copy(
                result.at[i], out_ref.at[:, out_rows(order, first), :], sems.at[i]
            )
            copy.start()
            copies.append(copy)
    for copy in copies:
        copy.wait()


def backward(order_ids, beam, got, legendre, own):
    degrees = beam.shape[1]
    tiles = legendre.shape[0] // TILE
    cuts = (0, 17)
    per_tile = 2 * TILE // LANES
    return pl.pallas_call(
        lambda *refs: backward_kernel(cuts, *refs),
        name="backward",
        out_shape=jax.ShapeDtypeStruct((own, ORD_DEV * 2 * degrees // LANES, LANES), F32),
        in_specs=[pl.BlockSpec(memory_space=pltpu.VMEM)] * 4,
        out_specs=pl.BlockSpec(memory_space=pl.ANY),
        scratch_shapes=[
            pltpu.VMEM(got.shape, F32),
            pltpu.VMEM((legendre.shape[1], LANES), F32),
            pltpu.VMEM((LANES, legendre.shape[0]), F32),
            pltpu.VMEM((tiles, own, per_tile, LANES), F32),
            pltpu.VMEM((own, per_tile, LANES), F32),
            pltpu.SMEM(order_ids.shape, jnp.int32),
            pltpu.SemaphoreType.DMA((tiles + 1,)),
            pltpu.SemaphoreType.DMA((degrees // TILE - 1,)),
        ],
        compiler_params=limits(8),
    )(on_chip(order_ids), beam, on_chip(got), legendre)


def on_device(harmonics, legendre, beam_window, order_ids, noise_weight):
    maps, _, _, degrees = harmonics.shape
    lats = legendre.shape[2]
    nlon = noise_weight.shape[2]
    orders_all = order_ids.shape[0]
    groups = beam_window.shape[0]
    tiles = degrees // LANES
    own = maps // groups
    pairs = orders_all // ORD_DEV
    scales = (1.0 / math.sqrt(2.0 * orders_all), 1.0 / math.sqrt(1.0 * nlon))
    harm = harmonics.reshape(maps, ORD_DEV, 2, tiles, LANES).transpose(0, 1, 3, 2, 4)
    harm = harm.reshape(maps, ORD_DEV, -1, LANES)
    own_weight = noise_weight[0]
    near = lax.ppermute(own_weight, "freq", [(i, i ^ 1) for i in range(groups)])
    columns, legendre, table, signs, beam = forward(
        order_ids, beam_window, harm, legendre, nlon
    )
    signs, near = lax.optimization_barrier((signs, near))
    pair = jnp.concatenate([own_weight, near], 0)
    weights = [pair, lax.ppermute(pair, "freq", [(i, i ^ 2) for i in range(groups)])]
    columns = columns.reshape(pairs, lats // pairs, -1)
    got = lax.all_to_all(columns, "order", split_axis=0, concat_axis=0, tiled=True)
    terms = pixels(got.reshape(lats, -1), table, signs, weights, scales)
    terms = terms.reshape(pairs, -1, LANES)
    back = lax.all_to_all(terms, "order", split_axis=0, concat_axis=0, tiled=True)
    out = backward(order_ids, beam, back.reshape(-1, LANES), legendre, own)
    out = out.reshape(own, ORD_DEV, tiles, 2, LANES).transpose(0, 1, 3, 2, 4)
    return out.reshape(own, ORD_DEV, 2, degrees)


def solution(mesh):
    return jax.shard_map(
        on_device,
        mesh=mesh,
        in_specs=(
            P(None, "order", None, None),
            P("order", None, None),
            P(),
            P(),
            P("freq", "order", None),
        ),
        out_specs=P("freq", "order", None, None),
        check_vma=False,
    )
```

```python
import math

import jax
import jax.numpy as jnp
from jax import lax
from jax.experimental import pallas as pl
from jax.experimental.pallas import tpu as pltpu
from jax.sharding import PartitionSpec as P

ORD_DEV = 2
LANES = 128
F32 = jnp.float32
BF16 = jnp.bfloat16


def limits(mib):
    return pltpu.CompilerParams(vmem_limit_bytes=mib << 20)


def on_chip(value):
    return pltpu.with_memory_space_constraint(value, pltpu.VMEM)


def off_chip(value):
    return pltpu.with_memory_space_constraint(value, pltpu.HBM)


def lane_ids(shape):
    return lax.broadcasted_iota(jnp.int32, shape, len(shape) - 1)


def swap_halves(a, b):
    low = lane_ids(a.shape) < LANES // 2
    first = jnp.where(low, a, pltpu.roll(b, LANES // 2, a.ndim - 1))
    second = jnp.where(low, pltpu.roll(a, LANES // 2, a.ndim - 1), b)
    return first, second


def cos_sin(turns, nlon):
    quarter = nlon // 4
    quadrant = (turns + quarter // 2) // quarter
    x = (turns - quadrant * quarter).astype(F32) * (2.0 * math.pi / nlon)
    y = x * x
    cos = 1.0 + y * (-0.5 + y * (1.0 / 24 + y * (-1.0 / 720 + y * (1.0 / 40320))))
    sin = x + x * y * (-1.0 / 6 + y * (1.0 / 120 + y * (-1.0 / 5040 + y * (1.0 / 362880))))
    swap = (quadrant & 1) == 1
    first = jnp.where(swap, sin, cos)
    second = jnp.where(swap, cos, sin)
    first = jnp.where(((quadrant + 1) & 2) == 2, -first, first)
    second = jnp.where((quadrant & 2) == 2, -second, second)
    return first, second


def table_angles(nlon, ids_row, sign_ref, slots, small, fine, mids):
    rows = ids_row.shape[1]
    half = rows // ORD_DEV
    slots[...] = jnp.broadcast_to(ids_row.astype(F32), (rows, rows)).T
    lane = lane_ids((half, LANES))
    steps = jnp.where(lane < LANES // 2, lane * LANES, (lane - LANES // 2) * (mids * LANES))
    for o in range(ORD_DEV):
        wide_ids = slots[pl.ds(o, half, stride=ORD_DEV), :]
        ids = wide_ids.astype(jnp.int32)
        factor = jnp.where((ids == 0) | (lane < LANES // 2), 1.0, 2.0)
        part = pl.ds(o * half, half)
        cos, sin = cos_sin((ids * steps) & (nlon - 1), nlon)
        small[0, part, :] = factor * cos
        small[1, part, :] = factor * sin
        cos, sin = cos_sin((ids * lane) & (nlon - 1), nlon)
        fine[0, part, :] = cos
        fine[1, part, :] = sin
        across = jnp.concatenate([wide_ids, wide_ids], 0).T[0:8]
        odd = across.astype(jnp.int32) & 1
        sign_ref[pl.ds(o * 8, 8), :] = (1 - 2 * odd).astype(F32)


def table_rows(out_ref, small, fine, mids, blocks):
    rows = small.shape[1]
    half = rows // ORD_DEV
    span = mids * LANES
    coarses = out_ref.shape[1] // span
    block = 16
    shape = (block, LANES)
    for r in blocks:
        part = pl.ds(r, block)
        sc, ss = small[0, part, :], small[1, part, :]
        fc, fs = fine[0, part, :], fine[1, part, :]
        at = (r // half) * rows + r % half
        lead = []
        for p in range(coarses):
            k = LANES // 2 + p
            cs = jnp.broadcast_to(ss[:, k : k + 1], shape)
            lead.append((jnp.broadcast_to(sc[:, k : k + 1], shape), cs))
        for q in range(mids):
            mc = jnp.broadcast_to(sc[:, q : q + 1], shape)
            ms = jnp.broadcast_to(ss[:, q : q + 1], shape)
            cos = mc * fc - ms * fs
            sin = ms * fc + mc * fs
            for p in range(coarses):
                cc, cs = lead[p]
                cols = pl.ds(p * span + q * LANES, LANES)
                out_ref[pl.ds(at, block), cols] = (cc * cos - cs * sin).astype(BF16)
                out_ref[pl.ds(at + half, block), cols] = (-(cs * cos) - cc * sin).astype(BF16)


TILE = 2 * LANES
PAD = 9


def lower_slot(ids_ref, slot):
    return jnp.where(ids_ref[slot] < ids_ref[slot + 1], 0, 1)


def live_steps(ids_ref, slot, degrees):
    tiles = degrees // TILE
    low = lower_slot(ids_ref, slot)
    first_low = ids_ref[slot + low] // TILE
    first_high = ids_ref[slot + 1 - low] // TILE
    count = tiles // 2 - first_low
    steps = [(low, degrees // 2 + k * TILE) for k in range(tiles // 2)]
    for k in range(tiles // 2 + 1):
        later = k >= count
        tile = jnp.where(later, first_high + k - count, first_low + k)
        steps.append((jnp.where(later, 1 - low, low), pl.multiple_of(tile * TILE, TILE)))
    return steps


def dead_steps(ids_ref, slot, degrees):
    tiles = degrees // TILE
    low = lower_slot(ids_ref, slot)
    count = ids_ref[slot + low] // TILE
    steps = []
    for k in range(tiles - 1):
        later = k >= count
        tile = jnp.where(later, k - count, k)
        steps.append((jnp.where(later, 1 - low, low), pl.multiple_of(tile * TILE, TILE)))
    return steps


def forward_kernel(
    nlon,
    plan,
    ids_hbm,
    ids_row_hbm,
    beam_ref,
    harm_ref,
    leg_ref,
    out_ref,
    leg_v,
    table_ref,
    sign_ref,
    own_beam,
    ids_row,
    beam_v,
    harm_v,
    wide,
    lhs,
    slots,
    small,
    fine,
    partial,
    ids_ref,
    sems,
    leg_sems,
):
    degrees = leg_ref.shape[1]
    upper = degrees // 2
    groups = beam_ref.shape[0]
    maps, _, rows, _ = harm_ref.shape
    own = maps // groups
    mids = 8
    slot = lax.axis_index("order") * ORD_DEV
    group = lax.axis_index("freq")
    copies = [
        pltpu.make_async_copy(ids_hbm, ids_ref, sems.at[0]),
        pltpu.make_async_copy(ids_row_hbm, ids_row, sems.at[1]),
        pltpu.make_async_copy(beam_ref, beam_v, sems.at[2]),
        pltpu.make_async_copy(harm_ref.at[pl.ds(group * own, own)], harm_v, sems.at[3]),
    ]

    def upper_copy(order):
        return pltpu.make_async_copy(
            leg_ref.at[order, pl.ds(upper, upper), :], leg_v.at[pl.ds(0, upper), :], sems.at[4]
        )

    for copy in copies:
        copy.start()
    upper_copy(0).start()
    copies[0].wait()
    steps = live_steps(ids_ref, slot, degrees)
    fixed = upper // TILE
    leg_copies = []
    for k, (order, start) in enumerate(steps[fixed:]):
        copy = pltpu.make_async_copy(
            leg_ref.at[order, pl.ds(start, TILE), :],
            leg_v.at[pl.ds(upper + k * TILE, TILE), :],
            leg_sems.at[k],
        )
        copy.start()
        leg_copies.append(copy)
    copies[1].wait()
    table_angles(nlon, ids_row[...], sign_ref, slots, small, fine, mids)
    copies[2].wait()
    for k in range(groups):
        own_beam[k : k + 1, :] = beam_v[pl.ds(group ^ k, 1), :]
    copies[3].wait()
    for b in range(own):
        for o in range(ORD_DEV):
            wide[pl.ds(b * (ORD_DEV * rows + PAD) + o * rows, rows), :] = harm_v[b, o].astype(F32)
    lane = lane_ids((1, LANES))
    blank = jnp.zeros((2 * maps, TILE), BF16)

    def prepare(some):
        for i in some:
            order, first = steps[i]
            at = pl.multiple_of(order * (2 * maps), 2 * maps)
            lhs[pl.ds(2 * maps - at, 2 * maps), pl.ds(i * TILE, TILE)] = blank
            for t in range(TILE // LANES):
                start = first + t * LANES
                if not isinstance(start, int):
                    start = pl.multiple_of(start, LANES)
                live = lane + start >= ids_ref[slot + order]
                shaping = jnp.where(live, own_beam[:, pl.ds(start, LANES)], 0.0)
                for c in range(2):
                    row = order * rows + start // LANES * 2 + c
                    values = wide[pl.ds(row, own, stride=ORD_DEV * rows + PAD), :]
                    shaped = jnp.concatenate(
                        [values * shaping[k : k + 1] for k in range(groups)], 0
                    )
                    lhs[pl.ds(at + c * maps, maps), pl.ds(i * TILE + t * LANES, LANES)] = (
                        shaped.astype(BF16)
                    )

    table_blocks = list(range(0, small.shape[1], 16))
    prepare(range(fixed))
    table_rows(table_ref, small, fine, mids, table_blocks[: plan[0]])
    upper_copy(0).wait()

    @pl.when(lower_slot(ids_ref, slot) == 1)
    def _():
        copy = upper_copy(1)
        copy.start()
        copy.wait()

    partial[...] = jnp.dot(
        lhs[:, pl.ds(0, upper)], leg_v[pl.ds(0, upper), :], preferred_element_type=F32
    )
    prepare(range(fixed, len(steps)))
    table_rows(table_ref, small, fine, mids, table_blocks[plan[0] : plan[1]])

    def arrived(k, carry):
        pltpu.make_async_copy(
            leg_ref.at[0, pl.ds(0, TILE), :],
            leg_v.at[pl.ds(pl.multiple_of(upper + k * TILE, TILE), TILE), :],
            leg_sems.at[k],
        ).wait()
        return carry

    lax.fori_loop(0, len(leg_copies), arrived, 0)
    rest = pl.ds(upper, leg_v.shape[0] - upper)
    total = partial[...] + jnp.dot(lhs[:, rest], leg_v[rest, :], preferred_element_type=F32)
    table_rows(table_ref, small, fine, mids, table_blocks[plan[1] :])
    out_ref[...] = total.T.astype(BF16)


def forward(order_ids, beam, harm, legendre, nlon):
    degrees, lats = legendre.shape[1:]
    maps = harm.shape[0]
    own = maps // beam.shape[0]
    orders = order_ids.shape[0]
    ids_row = order_ids.reshape(1, -1)
    live = degrees + TILE
    return pl.pallas_call(
        lambda *refs: forward_kernel(nlon, (8, 8), *refs),
        name="forward",
        out_shape=(
            pltpu.VMEM((lats, ORD_DEV * 2 * maps), BF16),
            pltpu.VMEM((live, lats), BF16),
            pltpu.VMEM((2 * orders, nlon // 2), BF16),
            pltpu.VMEM((8 * ORD_DEV, LANES), F32),
            pltpu.VMEM(beam.shape, F32),
        ),
        in_specs=[pl.BlockSpec(memory_space=pl.ANY)] * 5,
        out_specs=(pl.BlockSpec(memory_space=pltpu.VMEM),) * 5,
        scratch_shapes=[
            pltpu.VMEM(ids_row.shape, jnp.int32),
            pltpu.VMEM(beam.shape, F32),
            pltpu.VMEM((own,) + harm.shape[1:], BF16),
            pltpu.VMEM((own * (ORD_DEV * harm.shape[2] + PAD), LANES), F32),
            pltpu.VMEM((ORD_DEV * 2 * maps, live), BF16),
            pltpu.VMEM((orders, orders), F32),
            pltpu.VMEM((2, orders, LANES), F32),
            pltpu.VMEM((2, orders, LANES), F32),
            pltpu.VMEM((ORD_DEV * 2 * maps, lats), F32),
            pltpu.SMEM(order_ids.shape, jnp.int32),
            pltpu.SemaphoreType.DMA((5,)),
            pltpu.SemaphoreType.DMA((degrees // TILE // 2 + 1,)),
        ],
        compiler_params=limits(16),
    )(*[off_chip(v) for v in (order_ids, ids_row, beam, harm, legendre)])


def pixel_kernel(
    groups, chunk, scales, got_ref, table_ref, sign_ref, *refs
):
    weight_refs, (out_ref, wide, lhs, mixed) = refs[: groups // 2], refs[groups // 2 :]
    fwd_scale, back_scale = scales
    rows = weight_refs[0].shape[0] // 2
    pairs = got_ref.shape[0] // rows
    maps = got_ref.shape[1] // (2 * ORD_DEV)
    own = maps // groups
    size = rows * maps
    half = table_ref.shape[1]
    wide[...] = got_ref[...].astype(F32)
    signs = [sign_ref[pl.ds(o * 8, 1), :] for o in range(ORD_DEV)]
    for r in range(0, rows, 2):
        stacked = jnp.concatenate(
            [wide[pl.ds(r + i, pairs, stride=rows), :] for i in range(2)], 0
        )
        turned = stacked.T
        for o in range(ORD_DEV):
            cos = turned[(2 * o) * maps : (2 * o + 1) * maps]
            sin = turned[(2 * o + 1) * maps : (2 * o + 2) * maps]
            for i, part in enumerate(swap_halves(cos, sin)):
                cols = pl.ds(o * LANES, LANES)
                lhs[pl.ds((r + i) * maps, maps), cols] = part.astype(BF16)
                lhs[pl.ds(size + (r + i) * maps, maps), cols] = (part * signs[o]).astype(BF16)
    total = jnp.zeros((2 * size, 2 * LANES), F32)
    for j in range(half // chunk):
        cols = pl.ds(j * chunk, chunk)
        part = table_ref[:, cols]
        field = jnp.dot(lhs[...], part, preferred_element_type=F32)
        pieces = []
        for h in range(2):
            span = pl.ds(h * half + j * chunk, chunk)
            weights = [
                weight_refs[k // 2][pl.ds(k % 2 * rows, rows), span] * fwd_scale for k in range(groups)
            ]
            for r in range(rows):
                at = h * size + r * maps
                part_rows = [
                    field[at + k * own : at + (k + 1) * own] * weights[k][r : r + 1]
                    for k in range(groups)
                ]
                pieces.append(jnp.concatenate(part_rows, 0).astype(BF16))
        total += lax.dot_general(
            jnp.concatenate(pieces, 0), part, (((1,), (1,)), ((), ())), preferred_element_type=F32
        )
    sign = jnp.concatenate(signs, 1)
    total = (total[:size] + total[size:] * sign) * back_scale
    low_rows = rows // 2
    for f in range(groups):
        pieces = []
        for low in range(low_rows):
            for o in range(ORD_DEV):
                at = [(high * low_rows + low) * maps + f * own for high in range(2)]
                pieces += list(
                    swap_halves(
                        *[total[a : a + own, o * LANES : (o + 1) * LANES] for a in at]
                    )
                )
        turned = jnp.concatenate(pieces, 0).T
        for high in range(2):
            mixed[pl.ds(f * 2 + high, pairs, stride=2 * groups), :] = turned[
                high * pairs : (high + 1) * pairs
            ]
    out_ref[...] = mixed[...].astype(BF16)


def pixels(got, table, signs, weights, scales, chunk=256):
    groups = 2 * len(weights)
    return pl.pallas_call(
        lambda *refs: pixel_kernel(groups, chunk, scales, *refs),
        name="pixels",
        out_shape=pltpu.VMEM(got.shape, BF16),
        in_specs=[pl.BlockSpec(memory_space=pltpu.VMEM)] * (3 + len(weights)),
        out_specs=pl.BlockSpec(memory_space=pltpu.VMEM),
        scratch_shapes=[
            pltpu.VMEM(got.shape, F32),
            pltpu.VMEM((got.shape[0], 2 * LANES), BF16),
            pltpu.VMEM(got.shape, F32),
        ],
        compiler_params=limits(8),
    )(on_chip(got), table, signs, *[on_chip(w) for w in weights])


def backward_kernel(
    cuts, ids_vmem, beam_ref, got_ref, leg_ref, out_ref, wide, mixed, terms, result, blank, ids_ref, sems, zero_sems
):
    ids_copy = pltpu.make_async_copy(ids_vmem, ids_ref, sems.at[cuts[-1]])
    ids_copy.start()
    lats = leg_ref.shape[1]
    groups, degrees = beam_ref.shape
    slot = lax.axis_index("order") * ORD_DEV
    span = got_ref.shape[0] // groups
    width = LANES // groups
    lows = lats // span
    own = width // (2 * ORD_DEV)
    blank[...] = jnp.zeros_like(blank)
    rows_per = 2 * groups
    devices = got_ref.shape[0] // rows_per
    pitch = rows_per + 1
    values = got_ref[...].astype(F32)
    for d in range(devices):
        wide[pl.ds(d * pitch, rows_per), :] = values[d * rows_per : (d + 1) * rows_per]
    lane_group = lane_ids((devices, LANES)) // width
    for high in range(2):
        turned = []
        for k in range(groups):
            v = wide[pl.ds(k * 2 + high, devices, stride=pitch), :]
            turned.append([v if n == 0 else pltpu.roll(v, n * width, 1) for n in range(groups)])
        for low in range(lows):
            merged = turned[0][(0 - low) % groups]
            for k in range(1, groups):
                merged = jnp.where(lane_group == k, turned[k][(k - low) % groups], merged)
            mixed[pl.ds(high * lows + low, devices, stride=2 * lows), :] = merged
    rhs = mixed[...].astype(BF16)
    lane = lane_ids((1, LANES))
    ids_copy.wait()
    steps = live_steps(ids_ref, slot, degrees)
    per_tile = 2 * TILE // LANES
    per_order = 2 * degrees // LANES

    def out_rows(order, start):
        return pl.ds(order * per_order + start // LANES * 2, per_tile)

    copies = []
    for lo, hi in zip(cuts[:-1], cuts[1:]):
        cols = pl.ds(lo * TILE, (hi - lo) * TILE)
        terms[:, cols] = jnp.dot(leg_ref[cols, :], rhs, preferred_element_type=F32).T
        for i in range(lo, hi):
            order, first = steps[i]
            for t in range(TILE // LANES):
                start = first + t * LANES
                if not isinstance(start, int):
                    start = pl.multiple_of(start, LANES)
                live = lane + start >= ids_ref[slot + order]
                total = jnp.zeros((2 * own, LANES), F32)
                for f in range(groups):
                    at = pl.multiple_of(f * width + order * (2 * own), 2 * own)
                    part = terms[pl.ds(at, 2 * own), pl.ds(i * TILE + t * LANES, LANES)]
                    shaping = jnp.where(live, beam_ref[f : f + 1, pl.ds(start, LANES)], 0.0)
                    total += part * shaping
                for c in range(2):
                    result[i, :, t * 2 + c, :] = total[c * own : (c + 1) * own]
            copy = pltpu.make_async_copy(
                result.at[i], out_ref.at[:, out_rows(order, first), :], sems.at[i]
            )
            copy.start()
            copies.append(copy)
    for k, (order, start) in enumerate(dead_steps(ids_ref, slot, degrees)):
        copy = pltpu.make_async_copy(
            blank, out_ref.at[:, out_rows(order, start), :], zero_sems.at[k]
        )
        copy.start()
        copies.append(copy)
    for copy in copies:
        copy.wait()


def backward(order_ids, beam, got, legendre, own):
    degrees = beam.shape[1]
    tiles = legendre.shape[0] // TILE
    cuts = (0, 17)
    per_tile = 2 * TILE // LANES
    return pl.pallas_call(
        lambda *refs: backward_kernel(cuts, *refs),
        name="backward",
        out_shape=jax.ShapeDtypeStruct((own, ORD_DEV * 2 * degrees // LANES, LANES), F32),
        in_specs=[pl.BlockSpec(memory_space=pltpu.VMEM)] * 4,
        out_specs=pl.BlockSpec(memory_space=pl.ANY),
        scratch_shapes=[
            pltpu.VMEM((got.shape[0] // 8 * 9, LANES), F32),
            pltpu.VMEM((legendre.shape[1], LANES), F32),
            pltpu.VMEM((LANES, legendre.shape[0]), F32),
            pltpu.VMEM((tiles, own, per_tile, LANES), F32),
            pltpu.VMEM((own, per_tile, LANES), F32),
            pltpu.SMEM(order_ids.shape, jnp.int32),
            pltpu.SemaphoreType.DMA((tiles + 1,)),
            pltpu.SemaphoreType.DMA((degrees // TILE - 1,)),
        ],
        compiler_params=limits(8),
    )(on_chip(order_ids), beam, on_chip(got), legendre)


def on_device(harmonics, legendre, beam_window, order_ids, noise_weight):
    maps, _, _, degrees = harmonics.shape
    lats = legendre.shape[2]
    nlon = noise_weight.shape[2]
    orders_all = order_ids.shape[0]
    groups = beam_window.shape[0]
    tiles = degrees // LANES
    own = maps // groups
    pairs = orders_all // ORD_DEV
    scales = (1.0 / math.sqrt(2.0 * orders_all), 1.0 / math.sqrt(1.0 * nlon))
    harm = harmonics.reshape(maps, ORD_DEV, 2, tiles, LANES).transpose(0, 1, 3, 2, 4)
    harm = harm.reshape(maps, ORD_DEV, -1, LANES)
    own_weight = noise_weight[0]
    near = lax.ppermute(own_weight, "freq", [(i, i ^ 1) for i in range(groups)])
    columns, legendre, table, signs, beam = forward(
        order_ids, beam_window, harm, legendre, nlon
    )
    signs, near = lax.optimization_barrier((signs, near))
    pair = jnp.concatenate([own_weight, near], 0)
    weights = [pair, lax.ppermute(pair, "freq", [(i, i ^ 2) for i in range(groups)])]
    columns = columns.reshape(pairs, lats // pairs, -1)
    got = lax.all_to_all(columns, "order", split_axis=0, concat_axis=0, tiled=True)
    terms = pixels(got.reshape(lats, -1), table, signs, weights, scales)
    terms = terms.reshape(pairs, -1, LANES)
    back = lax.all_to_all(terms, "order", split_axis=0, concat_axis=0, tiled=True)
    out = backward(order_ids, beam, back.reshape(-1, LANES), legendre, own)
    out = out.reshape(own, ORD_DEV, tiles, 2, LANES).transpose(0, 1, 3, 2, 4)
    return out.reshape(own, ORD_DEV, 2, degrees)


def solution(mesh):
    return jax.shard_map(
        on_device,
        mesh=mesh,
        in_specs=(
            P(None, "order", None, None),
            P("order", None, None),
            P(),
            P(),
            P("freq", "order", None),
        ),
        out_specs=P("freq", "order", None, None),
        check_vma=False,
    )
```

```python
import math

import jax
import jax.numpy as jnp
from jax import lax
from jax.experimental import pallas as pl
from jax.experimental.pallas import tpu as pltpu
from jax.sharding import PartitionSpec as P

ORD_DEV = 2
LANES = 128
F32 = jnp.float32
BF16 = jnp.bfloat16


def limits(mib):
    return pltpu.CompilerParams(vmem_limit_bytes=mib << 20)


def on_chip(value):
    return pltpu.with_memory_space_constraint(value, pltpu.VMEM)


def off_chip(value):
    return pltpu.with_memory_space_constraint(value, pltpu.HBM)


def lane_ids(shape):
    return lax.broadcasted_iota(jnp.int32, shape, len(shape) - 1)


def swap_halves(a, b):
    low = lane_ids(a.shape) < LANES // 2
    first = jnp.where(low, a, pltpu.roll(b, LANES // 2, a.ndim - 1))
    second = jnp.where(low, pltpu.roll(a, LANES // 2, a.ndim - 1), b)
    return first, second


def cos_sin(turns, nlon):
    quarter = nlon // 4
    quadrant = (turns + quarter // 2) // quarter
    x = (turns - quadrant * quarter).astype(F32) * (2.0 * math.pi / nlon)
    y = x * x
    cos = 1.0 + y * (-0.5 + y * (1.0 / 24 + y * (-1.0 / 720 + y * (1.0 / 40320))))
    sin = x + x * y * (-1.0 / 6 + y * (1.0 / 120 + y * (-1.0 / 5040 + y * (1.0 / 362880))))
    swap = (quadrant & 1) == 1
    first = jnp.where(swap, sin, cos)
    second = jnp.where(swap, cos, sin)
    first = jnp.where(((quadrant + 1) & 2) == 2, -first, first)
    second = jnp.where((quadrant & 2) == 2, -second, second)
    return first, second


def table_angles(nlon, ids_row, sign_ref, slots, small, fine, mids):
    rows = ids_row.shape[1]
    half = rows // ORD_DEV
    slots[...] = jnp.broadcast_to(ids_row.astype(F32), (rows, rows)).T
    lane = lane_ids((half, LANES))
    steps = jnp.where(lane < LANES // 2, lane * LANES, (lane - LANES // 2) * (mids * LANES))
    for o in range(ORD_DEV):
        wide_ids = slots[pl.ds(o, half, stride=ORD_DEV), :]
        ids = wide_ids.astype(jnp.int32)
        factor = jnp.where((ids == 0) | (lane < LANES // 2), 1.0, 2.0)
        part = pl.ds(o * half, half)
        cos, sin = cos_sin((ids * steps) & (nlon - 1), nlon)
        small[0, part, :] = factor * cos
        small[1, part, :] = factor * sin
        cos, sin = cos_sin((ids * lane) & (nlon - 1), nlon)
        fine[0, part, :] = cos
        fine[1, part, :] = sin
        across = jnp.concatenate([wide_ids, wide_ids], 0).T[0:8]
        odd = across.astype(jnp.int32) & 1
        sign_ref[pl.ds(o * 8, 8), :] = (1 - 2 * odd).astype(F32)


def table_rows(out_ref, small, fine, mids, blocks):
    rows = small.shape[1]
    half = rows // ORD_DEV
    span = mids * LANES
    coarses = out_ref.shape[1] // span
    block = 16
    shape = (block, LANES)
    for r in blocks:
        part = pl.ds(r, block)
        sc, ss = small[0, part, :], small[1, part, :]
        fc, fs = fine[0, part, :], fine[1, part, :]
        at = (r // half) * rows + r % half
        lead = []
        for p in range(coarses):
            k = LANES // 2 + p
            cs = jnp.broadcast_to(ss[:, k : k + 1], shape)
            lead.append((jnp.broadcast_to(sc[:, k : k + 1], shape), cs))
        for q in range(mids):
            mc = jnp.broadcast_to(sc[:, q : q + 1], shape)
            ms = jnp.broadcast_to(ss[:, q : q + 1], shape)
            cos = mc * fc - ms * fs
            sin = ms * fc + mc * fs
            for p in range(coarses):
                cc, cs = lead[p]
                cols = pl.ds(p * span + q * LANES, LANES)
                out_ref[pl.ds(at, block), cols] = (cc * cos - cs * sin).astype(BF16)
                out_ref[pl.ds(at + half, block), cols] = (-(cs * cos) - cc * sin).astype(BF16)


TILE = 2 * LANES
PAD = 9


def lower_slot(ids_ref, slot):
    return jnp.where(ids_ref[slot] < ids_ref[slot + 1], 0, 1)


def live_steps(ids_ref, slot, degrees):
    tiles = degrees // TILE
    low = lower_slot(ids_ref, slot)
    first_low = ids_ref[slot + low] // TILE
    first_high = ids_ref[slot + 1 - low] // TILE
    count = tiles // 2 - first_low
    steps = [(low, degrees // 2 + k * TILE) for k in range(tiles // 2)]
    for k in range(tiles // 2 + 1):
        later = k >= count
        tile = jnp.where(later, first_high + k - count, first_low + k)
        steps.append((jnp.where(later, 1 - low, low), pl.multiple_of(tile * TILE, TILE)))
    return steps


def dead_steps(ids_ref, slot, degrees):
    tiles = degrees // TILE
    low = lower_slot(ids_ref, slot)
    count = ids_ref[slot + low] // TILE
    steps = []
    for k in range(tiles - 1):
        later = k >= count
        tile = jnp.where(later, k - count, k)
        steps.append((jnp.where(later, 1 - low, low), pl.multiple_of(tile * TILE, TILE)))
    return steps


def forward_kernel(
    nlon,
    plan,
    ids_hbm,
    ids_row_hbm,
    beam_ref,
    harm_ref,
    leg_ref,
    out_ref,
    leg_v,
    table_ref,
    sign_ref,
    own_beam,
    ids_row,
    beam_v,
    harm_v,
    wide,
    lhs,
    slots,
    small,
    fine,
    partial,
    ids_ref,
    sems,
    leg_sems,
):
    degrees = leg_ref.shape[1]
    upper = degrees // 2
    groups = beam_ref.shape[0]
    maps, _, rows, _ = harm_ref.shape
    own = maps // groups
    mids = 8
    slot = lax.axis_index("order") * ORD_DEV
    group = lax.axis_index("freq")
    copies = [
        pltpu.make_async_copy(ids_hbm, ids_ref, sems.at[0]),
        pltpu.make_async_copy(ids_row_hbm, ids_row, sems.at[1]),
        pltpu.make_async_copy(beam_ref, beam_v, sems.at[2]),
        pltpu.make_async_copy(harm_ref.at[pl.ds(group * own, own)], harm_v, sems.at[3]),
    ]

    def upper_copy(order):
        return pltpu.make_async_copy(
            leg_ref.at[order, pl.ds(upper, upper), :], leg_v.at[pl.ds(0, upper), :], sems.at[4]
        )

    for copy in copies:
        copy.start()
    upper_copy(0).start()
    copies[0].wait()
    steps = live_steps(ids_ref, slot, degrees)
    fixed = upper // TILE
    leg_copies = []
    for k, (order, start) in enumerate(steps[fixed:]):
        copy = pltpu.make_async_copy(
            leg_ref.at[order, pl.ds(start, TILE), :],
            leg_v.at[pl.ds(upper + k * TILE, TILE), :],
            leg_sems.at[k],
        )
        copy.start()
        leg_copies.append(copy)
    copies[1].wait()
    table_angles(nlon, ids_row[...], sign_ref, slots, small, fine, mids)
    copies[2].wait()
    for k in range(groups):
        own_beam[k : k + 1, :] = beam_v[pl.ds(group ^ k, 1), :]
    copies[3].wait()
    for b in range(own):
        for o in range(ORD_DEV):
            wide[pl.ds(b * (ORD_DEV * rows + PAD) + o * rows, rows), :] = harm_v[b, o].astype(F32)
    lane = lane_ids((1, LANES))
    blank = jnp.zeros((2 * maps, TILE), BF16)

    def prepare(some):
        for i in some:
            order, first = steps[i]
            at = pl.multiple_of(order * (2 * maps), 2 * maps)
            lhs[pl.ds(2 * maps - at, 2 * maps), pl.ds(i * TILE, TILE)] = blank
            for t in range(TILE // LANES):
                start = first + t * LANES
                if not isinstance(start, int):
                    start = pl.multiple_of(start, LANES)
                live = lane + start >= ids_ref[slot + order]
                shaping = jnp.where(live, own_beam[:, pl.ds(start, LANES)], 0.0)
                for c in range(2):
                    row = order * rows + start // LANES * 2 + c
                    values = wide[pl.ds(row, own, stride=ORD_DEV * rows + PAD), :]
                    shaped = jnp.concatenate(
                        [values * shaping[k : k + 1] for k in range(groups)], 0
                    )
                    lhs[pl.ds(at + c * maps, maps), pl.ds(i * TILE + t * LANES, LANES)] = (
                        shaped.astype(BF16)
                    )

    table_blocks = list(range(0, small.shape[1], 16))
    prepare(range(fixed))
    table_rows(table_ref, small, fine, mids, table_blocks[: plan[0]])
    upper_copy(0).wait()

    @pl.when(lower_slot(ids_ref, slot) == 1)
    def _():
        copy = upper_copy(1)
        copy.start()
        copy.wait()

    partial[...] = jnp.dot(
        lhs[:, pl.ds(0, upper)], leg_v[pl.ds(0, upper), :], preferred_element_type=F32
    )
    prepare(range(fixed, len(steps)))
    table_rows(table_ref, small, fine, mids, table_blocks[plan[0] : plan[1]])

    def arrived(k, carry):
        pltpu.make_async_copy(
            leg_ref.at[0, pl.ds(0, TILE), :],
            leg_v.at[pl.ds(pl.multiple_of(upper + k * TILE, TILE), TILE), :],
            leg_sems.at[k],
        ).wait()
        return carry

    lax.fori_loop(0, len(leg_copies), arrived, 0)
    rest = pl.ds(upper, leg_v.shape[0] - upper)
    total = partial[...] + jnp.dot(lhs[:, rest], leg_v[rest, :], preferred_element_type=F32)
    table_rows(table_ref, small, fine, mids, table_blocks[plan[1] :])
    out_ref[...] = total.T.astype(BF16)


def forward(order_ids, beam, harm, legendre, nlon):
    degrees, lats = legendre.shape[1:]
    maps = harm.shape[0]
    own = maps // beam.shape[0]
    orders = order_ids.shape[0]
    ids_row = order_ids.reshape(1, -1)
    live = degrees + TILE
    return pl.pallas_call(
        lambda *refs: forward_kernel(nlon, (4, 8), *refs),
        name="forward",
        out_shape=(
            pltpu.VMEM((lats, ORD_DEV * 2 * maps), BF16),
            pltpu.VMEM((live, lats), BF16),
            pltpu.VMEM((2 * orders, nlon // 2), BF16),
            pltpu.VMEM((8 * ORD_DEV, LANES), F32),
            pltpu.VMEM(beam.shape, F32),
        ),
        in_specs=[pl.BlockSpec(memory_space=pl.ANY)] * 5,
        out_specs=(pl.BlockSpec(memory_space=pltpu.VMEM),) * 5,
        scratch_shapes=[
            pltpu.VMEM(ids_row.shape, jnp.int32),
            pltpu.VMEM(beam.shape, F32),
            pltpu.VMEM((own,) + harm.shape[1:], BF16),
            pltpu.VMEM((own * (ORD_DEV * harm.shape[2] + PAD), LANES), F32),
            pltpu.VMEM((ORD_DEV * 2 * maps, live), BF16),
            pltpu.VMEM((orders, orders), F32),
            pltpu.VMEM((2, orders, LANES), F32),
            pltpu.VMEM((2, orders, LANES), F32),
            pltpu.VMEM((ORD_DEV * 2 * maps, lats), F32),
            pltpu.SMEM(order_ids.shape, jnp.int32),
            pltpu.SemaphoreType.DMA((5,)),
            pltpu.SemaphoreType.DMA((degrees // TILE // 2 + 1,)),
        ],
        compiler_params=limits(16),
    )(*[off_chip(v) for v in (order_ids, ids_row, beam, harm, legendre)])


def pixel_kernel(
    groups, chunk, scales, got_ref, table_ref, sign_ref, *refs
):
    weight_refs, (out_ref, wide, lhs, mixed) = refs[: groups // 2], refs[groups // 2 :]
    fwd_scale, back_scale = scales
    rows = weight_refs[0].shape[0] // 2
    pairs = got_ref.shape[0] // rows
    maps = got_ref.shape[1] // (2 * ORD_DEV)
    own = maps // groups
    size = rows * maps
    half = table_ref.shape[1]
    wide[...] = got_ref[...].astype(F32)
    signs = [sign_ref[pl.ds(o * 8, 1), :] for o in range(ORD_DEV)]
    for r in range(0, rows, 2):
        stacked = jnp.concatenate(
            [wide[pl.ds(r + i, pairs, stride=rows), :] for i in range(2)], 0
        )
        turned = stacked.T
        for o in range(ORD_DEV):
            cos = turned[(2 * o) * maps : (2 * o + 1) * maps]
            sin = turned[(2 * o + 1) * maps : (2 * o + 2) * maps]
            for i, part in enumerate(swap_halves(cos, sin)):
                cols = pl.ds(o * LANES, LANES)
                lhs[pl.ds((r + i) * maps, maps), cols] = part.astype(BF16)
                lhs[pl.ds(size + (r + i) * maps, maps), cols] = (part * signs[o]).astype(BF16)
    total = jnp.zeros((2 * size, 2 * LANES), F32)
    for j in range(half // chunk):
        cols = pl.ds(j * chunk, chunk)
        part = table_ref[:, cols]
        field = jnp.dot(lhs[...], part, preferred_element_type=F32)
        pieces = []
        for h in range(2):
            span = pl.ds(h * half + j * chunk, chunk)
            weights = [
                weight_refs[k // 2][pl.ds(k % 2 * rows, rows), span] * fwd_scale for k in range(groups)
            ]
            for r in range(rows):
                at = h * size + r * maps
                part_rows = [
                    field[at + k * own : at + (k + 1) * own] * weights[k][r : r + 1]
                    for k in range(groups)
                ]
                pieces.append(jnp.concatenate(part_rows, 0).astype(BF16))
        total += lax.dot_general(
            jnp.concatenate(pieces, 0), part, (((1,), (1,)), ((), ())), preferred_element_type=F32
        )
    sign = jnp.concatenate(signs, 1)
    total = (total[:size] + total[size:] * sign) * back_scale
    low_rows = rows // 2
    for f in range(groups):
        pieces = []
        for low in range(low_rows):
            for o in range(ORD_DEV):
                at = [(high * low_rows + low) * maps + f * own for high in range(2)]
                pieces += list(
                    swap_halves(
                        *[total[a : a + own, o * LANES : (o + 1) * LANES] for a in at]
                    )
                )
        turned = jnp.concatenate(pieces, 0).T
        for high in range(2):
            mixed[pl.ds(f * 2 + high, pairs, stride=2 * groups), :] = turned[
                high * pairs : (high + 1) * pairs
            ]
    out_ref[...] = mixed[...].astype(BF16)


def pixels(got, table, signs, weights, scales, chunk=256):
    groups = 2 * len(weights)
    return pl.pallas_call(
        lambda *refs: pixel_kernel(groups, chunk, scales, *refs),
        name="pixels",
        out_shape=pltpu.VMEM(got.shape, BF16),
        in_specs=[pl.BlockSpec(memory_space=pltpu.VMEM)] * (3 + len(weights)),
        out_specs=pl.BlockSpec(memory_space=pltpu.VMEM),
        scratch_shapes=[
            pltpu.VMEM(got.shape, F32),
            pltpu.VMEM((got.shape[0], 2 * LANES), BF16),
            pltpu.VMEM(got.shape, F32),
        ],
        compiler_params=limits(8),
    )(on_chip(got), table, signs, *[on_chip(w) for w in weights])


def backward_kernel(
    cuts, ids_vmem, beam_ref, got_ref, leg_ref, out_ref, wide, mixed, terms, result, blank, ids_ref, sems, zero_sems
):
    ids_copy = pltpu.make_async_copy(ids_vmem, ids_ref, sems.at[cuts[-1]])
    ids_copy.start()
    lats = leg_ref.shape[1]
    groups, degrees = beam_ref.shape
    slot = lax.axis_index("order") * ORD_DEV
    span = got_ref.shape[0] // groups
    width = LANES // groups
    lows = lats // span
    own = width // (2 * ORD_DEV)
    blank[...] = jnp.zeros_like(blank)
    rows_per = 2 * groups
    devices = got_ref.shape[0] // rows_per
    pitch = rows_per + 1
    values = got_ref[...].astype(F32)
    for d in range(devices):
        wide[pl.ds(d * pitch, rows_per), :] = values[d * rows_per : (d + 1) * rows_per]
    lane_group = lane_ids((devices, LANES)) // width
    for high in range(2):
        turned = []
        for k in range(groups):
            v = wide[pl.ds(k * 2 + high, devices, stride=pitch), :]
            turned.append([v if n == 0 else pltpu.roll(v, n * width, 1) for n in range(groups)])
        for low in range(lows):
            merged = turned[0][(0 - low) % groups]
            for k in range(1, groups):
                merged = jnp.where(lane_group == k, turned[k][(k - low) % groups], merged)
            mixed[pl.ds(high * lows + low, devices, stride=2 * lows), :] = merged
    rhs = mixed[...].astype(BF16)
    lane = lane_ids((1, LANES))
    ids_copy.wait()
    steps = live_steps(ids_ref, slot, degrees)
    per_tile = 2 * TILE // LANES
    per_order = 2 * degrees // LANES

    def out_rows(order, start):
        return pl.ds(order * per_order + start // LANES * 2, per_tile)

    copies = []
    for lo, hi in zip(cuts[:-1], cuts[1:]):
        cols = pl.ds(lo * TILE, (hi - lo) * TILE)
        terms[:, cols] = jnp.dot(leg_ref[cols, :], rhs, preferred_element_type=F32).T
        for i in range(lo, hi):
            order, first = steps[i]
            for t in range(TILE // LANES):
                start = first + t * LANES
                if not isinstance(start, int):
                    start = pl.multiple_of(start, LANES)
                live = lane + start >= ids_ref[slot + order]
                total = jnp.zeros((2 * own, LANES), F32)
                for f in range(groups):
                    at = pl.multiple_of(f * width + order * (2 * own), 2 * own)
                    part = terms[pl.ds(at, 2 * own), pl.ds(i * TILE + t * LANES, LANES)]
                    shaping = jnp.where(live, beam_ref[f : f + 1, pl.ds(start, LANES)], 0.0)
                    total += part * shaping
                for c in range(2):
                    result[i, :, t * 2 + c, :] = total[c * own : (c + 1) * own]
            copy = pltpu.make_async_copy(
                result.at[i], out_ref.at[:, out_rows(order, first), :], sems.at[i]
            )
            copy.start()
            copies.append(copy)
    for k, (order, start) in enumerate(dead_steps(ids_ref, slot, degrees)):
        copy = pltpu.make_async_copy(
            blank, out_ref.at[:, out_rows(order, start), :], zero_sems.at[k]
        )
        copy.start()
        copies.append(copy)
    for copy in copies:
        copy.wait()


def backward(order_ids, beam, got, legendre, own):
    degrees = beam.shape[1]
    tiles = legendre.shape[0] // TILE
    cuts = (0, 17)
    per_tile = 2 * TILE // LANES
    return pl.pallas_call(
        lambda *refs: backward_kernel(cuts, *refs),
        name="backward",
        out_shape=jax.ShapeDtypeStruct((own, ORD_DEV * 2 * degrees // LANES, LANES), F32),
        in_specs=[pl.BlockSpec(memory_space=pltpu.VMEM)] * 4,
        out_specs=pl.BlockSpec(memory_space=pl.ANY),
        scratch_shapes=[
            pltpu.VMEM((got.shape[0] // 8 * 9, LANES), F32),
            pltpu.VMEM((legendre.shape[1], LANES), F32),
            pltpu.VMEM((LANES, legendre.shape[0]), F32),
            pltpu.VMEM((tiles, own, per_tile, LANES), F32),
            pltpu.VMEM((own, per_tile, LANES), F32),
            pltpu.SMEM(order_ids.shape, jnp.int32),
            pltpu.SemaphoreType.DMA((tiles + 1,)),
            pltpu.SemaphoreType.DMA((degrees // TILE - 1,)),
        ],
        compiler_params=limits(8),
    )(on_chip(order_ids), beam, on_chip(got), legendre)


def on_device(harmonics, legendre, beam_window, order_ids, noise_weight):
    maps, _, _, degrees = harmonics.shape
    lats = legendre.shape[2]
    nlon = noise_weight.shape[2]
    orders_all = order_ids.shape[0]
    groups = beam_window.shape[0]
    tiles = degrees // LANES
    own = maps // groups
    pairs = orders_all // ORD_DEV
    scales = (1.0 / math.sqrt(2.0 * orders_all), 1.0 / math.sqrt(1.0 * nlon))
    harm = harmonics.reshape(maps, ORD_DEV, 2, tiles, LANES).transpose(0, 1, 3, 2, 4)
    harm = harm.reshape(maps, ORD_DEV, -1, LANES)
    own_weight = noise_weight[0]
    near = lax.ppermute(own_weight, "freq", [(i, i ^ 1) for i in range(groups)])
    columns, legendre, table, signs, beam = forward(
        order_ids, beam_window, harm, legendre, nlon
    )
    signs, near = lax.optimization_barrier((signs, near))
    pair = jnp.concatenate([own_weight, near], 0)
    weights = [pair, lax.ppermute(pair, "freq", [(i, i ^ 2) for i in range(groups)])]
    columns = columns.reshape(pairs, lats // pairs, -1)
    got = lax.all_to_all(columns, "order", split_axis=0, concat_axis=0, tiled=True)
    terms = pixels(got.reshape(lats, -1), table, signs, weights, scales)
    terms = terms.reshape(pairs, -1, LANES)
    back = lax.all_to_all(terms, "order", split_axis=0, concat_axis=0, tiled=True)
    out = backward(order_ids, beam, back.reshape(-1, LANES), legendre, own)
    out = out.reshape(own, ORD_DEV, tiles, 2, LANES).transpose(0, 1, 3, 2, 4)
    return out.reshape(own, ORD_DEV, 2, degrees)


def solution(mesh):
    return jax.shard_map(
        on_device,
        mesh=mesh,
        in_specs=(
            P(None, "order", None, None),
            P("order", None, None),
            P(),
            P(),
            P("freq", "order", None),
        ),
        out_specs=P("freq", "order", None, None),
        check_vma=False,
    )
```
